32 devices in a mesh: group: 2 (over y), row: 4 (over z), col: 2 (over x), sub: 2 (over core).
Axes of the slice: x: 2, y: 2, z: 4, core: 2. Of those that a mesh axis runs over, the one named last changes fastest.
Arguments:
- anomalies: bfloat16 [2048, 2048], P(('group', 'row', 'sub')), parts along dimension 0, may hold values from -6 to 6
- innovations: float32 [4096], P(('group', 'row', 'col', 'sub')), parts along dimension 0, may hold values from -12 to 12
- obs_error: float32 [4096], P(('group', 'row', 'col', 'sub')), parts along dimension 0, may hold values from 0.5 to 2
- track_pos: float32 [4096], P('group'), parts along dimension 0, may hold values from 0 to 1
- taper_class: int32 [8, 4], P('group'), parts along dimension 0, may hold values from 0 to 3, as said below
Outputs:
- solution: float32 [4096], P(('group', 'row', 'col', 'sub')), parts along dimension 0
- residual: float32 [4096], P(('group', 'row', 'col', 'sub')), parts along dimension 0
The draws below stay inside these ranges and needn't reach their ends.
There are 2 independent parts, one for each index of `group`. The reference program is written for one: setup_inputs(seed, part) draws one part's arguments, and reference() takes and returns one part's arrays. A program takes and returns all parts, laid end to end along the dimension named above; each array names one. Nothing has to cross between parts.
Inputs may be any that keep to these rules, and one draw needn't show every extreme that they name: `taper_class`: tiles are spatial blocks of the region, laid along the plume in an order given by a permutation pos of the 4 tiles; entry (a, b) is the distance |pos[a] - pos[b]| in tiles.
All inputs are finite; a program needn't handle non-finite values.
Results may differ from the reference program's by a relative error of at most 0.0003.
Values may be sent and summed in bfloat16 or wider, within the bound.
No kernel may reach another device: no remote copies, remote signals or barrier semaphores. Data moves between devices by JAX's collectives and lax.ppermute only.
A program may use at most 64 MiB of HBM per device.

```python
import math
import jax
import jax.numpy as jnp
from jax import lax

M = 1024
OBS_ROW = 512
ITERS = 2
NTILE = 4
NOBS = 2048
REACH = 2


def draw_taper_class(key, part):
    order = jax.random.permutation(key, NTILE).astype(jnp.int32)
    return jnp.abs(order[:, None] - order[None, :]).astype(jnp.int32)


def draw_innovations(key, part):
    ramp = jnp.arange(NOBS, dtype=jnp.float32) / NOBS
    values = jnp.clip(jax.random.normal(key, (NOBS,), jnp.float32), -4.0, 4.0)
    return values * (1.0 + 2.0 * ramp)


def shard_levels(stream_key, dims, pieces, low, high):
    gain = 1.0
    for axis_at, shards_of in pieces:
        heights = jax.random.uniform(jax.random.fold_in(jax.random.fold_in(stream_key, 6), axis_at), (shards_of,), jnp.float32, low / len(pieces), high / len(pieces))
        gain = gain * jnp.repeat(jnp.exp(heights), dims[axis_at] // shards_of).reshape((-1,) + (1,) * (len(dims) - 1 - axis_at))
    return gain


def noise(key, shape, scale, limit, split=(), kind=jnp.bfloat16):
    level = shard_levels(key, shape, split, -0.22, 0.18) if split else 1.0
    array = jax.random.normal(key, shape, jnp.float32) * scale * level
    return jnp.minimum(jnp.maximum(array, -limit), limit).astype(kind)


def setup_inputs(seed: int = 0, part: int = 0) -> dict:
    keys = jax.random.split(jax.random.key(seed), 6)
    part_splits = jax.random.split(jax.random.fold_in(keys[5], part), 6)
    anomalies = noise(part_splits[0], (M, NOBS), 1.0, 6.0, ((0, 8),))
    innovations = draw_innovations(jax.random.fold_in(jax.random.fold_in(keys[5], part), 71), part)
    obs_error = jnp.clip(jnp.exp(math.log(2.0) - 1.3862944 * jax.random.uniform(part_splits[2], (NOBS,), jnp.float32) ** shard_levels(part_splits[2], (NOBS,), ((0, 16),), -0.2, 0.2)), 0.5, 2.0)
    track_pos = jnp.clip(jax.random.uniform(part_splits[3], (NOBS,), jnp.float32, 0.0, 1.0), 0.0, 1.0)
    taper_class = draw_taper_class(jax.random.fold_in(jax.random.fold_in(keys[5], part), 71), part)
    return dict(anomalies=anomalies, innovations=innovations, obs_error=obs_error, track_pos=track_pos, taper_class=taper_class)


track_width = 0.0001


def reference(anomalies, innovations, obs_error, track_pos, taper_class):
    ensemble = anomalies.astype(jnp.float32)
    member_total = anomalies.shape[0]
    inverse_members = 1.0 / (member_total - 1)
    tile_weight = jnp.maximum(0.0, 1.0 - taper_class.astype(jnp.float32) / REACH)
    weight_cols = jnp.repeat(tile_weight, OBS_ROW, axis=1)
    row_ensemble = ensemble.reshape(member_total, NTILE, OBS_ROW).transpose(1, 0, 2)
    row_pos = track_pos.reshape(NTILE, OBS_ROW)

    def apply_matrix(direction):
        def one_row(entry):
            block_ens, block_pos, block_weight = entry
            product = jnp.dot(block_ens.T, ensemble, precision=lax.Precision.HIGHEST)
            distance = block_pos[:, None] - track_pos[None, :]
            taper = block_weight[None, :] * jnp.exp(-(distance * distance) / track_width)
            tile_rows = product * (taper * inverse_members)
            return jnp.dot(tile_rows, direction, precision=lax.Precision.HIGHEST)

        return lax.map(one_row, (row_ensemble, row_pos, weight_cols)).reshape(NOBS)

    solution = jnp.zeros_like(innovations)
    residual = innovations
    direction = innovations
    norm_now = jnp.sum(residual * residual)
    for turn_index in range(ITERS):
        image = apply_matrix(direction) + obs_error * direction
        alpha = norm_now / jnp.sum(direction * image)
        solution = solution + alpha * direction
        residual = residual - alpha * image
        if turn_index + 1 < ITERS:
            norm_next = jnp.sum(residual * residual)
            direction = residual + (norm_next / norm_now) * direction
            norm_now = norm_next
    return solution, residual
```

```python
import functools

import jax
import jax.numpy as jnp
from jax import lax
from jax.experimental import pallas as pl
from jax.experimental.pallas import tpu as pltpu
from jax.sharding import PartitionSpec as P

ITERS = 2
LANES = 128


track_width = 0.0001


def share_kernel(reach_tiles, inverse_members, class_ref, pos_ref, own_ref, mate_ref, share_ref, both, turned, column):
    tiles = class_ref.shape[0]
    members, total_obs = own_ref.shape
    block_len = total_obs // tiles
    both[:members, :] = own_ref[...]
    both[members:, :] = mate_ref[...]
    turned[:, :members] = own_ref[...].T
    turned[:, members:] = mate_ref[...].T
    for piece in range(total_obs // LANES):
        at = piece * LANES
        row = jnp.broadcast_to(pos_ref[:, at : at + LANES], (LANES, LANES))
        column[at : at + LANES, :] = row.T
    rows = 128

    def one_pair(pair, carry):
        a, b = pair // tiles, pair % tiles
        klass = class_ref[a, b]

        @pl.when(klass < reach_tiles)
        def _():
            weight = jnp.maximum(0.0, 1.0 - klass.astype(jnp.float32) / reach_tiles)
            columns = pl.ds(pl.multiple_of(b * block_len, LANES), block_len)
            right = both[:, columns]
            right_pos = pos_ref[:, columns]

            def one_chunk(chunk, carry):
                at = pl.ds(pl.multiple_of(a * block_len + chunk * rows, rows), rows)
                product = jnp.dot(turned[at, :], right, preferred_element_type=jnp.float32)
                left_pos = jnp.concatenate([column[at, :]] * (block_len // LANES), axis=1)
                distance = left_pos - right_pos
                taper = weight * jnp.exp(-(distance * distance) * (1.0 / track_width))
                share_ref[at, columns] = product * (taper * inverse_members)
                return carry

            lax.fori_loop(0, block_len // rows, one_chunk, 0)

        return carry

    lax.fori_loop(0, tiles * tiles, one_pair, 0)


def apply_share(reach_tiles, class_ref, share_ref, vector, sums, out_ref):
    tiles = class_ref.shape[0]
    total_obs = share_ref.shape[0]
    block_len = total_obs // tiles
    pieces = block_len // LANES
    rows = 64

    def add_tile(a, b, first):
        def one_chunk(chunk, carry):
            at = pl.ds(pl.multiple_of(a * block_len + chunk * rows, rows), rows)
            total = None if first else sums[at, :]
            for piece in range(pieces):
                begin = b * block_len + piece * LANES
                term = share_ref[at, begin : begin + LANES] * vector[b * pieces + piece : b * pieces + piece + 1, :]
                total = term if total is None else total + term
            sums[at, :] = total
            return carry

        lax.fori_loop(0, block_len // rows, one_chunk, 0)

    for a in range(tiles):
        add_tile(a, a, True)
        for b in range(tiles):
            if b != a:
                pl.when(class_ref[a, b] < reach_tiles)(functools.partial(add_tile, a, b, False))
    ones = jnp.ones((8, LANES), jnp.float32)
    for piece in range(total_obs // LANES):
        folded = lax.dot_general(
            ones,
            sums[piece * LANES : (piece + 1) * LANES, :],
            (((1,), (1,)), ((), ())),
            precision=lax.Precision.HIGHEST,
            preferred_element_type=jnp.float32,
        )
        out_ref[piece : piece + 1, :] = folded[0:1, :]


def first_kernel(reach_tiles, class_ref, share_ref, vectors_ref, out_ref, vector, sums):
    vector[...] = vectors_ref[:, :LANES]
    apply_share(reach_tiles, class_ref, share_ref, vector, sums, out_ref)


def total_of(x):
    return jnp.sum(jnp.sum(x, axis=0, keepdims=True), axis=1, keepdims=True)


def second_kernel(reach_tiles, peers, place_ref, class_ref, share_ref, vectors_ref, *refs):
    parts, refs = refs[:peers], refs[peers:]
    sent, refs = refs[:peers], refs[peers:]
    state_ref, direction, residual, start, sums, product = refs
    innovations, obs_error = vectors_ref[:, :LANES], vectors_ref[:, LANES:]
    image = obs_error * innovations
    for part in parts:
        image = image + part[...]
    norm_now = total_of(innovations * innovations)
    alpha = norm_now / total_of(innovations * image)
    residual_now = innovations - alpha * image
    norm_next = total_of(residual_now * residual_now)
    direction_now = residual_now + (norm_next / norm_now) * innovations
    residual[...] = residual_now
    direction[...] = direction_now
    start[...] = alpha * innovations
    apply_share(reach_tiles, class_ref, share_ref, direction, sums, product)
    curvature = total_of(direction_now * product[...])
    extra = obs_error * direction_now
    own_curvature = total_of(direction_now * extra)
    row_index, within, per_row = place_ref[0], place_ref[1], place_ref[2]
    for peer in range(peers):
        at = (row_index ^ peer) * per_row + within
        sent[peer][0:1, :] = product[pl.ds(at, 1), :]
        sent[peer][1:2, :] = jnp.broadcast_to(curvature, (1, LANES))
    own = row_index * per_row + within
    state_ref[0:1, :] = start[pl.ds(own, 1), :]
    state_ref[1:2, :] = residual[pl.ds(own, 1), :]
    state_ref[2:3, :] = direction[pl.ds(own, 1), :]
    product[...] = extra
    state_ref[3:4, :] = product[pl.ds(own, 1), :]
    state_ref[4:5, :] = jnp.broadcast_to(norm_next, (1, LANES))
    state_ref[5:6, :] = jnp.broadcast_to(own_curvature, (1, LANES))


VMEM_SPEC = pl.BlockSpec(memory_space=pltpu.VMEM)
SMEM_SPEC = pl.BlockSpec(memory_space=pltpu.SMEM)


def swap_rows(x, mask):
    row_count = lax.axis_size("row")
    return lax.ppermute(x, "row", [(i, i ^ mask) for i in range(row_count)])


def vectors_only(anomalies, innovations, obs_error, track_pos, taper_class):
    row_count = lax.axis_size("row")
    col_count = lax.axis_size("col")
    sub_count = lax.axis_size("sub")
    row_index = lax.axis_index("row")
    within = lax.axis_index("col") * sub_count + lax.axis_index("sub")
    local_members, total_obs = anomalies.shape
    member_total = local_members * row_count * sub_count
    inverse_members = 1.0 / (member_total - 1)
    reach_tiles = max(2, row_count // 4)
    per_row = col_count * sub_count
    devices = row_count * per_row
    pieces = total_obs // LANES
    f32 = jnp.float32

    packed = jnp.concatenate([innovations, obs_error]).reshape(1, 2 * LANES)
    packed = jnp.broadcast_to(packed, (devices, 2 * LANES))
    vectors = lax.all_to_all(packed, ("row", "col", "sub"), split_axis=0, concat_axis=0, tiled=True)
    mate = lax.ppermute(anomalies, "sub", [(0, 1), (1, 0)])

    params = pltpu.CompilerParams(vmem_limit_bytes=16 * 1024 * 1024)
    share = pl.pallas_call(
        functools.partial(share_kernel, reach_tiles, inverse_members),
        out_shape=pltpu.VMEM((total_obs, total_obs), f32),
        in_specs=[SMEM_SPEC, VMEM_SPEC, VMEM_SPEC, VMEM_SPEC],
        out_specs=VMEM_SPEC,
        scratch_shapes=[
            pltpu.VMEM((2 * local_members, total_obs), anomalies.dtype),
            pltpu.VMEM((total_obs, 2 * local_members), anomalies.dtype),
            pltpu.VMEM((total_obs, LANES), f32),
        ],
        compiler_params=params,
        cost_estimate=pl.CostEstimate(
            flops=4 * local_members * total_obs * total_obs,
            bytes_accessed=4 * local_members * total_obs,
            transcendentals=total_obs * total_obs,
        ),
        name="share",
    )(taper_class, track_pos.reshape(1, total_obs), anomalies, mate)

    part = pl.pallas_call(
        functools.partial(first_kernel, reach_tiles),
        out_shape=pltpu.VMEM((pieces, LANES), f32),
        in_specs=[SMEM_SPEC, VMEM_SPEC, VMEM_SPEC],
        out_specs=VMEM_SPEC,
        scratch_shapes=[pltpu.VMEM((pieces, LANES), f32), pltpu.VMEM((total_obs, LANES), f32)],
        compiler_params=params,
        name="first",
    )(taper_class, share, vectors)
    parts = [part] + [swap_rows(part, mask) for mask in range(1, row_count)]

    place = jnp.stack([row_index, within, jnp.int32(per_row)]).astype(jnp.int32)
    *sent, state = pl.pallas_call(
        functools.partial(second_kernel, reach_tiles, row_count),
        out_shape=[pltpu.VMEM((8, LANES), f32) for _ in range(row_count + 1)],
        in_specs=[SMEM_SPEC, SMEM_SPEC, VMEM_SPEC, VMEM_SPEC] + [VMEM_SPEC] * row_count,
        out_specs=[VMEM_SPEC] * (row_count + 1),
        scratch_shapes=[pltpu.VMEM((pieces, LANES), f32)] * 3
        + [pltpu.VMEM((total_obs, LANES), f32), pltpu.VMEM((pieces, LANES), f32)],
        compiler_params=params,
        name="second",
    )(place, taper_class, share, vectors, *parts)
    got = [sent[0]] + [swap_rows(sent[mask], mask) for mask in range(1, row_count)]
    image, curvature = state[3], state[5]
    for piece in got:
        image = image + piece[0]
        curvature = curvature + piece[1]
    alpha = state[4] / curvature
    return state[0] + alpha * state[2], state[1] - alpha * image


def fits(anomalies, innovations, obs_error, track_pos, taper_class):
    row_count = lax.axis_size("row")
    local_members, total_obs = anomalies.shape
    share_bytes = 4 * total_obs * total_obs
    return (
        ITERS == 2
        and row_count in (2, 4)
        and lax.axis_size("sub") == 2
        and innovations.shape[0] == LANES
        and total_obs % (row_count * LANES) == 0
        and local_members % LANES == 0
        and share_bytes <= 16 * 1024 * 1024
    )


def per_device(*args):
    return vectors_only(*args) if fits(*args) else blocks(*args)


def squares(residual):
    return lax.psum(jnp.sum(residual * residual), ("row", "col", "sub"))


def blocks(anomalies, innovations, obs_error, track_pos, taper_class):
    row_count = lax.axis_size("row")
    col_count = lax.axis_size("col")
    sub_count = lax.axis_size("sub")
    row_index = lax.axis_index("row")
    col_index = lax.axis_index("col")
    local_members, total_obs = anomalies.shape
    block_len = total_obs // row_count
    quarter_len = block_len // col_count
    member_total = local_members * row_count * sub_count
    inverse_members = 1.0 / (member_total - 1)
    reach_tiles = max(2, row_count // 4)
    class_row = lax.dynamic_index_in_dim(taper_class, row_index, 0, keepdims=False)
    tile_weight = jnp.maximum(0.0, 1.0 - class_row.astype(jnp.float32) / reach_tiles)
    row_pos = lax.dynamic_slice_in_dim(track_pos, row_index * block_len, block_len, 0)
    col_pos = lax.dynamic_index_in_dim(
        track_pos.reshape(row_count, col_count, quarter_len), col_index, 1, keepdims=False
    )
    own_block = lax.all_to_all(anomalies, "row", split_axis=1, concat_axis=0, tiled=True)
    own_quarter = lax.dynamic_slice_in_dim(own_block, col_index * quarter_len, quarter_len, 1)

    def one_tile(piece, block_index, keep_factor):
        product = jnp.einsum("mi,mq->iq", own_block, piece, preferred_element_type=jnp.float32)
        column_pos = lax.dynamic_index_in_dim(col_pos, block_index, 0, keepdims=False)
        weight_here = lax.dynamic_index_in_dim(tile_weight, block_index, 0, keepdims=False)
        distance = row_pos[:, None] - column_pos[None, :]
        taper = weight_here * keep_factor * jnp.exp(-(distance * distance) / track_width)
        return product * (taper * inverse_members)

    def one_entry(entry):
        return one_tile(entry[0], entry[1], 1.0)

    piece = lax.all_gather(own_quarter[None], "row", axis=0, tiled=True)
    indices = jnp.arange(piece.shape[0], dtype=jnp.int32)
    tiles = lax.map(one_entry, (piece, indices))
    solution = jnp.zeros_like(innovations)
    residual = innovations
    direction_vec = innovations
    norm_now = squares(residual)
    for turn_index in range(ITERS):
        column_vec = lax.all_gather(direction_vec, ("row", "sub"), axis=0, tiled=True).reshape(
            row_count, quarter_len
        )
        direct = jnp.einsum("jiq,jq->i", tiles, column_vec, precision=lax.Precision.HIGHEST)
        extra = obs_error * direction_vec
        own_part = lax.psum_scatter(direct, ("col", "sub"), scatter_dimension=0, tiled=True)
        image = own_part + extra
        alpha = norm_now / lax.psum(jnp.sum(direction_vec * image), ("row", "col", "sub"))
        solution = solution + alpha * direction_vec
        residual = residual - alpha * image
        if turn_index + 1 < ITERS:
            norm_next = squares(residual)
            direction_vec = residual + norm_next / norm_now * direction_vec
            norm_now = norm_next
    return (solution, residual)


def solution(mesh):
    in_specs = (
        P(("group", "row", "sub"), None),
        P(("group", "row", "col", "sub")),
        P(("group", "row", "col", "sub")),
        P("group"),
        P("group", None),
    )
    out_specs = (P(("group", "row", "col", "sub")), P(("group", "row", "col", "sub")))
    return jax.shard_map(
        per_device, mesh=mesh, in_specs=in_specs, out_specs=out_specs, check_vma=False
    )
```

```python
import functools
import math

import jax
import jax.numpy as jnp
from jax import lax
from jax.experimental import pallas as pl
from jax.experimental.pallas import tpu as pltpu
from jax.sharding import PartitionSpec as P

ITERS = 2
LANES = 128


track_width = 0.0001
exp2_rate = -math.log2(math.e) / track_width


def for_each_pair(reach_tiles, class_ref, action):
    tiles = class_ref.shape[0]

    def one_pair(pair, carry):
        a, b = pair // tiles, pair % tiles
        pl.when(class_ref[a, b] < reach_tiles)(lambda: action(pair, a, b))
        return carry

    lax.fori_loop(0, tiles * tiles, one_pair, 0)


def tile_at(a, b, block_len):
    top = pl.multiple_of(a * block_len, LANES)
    left = pl.multiple_of(b * block_len, LANES)
    return pl.ds(top, block_len), pl.ds(left, block_len)


def pack_kernel(innovations_ref, obs_error_ref, packed_ref, row, arrived):
    copies = [
        pltpu.make_async_copy(ref, row.at[:, pl.ds(at * LANES, LANES)], arrived.at[at])
        for at, ref in enumerate((innovations_ref, obs_error_ref))
    ]
    for copy in copies:
        copy.start()
    for copy in copies:
        copy.wait()
    packed_ref[...] = jnp.broadcast_to(row[...], packed_ref.shape)


def share_kernel(reach_tiles, class_hbm, pos_hbm, own_ref, mate_ref, share_ref, *scratch):
    class_ref, pos_ref, both, turned, column, tiles_here, arrived, left = scratch
    members, total_obs = own_ref.shape
    block_len = total_obs // class_ref.shape[0]
    pos_copy = pltpu.make_async_copy(pos_hbm, pos_ref, arrived.at[0])
    own_copy = pltpu.make_async_copy(own_ref, both.at[pl.ds(0, members), :], arrived.at[1])
    class_copy = pltpu.make_async_copy(class_hbm, class_ref, arrived.at[2])
    for copy in (pos_copy, own_copy, class_copy):
        copy.start()
    both[members:, :] = mate_ref[...]
    turned[:, members:] = mate_ref[...].T
    pos_copy.wait()
    spread_columns(pos_ref[...], column)
    own_copy.wait()
    turned[:, :members] = both[:members, :].T
    class_copy.wait()
    rows = 128

    def out_copy(pair, a, b):
        at = tile_at(a, b, block_len)
        return pltpu.make_async_copy(tiles_here.at[at], share_ref.at[at], left.at[pair])

    def make_tile(pair, a, b):
        at = tile_at(a, b, block_len)
        right = both[:, at[1]]
        right_pos = pos_ref[:, at[1]]
        left_turned, left_column, tile = turned.at[at[0], :], column.at[at[0], :], tiles_here.at[at]
        for begin in range(0, block_len, rows):
            part = slice(begin, begin + rows)
            product = jnp.dot(left_turned[part, :], right, preferred_element_type=jnp.float32)
            left_pos = jnp.concatenate([left_column[part, :]] * (block_len // LANES), axis=1)
            distance = left_pos - right_pos
            tile[part, :] = product * jnp.exp2(distance * distance * exp2_rate)
        out_copy(pair, a, b).start()

    for_each_pair(reach_tiles, class_ref, make_tile)
    for_each_pair(reach_tiles, class_ref, lambda *at: out_copy(*at).wait())


def spread_columns(row, column):
    for begin in range(0, column.shape[0], LANES):
        square = jnp.broadcast_to(row[:, begin : begin + LANES], (LANES, LANES))
        column[begin : begin + LANES, :] = square.T


def apply_share(reach_tiles, inverse_members, class_ref, share_ref, vector, column, sums, out_ref, ready=None):
    total_obs = share_ref.shape[0]
    block_len = total_obs // class_ref.shape[0]
    lanes = block_len // LANES
    for piece in range(total_obs // LANES):
        square = jnp.broadcast_to(vector[piece : piece + 1, :], (LANES, LANES))
        column[piece * LANES : (piece + 1) * LANES, :] = square.T
    sums[...] = jnp.zeros_like(sums)

    def add_tile(pair, a, b):
        if ready is not None:
            ready(pair, a, b)
        weight = jnp.maximum(0.0, 1.0 - class_ref[a, b].astype(jnp.float32) / reach_tiles) * inverse_members
        at = tile_at(a, b, block_len)
        tile, factor = share_ref.at[at], column.at[at[0], :]
        totals = [None] * lanes
        for begin in range(0, block_len, 8):
            part = slice(begin, begin + 8)
            for lane in range(lanes):
                term = tile[part, lane * LANES : (lane + 1) * LANES] * factor[part, :]
                totals[lane] = term if totals[lane] is None else totals[lane] + term
        into = sums.at[:, at[1]]
        for lane in range(lanes):
            into[:, lane * LANES : (lane + 1) * LANES] += weight * totals[lane]

    for_each_pair(reach_tiles, class_ref, add_tile)
    for piece in range(total_obs // LANES):
        out_ref[piece : piece + 1, :] = jnp.sum(sums[:, piece * LANES : (piece + 1) * LANES], axis=0, keepdims=True)


def first_kernel(
    reach_tiles, inverse_members, class_ref, stored_ref, vectors_ref, share_ref, out_ref, vector, column, sums, arrived
):
    block_len = stored_ref.shape[0] // class_ref.shape[0]

    def in_copy(pair, a, b):
        at = tile_at(a, b, block_len)
        return pltpu.make_async_copy(stored_ref.at[at], share_ref.at[at], arrived.at[pair])

    for_each_pair(reach_tiles, class_ref, lambda *at: in_copy(*at).start())
    vector[...] = vectors_ref[:, 0, :LANES]
    ready = lambda *at: in_copy(*at).wait()
    apply_share(reach_tiles, inverse_members, class_ref, share_ref, vector, column, sums, out_ref, ready)


def total_of(x):
    return jnp.sum(jnp.sum(x, axis=0, keepdims=True), axis=1, keepdims=True)


def second_kernel(reach_tiles, inverse_members, peers, place_ref, class_ref, share_ref, vectors_ref, *refs):
    parts, refs = refs[:peers], refs[peers:]
    sent, refs = refs[:peers], refs[peers:]
    state_ref, direction, residual, start, column, sums, product = refs
    innovations, obs_error = vectors_ref[:, 0, :LANES], vectors_ref[:, 0, LANES:]
    image = obs_error * innovations
    for part in parts:
        image = image + part[...]
    norm_now = total_of(innovations * innovations)
    alpha = norm_now / total_of(innovations * image)
    residual_now = innovations - alpha * image
    norm_next = total_of(residual_now * residual_now)
    direction_now = residual_now + (norm_next / norm_now) * innovations
    residual[...] = residual_now
    direction[...] = direction_now
    start[...] = alpha * innovations
    apply_share(reach_tiles, inverse_members, class_ref, share_ref, direction, column, sums, product)
    curvature = total_of(direction_now * product[...])
    extra = obs_error * direction_now
    own_curvature = total_of(direction_now * extra)
    row_index, within, per_row = place_ref[0], place_ref[1], place_ref[2]
    for peer in range(peers):
        at = (row_index ^ peer) * per_row + within
        sent[peer][0:1, :] = product[pl.ds(at, 1), :]
        sent[peer][1:2, :] = jnp.broadcast_to(curvature, (1, LANES))
    own = row_index * per_row + within
    state_ref[0:1, :] = start[pl.ds(own, 1), :]
    state_ref[1:2, :] = residual[pl.ds(own, 1), :]
    state_ref[2:3, :] = direction[pl.ds(own, 1), :]
    product[...] = extra
    state_ref[3:4, :] = product[pl.ds(own, 1), :]
    state_ref[4:5, :] = jnp.broadcast_to(norm_next, (1, LANES))
    state_ref[5:6, :] = jnp.broadcast_to(own_curvature, (1, LANES))


def last_kernel(state_ref, *refs):
    parts, (solution_ref, residual_ref) = refs[:-2], refs[-2:]
    image, curvature = state_ref[3:4, :], state_ref[5:6, :]
    for part in parts:
        image = image + part[0:1, :]
        curvature = curvature + part[1:2, :]
    alpha = state_ref[4:5, :] / curvature
    solution_ref[...] = state_ref[0:1, :] + alpha * state_ref[2:3, :]
    residual_ref[...] = state_ref[1:2, :] - alpha * image


VMEM_SPEC = pl.BlockSpec(memory_space=pltpu.VMEM)
SMEM_SPEC = pl.BlockSpec(memory_space=pltpu.SMEM)
HBM_SPEC = pl.BlockSpec(memory_space=pltpu.HBM)


def in_hbm(x):
    return pltpu.with_memory_space_constraint(x, pltpu.HBM)


def swap_rows(x, mask):
    row_count = lax.axis_size("row")
    return lax.ppermute(x, "row", [(i, i ^ mask) for i in range(row_count)])


def vectors_only(anomalies, innovations, obs_error, track_pos, taper_class):
    row_count = lax.axis_size("row")
    col_count = lax.axis_size("col")
    sub_count = lax.axis_size("sub")
    row_index = lax.axis_index("row")
    within = lax.axis_index("col") * sub_count + lax.axis_index("sub")
    local_members, total_obs = anomalies.shape
    member_total = local_members * row_count * sub_count
    inverse_members = 1.0 / (member_total - 1)
    reach_tiles = max(2, row_count // 4)
    per_row = col_count * sub_count
    devices = row_count * per_row
    pieces = total_obs // LANES
    f32 = jnp.float32

    packed = pl.pallas_call(
        pack_kernel,
        out_shape=pltpu.VMEM((devices, 1, 2 * LANES), f32),
        in_specs=[HBM_SPEC, HBM_SPEC],
        out_specs=VMEM_SPEC,
        scratch_shapes=[pltpu.VMEM((1, 2 * LANES), f32), pltpu.SemaphoreType.DMA((2,))],
        compiler_params=pltpu.CompilerParams(vmem_limit_bytes=1024 * 1024),
        name="pack",
    )(in_hbm(innovations.reshape(1, LANES)), in_hbm(obs_error.reshape(1, LANES)))
    mate = lax.ppermute(anomalies, "sub", [(0, 1), (1, 0)])

    pairs = row_count * row_count
    share = pl.pallas_call(
        functools.partial(share_kernel, reach_tiles),
        out_shape=jax.ShapeDtypeStruct((total_obs, total_obs), f32),
        in_specs=[HBM_SPEC, HBM_SPEC, HBM_SPEC, VMEM_SPEC],
        out_specs=HBM_SPEC,
        scratch_shapes=[
            pltpu.SMEM(taper_class.shape, jnp.int32),
            pltpu.VMEM((1, total_obs), f32),
            pltpu.VMEM((2 * local_members, total_obs), anomalies.dtype),
            pltpu.VMEM((total_obs, 2 * local_members), anomalies.dtype),
            pltpu.VMEM((total_obs, LANES), f32),
            pltpu.VMEM((total_obs, total_obs), f32),
            pltpu.SemaphoreType.DMA((3,)),
            pltpu.SemaphoreType.DMA((pairs,)),
        ],
        compiler_params=pltpu.CompilerParams(vmem_limit_bytes=40 * 1024 * 1024),
        cost_estimate=pl.CostEstimate(
            flops=4 * local_members * total_obs * total_obs,
            bytes_accessed=4 * total_obs * total_obs,
            transcendentals=total_obs * total_obs,
        ),
        name="share",
    )(in_hbm(taper_class), in_hbm(track_pos.reshape(1, total_obs)), in_hbm(anomalies), mate)
    vectors = lax.all_to_all(packed, ("row", "col", "sub"), split_axis=0, concat_axis=0, tiled=True)

    params = pltpu.CompilerParams(vmem_limit_bytes=8 * 1024 * 1024)
    share, part = pl.pallas_call(
        functools.partial(first_kernel, reach_tiles, inverse_members),
        out_shape=[pltpu.VMEM((total_obs, total_obs), f32), pltpu.VMEM((pieces, LANES), f32)],
        in_specs=[SMEM_SPEC, HBM_SPEC, VMEM_SPEC],
        out_specs=[VMEM_SPEC, VMEM_SPEC],
        scratch_shapes=[
            pltpu.VMEM((pieces, LANES), f32),
            pltpu.VMEM((total_obs, LANES), f32),
            pltpu.VMEM((8, total_obs), f32),
            pltpu.SemaphoreType.DMA((pairs,)),
        ],
        compiler_params=params,
        name="first",
    )(taper_class, in_hbm(share), vectors)
    parts = [part] + [swap_rows(part, mask) for mask in range(1, row_count)]

    place = jnp.stack([row_index, within, jnp.int32(per_row)]).astype(jnp.int32)
    *sent, state = pl.pallas_call(
        functools.partial(second_kernel, reach_tiles, inverse_members, row_count),
        out_shape=[pltpu.VMEM((8, LANES), f32) for _ in range(row_count + 1)],
        in_specs=[SMEM_SPEC, SMEM_SPEC, VMEM_SPEC, VMEM_SPEC] + [VMEM_SPEC] * row_count,
        out_specs=[VMEM_SPEC] * (row_count + 1),
        scratch_shapes=[pltpu.VMEM((pieces, LANES), f32)] * 3
        + [
            pltpu.VMEM((total_obs, LANES), f32),
            pltpu.VMEM((8, total_obs), f32),
            pltpu.VMEM((pieces, LANES), f32),
        ],
        compiler_params=params,
        name="second",
    )(place, taper_class, share, vectors, *parts)
    got = [sent[0]] + [swap_rows(sent[mask], mask) for mask in range(1, row_count)]
    solution_part, residual_part = pl.pallas_call(
        last_kernel,
        out_shape=[jax.ShapeDtypeStruct((1, LANES), f32)] * 2,
        in_specs=[VMEM_SPEC] * (row_count + 1),
        out_specs=[VMEM_SPEC] * 2,
        compiler_params=pltpu.CompilerParams(vmem_limit_bytes=1024 * 1024),
        name="last",
    )(state, *got)
    return solution_part.reshape(LANES), residual_part.reshape(LANES)


def fits(anomalies, innovations, obs_error, track_pos, taper_class):
    row_count = lax.axis_size("row")
    local_members, total_obs = anomalies.shape
    share_bytes = 4 * total_obs * total_obs
    return (
        ITERS == 2
        and row_count in (2, 4)
        and lax.axis_size("sub") == 2
        and innovations.shape[0] == LANES
        and total_obs % (row_count * LANES) == 0
        and local_members % LANES == 0
        and share_bytes <= 16 * 1024 * 1024
    )


def per_device(*args):
    return vectors_only(*args) if fits(*args) else blocks(*args)


def squares(residual):
    return lax.psum(jnp.sum(residual * residual), ("row", "col", "sub"))


def blocks(anomalies, innovations, obs_error, track_pos, taper_class):
    row_count = lax.axis_size("row")
    col_count = lax.axis_size("col")
    sub_count = lax.axis_size("sub")
    row_index = lax.axis_index("row")
    col_index = lax.axis_index("col")
    local_members, total_obs = anomalies.shape
    block_len = total_obs // row_count
    quarter_len = block_len // col_count
    member_total = local_members * row_count * sub_count
    inverse_members = 1.0 / (member_total - 1)
    reach_tiles = max(2, row_count // 4)
    class_row = lax.dynamic_index_in_dim(taper_class, row_index, 0, keepdims=False)
    tile_weight = jnp.maximum(0.0, 1.0 - class_row.astype(jnp.float32) / reach_tiles)
    row_pos = lax.dynamic_slice_in_dim(track_pos, row_index * block_len, block_len, 0)
    col_pos = lax.dynamic_index_in_dim(
        track_pos.reshape(row_count, col_count, quarter_len), col_index, 1, keepdims=False
    )
    own_block = lax.all_to_all(anomalies, "row", split_axis=1, concat_axis=0, tiled=True)
    own_quarter = lax.dynamic_slice_in_dim(own_block, col_index * quarter_len, quarter_len, 1)

    def one_tile(piece, block_index, keep_factor):
        product = jnp.einsum("mi,mq->iq", own_block, piece, preferred_element_type=jnp.float32)
        column_pos = lax.dynamic_index_in_dim(col_pos, block_index, 0, keepdims=False)
        weight_here = lax.dynamic_index_in_dim(tile_weight, block_index, 0, keepdims=False)
        distance = row_pos[:, None] - column_pos[None, :]
        taper = weight_here * keep_factor * jnp.exp(-(distance * distance) / track_width)
        return product * (taper * inverse_members)

    def one_entry(entry):
        return one_tile(entry[0], entry[1], 1.0)

    piece = lax.all_gather(own_quarter[None], "row", axis=0, tiled=True)
    indices = jnp.arange(piece.shape[0], dtype=jnp.int32)
    tiles = lax.map(one_entry, (piece, indices))
    solution = jnp.zeros_like(innovations)
    residual = innovations
    direction_vec = innovations
    norm_now = squares(residual)
    for turn_index in range(ITERS):
        column_vec = lax.all_gather(direction_vec, ("row", "sub"), axis=0, tiled=True).reshape(
            row_count, quarter_len
        )
        direct = jnp.einsum("jiq,jq->i", tiles, column_vec, precision=lax.Precision.HIGHEST)
        extra = obs_error * direction_vec
        own_part = lax.psum_scatter(direct, ("col", "sub"), scatter_dimension=0, tiled=True)
        image = own_part + extra
        alpha = norm_now / lax.psum(jnp.sum(direction_vec * image), ("row", "col", "sub"))
        solution = solution + alpha * direction_vec
        residual = residual - alpha * image
        if turn_index + 1 < ITERS:
            norm_next = squares(residual)
            direction_vec = residual + norm_next / norm_now * direction_vec
            norm_now = norm_next
    return (solution, residual)


def solution(mesh):
    in_specs = (
        P(("group", "row", "sub"), None),
        P(("group", "row", "col", "sub")),
        P(("group", "row", "col", "sub")),
        P("group"),
        P("group", None),
    )
    out_specs = (P(("group", "row", "col", "sub")), P(("group", "row", "col", "sub")))
    return jax.shard_map(
        per_device, mesh=mesh, in_specs=in_specs, out_specs=out_specs, check_vma=False
    )
```

```python
import functools
import math

import jax
import jax.numpy as jnp
from jax import lax
from jax.experimental import pallas as pl
from jax.experimental.pallas import tpu as pltpu
from jax.sharding import PartitionSpec as P

ITERS = 2
LANES = 128
KEPT_BYTES = 3 * 1024 * 1024


track_width = 0.0001
exp2_rate = -math.log2(math.e) / track_width


def off_diagonal(tiles):
    return tiles * (tiles - 1) // 2


def for_each_pair(reach_tiles, class_ref, action):
    tiles = class_ref.shape[0]

    def one_pair(pair, carry):
        a, b = pair // tiles, pair % tiles
        slot = a * tiles - (a * (a + 1)) // 2 + b - a - 1
        pl.when(jnp.logical_and(a < b, class_ref[a, b] < reach_tiles))(lambda: action(slot, a, b))
        return carry

    lax.fori_loop(0, tiles * tiles, one_pair, 0)


def block_at(a, block_len):
    return pl.ds(pl.multiple_of(a * block_len, LANES), block_len)


def pack_kernel(innovations_ref, obs_error_ref, packed_ref, row, arrived):
    copies = [
        pltpu.make_async_copy(ref, row.at[:, pl.ds(at * LANES, LANES)], arrived.at[at])
        for at, ref in enumerate((innovations_ref, obs_error_ref))
    ]
    for copy in copies:
        copy.start()
    for copy in copies:
        copy.wait()
    packed_ref[...] = jnp.broadcast_to(row[...], packed_ref.shape)


def share_kernel(reach_tiles, class_hbm, pos_hbm, own_ref, mate_ref, kept_ref, stored_ref, *scratch):
    class_ref, pos_ref, both, turned, column, made, arrived, left = scratch
    members, total_obs = own_ref.shape
    tiles = class_ref.shape[0]
    block_len = total_obs // tiles
    kept = kept_ref.shape[0]
    pos_copy = pltpu.make_async_copy(pos_hbm, pos_ref, arrived.at[0])
    own_copy = pltpu.make_async_copy(own_ref, both.at[pl.ds(0, members), :], arrived.at[1])
    class_copy = pltpu.make_async_copy(class_hbm, class_ref, arrived.at[2])
    mate_copy = pltpu.make_async_copy(mate_ref, both.at[pl.ds(members, members), :], arrived.at[3])
    for copy in (pos_copy, own_copy, mate_copy, class_copy):
        copy.start()
    pos_copy.wait()
    spread_columns(pos_ref[...], column)
    own_copy.wait()
    turned[:, :members] = both[:members, :].T
    mate_copy.wait()
    turned[:, members:] = both[members:, :].T
    class_copy.wait()
    rows = 128

    def out_copy(slot):
        return pltpu.make_async_copy(made.at[slot], stored_ref.at[slot], left.at[slot])

    def make_tile(tile, a, b):
        rows_at, columns_at = block_at(a, block_len), block_at(b, block_len)
        right = both[:, columns_at]
        right_pos = pos_ref[:, columns_at]
        left_turned, left_column = turned.at[rows_at, :], column.at[rows_at, :]
        for begin in range(0, block_len, rows):
            part = slice(begin, begin + rows)
            product = jnp.dot(left_turned[part, :], right, preferred_element_type=jnp.float32)
            left_pos = jnp.concatenate([left_column[part, :]] * (block_len // LANES), axis=1)
            distance = left_pos - right_pos
            tile[part, :] = product * jnp.exp2(distance * distance * exp2_rate)

    def make_pair(slot, a, b):
        slot = slot + tiles - kept
        make_tile(made.at[slot], a, b)
        out_copy(slot).start()

    def make_stored(slot, carry):
        make_tile(made.at[slot], slot + kept, slot + kept)
        out_copy(slot).start()
        return carry

    def make_kept(slot, carry):
        make_tile(kept_ref.at[slot], slot, slot)
        return carry

    for_each_pair(reach_tiles, class_ref, make_pair)
    lax.fori_loop(0, tiles - kept, make_stored, 0)
    lax.fori_loop(0, kept, make_kept, 0)
    for_each_pair(reach_tiles, class_ref, lambda slot, a, b: out_copy(slot + tiles - kept).wait())
    for slot in range(tiles - kept):
        out_copy(slot).wait()


def spread_columns(row, column):
    for begin in range(0, column.shape[0], LANES):
        square = jnp.broadcast_to(row[:, begin : begin + LANES], (LANES, LANES))
        column[begin : begin + LANES, :] = square.T


def apply_share(
    reach_tiles, inverse_members, class_ref, kept_ref, stored_ref, vector, column, across, sums, out_ref, ready=None
):
    tiles = class_ref.shape[0]
    kept = kept_ref.shape[0]
    block_len = kept_ref.shape[1]
    lanes = block_len // LANES
    for piece in range(tiles * lanes):
        square = jnp.broadcast_to(vector[piece : piece + 1, :], (LANES, LANES))
        column[piece * LANES : (piece + 1) * LANES, :] = square.T
    sums[...] = jnp.zeros_like(sums)

    def add_diagonal(tile, a):
        at = block_at(a, block_len)
        factor = column.at[at, :]
        totals = [None] * lanes
        for begin in range(0, block_len, 8):
            part = slice(begin, begin + 8)
            for lane in range(lanes):
                term = tile[part, lane * LANES : (lane + 1) * LANES] * factor[part, :]
                totals[lane] = term if totals[lane] is None else totals[lane] + term
        into = sums.at[:, at]
        for lane in range(lanes):
            into[:, lane * LANES : (lane + 1) * LANES] += tile_weight(class_ref[a, a]) * totals[lane]

    def tile_weight(klass):
        return jnp.maximum(0.0, 1.0 - klass.astype(jnp.float32) / reach_tiles) * inverse_members

    def add_pair(slot, a, b):
        slot = slot + tiles - kept
        if ready is not None:
            ready(slot)
        weight = tile_weight(class_ref[a, b])
        at_a, at_b = block_at(a, block_len), block_at(b, block_len)
        tile, factor = stored_ref.at[slot], column.at[at_a, :]
        rows_b = [jnp.broadcast_to(vector[pl.ds(b * lanes + lane, 1), :], (8, LANES)) for lane in range(lanes)]
        totals = [None] * lanes
        for begin in range(0, block_len, 8):
            part = slice(begin, begin + 8)
            line = None
            for lane in range(lanes):
                here = tile[part, lane * LANES : (lane + 1) * LANES]
                term = here * factor[part, :]
                totals[lane] = term if totals[lane] is None else totals[lane] + term
                term = here * rows_b[lane]
                line = term if line is None else line + term
            across[part, :] = line
        into_a, into_b = sums.at[:, at_a], sums.at[:, at_b]
        for lane in range(lanes):
            where = slice(lane * LANES, (lane + 1) * LANES)
            into_b[:, where] += weight * totals[lane]
            turned = across[where, :].T
            folded = turned[:8, :]
            for begin in range(8, LANES, 8):
                folded = folded + turned[begin : begin + 8, :]
            into_a[:, where] += weight * folded

    def one_kept(slot, carry):
        add_diagonal(kept_ref.at[slot], slot)
        return carry

    def one_stored(slot, carry):
        if ready is not None:
            ready(slot)
        add_diagonal(stored_ref.at[slot], slot + kept)
        return carry

    lax.fori_loop(0, kept, one_kept, 0)
    lax.fori_loop(0, tiles - kept, one_stored, 0)
    for_each_pair(reach_tiles, class_ref, add_pair)
    for piece in range(tiles * lanes):
        out_ref[piece : piece + 1, :] = jnp.sum(sums[:, piece * LANES : (piece + 1) * LANES], axis=0, keepdims=True)


def first_kernel(reach_tiles, inverse_members, class_ref, kept_ref, hbm_ref, vectors_ref, stored_ref, out_ref, *scratch):
    vector, column, across, sums, arrived = scratch
    tiles = class_ref.shape[0]
    kept = kept_ref.shape[0]

    def in_copy(slot):
        return pltpu.make_async_copy(hbm_ref.at[slot], stored_ref.at[slot], arrived.at[slot])

    for slot in range(tiles - kept):
        in_copy(slot).start()
    for_each_pair(reach_tiles, class_ref, lambda slot, a, b: in_copy(slot + tiles - kept).start())
    vector[...] = vectors_ref[:, 0, :LANES]
    ready = lambda slot: in_copy(slot).wait()
    refs = (class_ref, kept_ref, stored_ref, vector, column, across, sums, out_ref)
    apply_share(reach_tiles, inverse_members, *refs, ready)


def total_of(x):
    return jnp.sum(jnp.sum(x, axis=0, keepdims=True), axis=1, keepdims=True)


def second_kernel(reach_tiles, inverse_members, peers, place_ref, class_ref, kept_ref, stored_ref, *refs):
    vectors_ref, parts, refs = refs[0], refs[1 : peers + 1], refs[peers + 1 :]
    sent, refs = refs[:peers], refs[peers:]
    state_ref, direction, residual, start, column, across, sums, product = refs
    innovations, obs_error = vectors_ref[:, 0, :LANES], vectors_ref[:, 0, LANES:]
    image = obs_error * innovations
    for part in parts:
        image = image + part[...]
    norm_now = total_of(innovations * innovations)
    alpha = norm_now / total_of(innovations * image)
    residual_now = innovations - alpha * image
    norm_next = total_of(residual_now * residual_now)
    direction_now = residual_now + (norm_next / norm_now) * innovations
    residual[...] = residual_now
    direction[...] = direction_now
    start[...] = alpha * innovations
    shared = (class_ref, kept_ref, stored_ref, direction, column, across, sums, product)
    apply_share(reach_tiles, inverse_members, *shared)
    curvature = total_of(direction_now * product[...])
    extra = obs_error * direction_now
    own_curvature = total_of(direction_now * extra)
    row_index, within, per_row = place_ref[0], place_ref[1], place_ref[2]
    for peer in range(peers):
        at = (row_index ^ peer) * per_row + within
        sent[peer][0:1, :] = product[pl.ds(at, 1), :]
        sent[peer][1:2, :] = jnp.broadcast_to(curvature, (1, LANES))
    own = row_index * per_row + within
    state_ref[0:1, :] = start[pl.ds(own, 1), :]
    state_ref[1:2, :] = residual[pl.ds(own, 1), :]
    state_ref[2:3, :] = direction[pl.ds(own, 1), :]
    product[...] = extra
    state_ref[3:4, :] = product[pl.ds(own, 1), :]
    state_ref[4:5, :] = jnp.broadcast_to(norm_next, (1, LANES))
    state_ref[5:6, :] = jnp.broadcast_to(own_curvature, (1, LANES))


def last_kernel(state_ref, *refs):
    parts, (solution_ref, residual_ref) = refs[:-2], refs[-2:]
    image, curvature = state_ref[3:4, :], state_ref[5:6, :]
    for part in parts:
        image = image + part[0:1, :]
        curvature = curvature + part[1:2, :]
    alpha = state_ref[4:5, :] / curvature
    solution_ref[...] = state_ref[0:1, :] + alpha * state_ref[2:3, :]
    residual_ref[...] = state_ref[1:2, :] - alpha * image


VMEM_SPEC = pl.BlockSpec(memory_space=pltpu.VMEM)
SMEM_SPEC = pl.BlockSpec(memory_space=pltpu.SMEM)
HBM_SPEC = pl.BlockSpec(memory_space=pltpu.HBM)


def in_hbm(x):
    return pltpu.with_memory_space_constraint(x, pltpu.HBM)


def swap_rows(x, mask):
    row_count = lax.axis_size("row")
    return lax.ppermute(x, "row", [(i, i ^ mask) for i in range(row_count)])


def vectors_only(anomalies, innovations, obs_error, track_pos, taper_class):
    row_count = lax.axis_size("row")
    col_count = lax.axis_size("col")
    sub_count = lax.axis_size("sub")
    row_index = lax.axis_index("row")
    within = lax.axis_index("col") * sub_count + lax.axis_index("sub")
    local_members, total_obs = anomalies.shape
    member_total = local_members * row_count * sub_count
    inverse_members = 1.0 / (member_total - 1)
    reach_tiles = max(2, row_count // 4)
    per_row = col_count * sub_count
    devices = row_count * per_row
    pieces = total_obs // LANES
    f32 = jnp.float32

    packed = pl.pallas_call(
        pack_kernel,
        out_shape=pltpu.VMEM((devices, 1, 2 * LANES), f32),
        in_specs=[HBM_SPEC, HBM_SPEC],
        out_specs=VMEM_SPEC,
        scratch_shapes=[pltpu.VMEM((1, 2 * LANES), f32), pltpu.SemaphoreType.DMA((2,))],
        compiler_params=pltpu.CompilerParams(vmem_limit_bytes=1024 * 1024),
        name="pack",
    )(in_hbm(innovations.reshape(1, LANES)), in_hbm(obs_error.reshape(1, LANES)))
    mate = lax.ppermute(anomalies, "sub", [(0, 1), (1, 0)])

    block_len = total_obs // row_count
    kept_count = min(row_count, KEPT_BYTES // (4 * block_len * block_len))
    stored_count = row_count - kept_count + off_diagonal(row_count)
    kept_shape, stored_shape = (kept_count, block_len, block_len), (stored_count, block_len, block_len)
    work = [pltpu.VMEM((total_obs, LANES), f32), pltpu.VMEM((block_len, LANES), f32), pltpu.VMEM((8, total_obs), f32)]
    kept, stored = pl.pallas_call(
        functools.partial(share_kernel, reach_tiles),
        out_shape=[pltpu.VMEM(kept_shape, f32), pltpu.HBM(stored_shape, f32)],
        in_specs=[HBM_SPEC] * 4,
        out_specs=[VMEM_SPEC, HBM_SPEC],
        scratch_shapes=[
            pltpu.SMEM(taper_class.shape, jnp.int32),
            pltpu.VMEM((1, total_obs), f32),
            pltpu.VMEM((2 * local_members, total_obs), anomalies.dtype),
            pltpu.VMEM((total_obs, 2 * local_members), anomalies.dtype),
            pltpu.VMEM((total_obs, LANES), f32),
            pltpu.VMEM(stored_shape, f32),
            pltpu.SemaphoreType.DMA((4,)),
            pltpu.SemaphoreType.DMA((stored_count,)),
        ],
        compiler_params=pltpu.CompilerParams(vmem_limit_bytes=24 * 1024 * 1024),
        cost_estimate=pl.CostEstimate(
            flops=4 * local_members * total_obs * total_obs,
            bytes_accessed=4 * total_obs * total_obs,
            transcendentals=total_obs * total_obs,
        ),
        name="share",
    )(in_hbm(taper_class), in_hbm(track_pos.reshape(1, total_obs)), in_hbm(anomalies), in_hbm(mate))
    vectors = lax.all_to_all(packed, ("row", "col", "sub"), split_axis=0, concat_axis=0, tiled=True)

    params = pltpu.CompilerParams(vmem_limit_bytes=8 * 1024 * 1024)
    stored, part = pl.pallas_call(
        functools.partial(first_kernel, reach_tiles, inverse_members),
        out_shape=[pltpu.VMEM(stored_shape, f32), pltpu.VMEM((pieces, LANES), f32)],
        in_specs=[SMEM_SPEC, VMEM_SPEC, HBM_SPEC, VMEM_SPEC],
        out_specs=[VMEM_SPEC, VMEM_SPEC],
        scratch_shapes=[pltpu.VMEM((pieces, LANES), f32)] + work + [pltpu.SemaphoreType.DMA((stored_count,))],
        compiler_params=params,
        name="first",
    )(taper_class, kept, in_hbm(stored), vectors)
    parts = [part] + [swap_rows(part, mask) for mask in reversed(range(1, row_count))]

    place = jnp.stack([row_index, within, jnp.int32(per_row)]).astype(jnp.int32)
    *sent, state = pl.pallas_call(
        functools.partial(second_kernel, reach_tiles, inverse_members, row_count),
        out_shape=[pltpu.VMEM((8, LANES), f32) for _ in range(row_count + 1)],
        in_specs=[SMEM_SPEC, SMEM_SPEC] + [VMEM_SPEC] * (row_count + 3),
        out_specs=[VMEM_SPEC] * (row_count + 1),
        scratch_shapes=[pltpu.VMEM((pieces, LANES), f32)] * 3 + work + [pltpu.VMEM((pieces, LANES), f32)],
        compiler_params=params,
        name="second",
    )(place, taper_class, kept, stored, vectors, *parts)
    got = [sent[0]] + [swap_rows(sent[mask], mask) for mask in reversed(range(1, row_count))]
    solution_part, residual_part = pl.pallas_call(
        last_kernel,
        out_shape=[jax.ShapeDtypeStruct((1, LANES), f32)] * 2,
        in_specs=[VMEM_SPEC] * (row_count + 1),
        out_specs=[VMEM_SPEC] * 2,
        compiler_params=pltpu.CompilerParams(vmem_limit_bytes=1024 * 1024),
        name="last",
    )(state, *got)
    return solution_part.reshape(LANES), residual_part.reshape(LANES)


def fits(anomalies, innovations, obs_error, track_pos, taper_class):
    row_count = lax.axis_size("row")
    local_members, total_obs = anomalies.shape
    share_bytes = 4 * total_obs * total_obs
    return (
        ITERS == 2
        and row_count in (2, 4)
        and lax.axis_size("sub") == 2
        and innovations.shape[0] == LANES
        and total_obs % (row_count * LANES) == 0
        and local_members % LANES == 0
        and share_bytes <= 16 * 1024 * 1024
    )


def per_device(*args):
    return vectors_only(*args) if fits(*args) else blocks(*args)


def squares(residual):
    return lax.psum(jnp.sum(residual * residual), ("row", "col", "sub"))


def blocks(anomalies, innovations, obs_error, track_pos, taper_class):
    row_count = lax.axis_size("row")
    col_count = lax.axis_size("col")
    sub_count = lax.axis_size("sub")
    row_index = lax.axis_index("row")
    col_index = lax.axis_index("col")
    local_members, total_obs = anomalies.shape
    block_len = total_obs // row_count
    quarter_len = block_len // col_count
    member_total = local_members * row_count * sub_count
    inverse_members = 1.0 / (member_total - 1)
    reach_tiles = max(2, row_count // 4)
    class_row = lax.dynamic_index_in_dim(taper_class, row_index, 0, keepdims=False)
    tile_weight = jnp.maximum(0.0, 1.0 - class_row.astype(jnp.float32) / reach_tiles)
    row_pos = lax.dynamic_slice_in_dim(track_pos, row_index * block_len, block_len, 0)
    col_pos = lax.dynamic_index_in_dim(
        track_pos.reshape(row_count, col_count, quarter_len), col_index, 1, keepdims=False
    )
    own_block = lax.all_to_all(anomalies, "row", split_axis=1, concat_axis=0, tiled=True)
    own_quarter = lax.dynamic_slice_in_dim(own_block, col_index * quarter_len, quarter_len, 1)

    def one_tile(piece, block_index, keep_factor):
        product = jnp.einsum("mi,mq->iq", own_block, piece, preferred_element_type=jnp.float32)
        column_pos = lax.dynamic_index_in_dim(col_pos, block_index, 0, keepdims=False)
        weight_here = lax.dynamic_index_in_dim(tile_weight, block_index, 0, keepdims=False)
        distance = row_pos[:, None] - column_pos[None, :]
        taper = weight_here * keep_factor * jnp.exp(-(distance * distance) / track_width)
        return product * (taper * inverse_members)

    def one_entry(entry):
        return one_tile(entry[0], entry[1], 1.0)

    piece = lax.all_gather(own_quarter[None], "row", axis=0, tiled=True)
    indices = jnp.arange(piece.shape[0], dtype=jnp.int32)
    tiles = lax.map(one_entry, (piece, indices))
    solution = jnp.zeros_like(innovations)
    residual = innovations
    direction_vec = innovations
    norm_now = squares(residual)
    for turn_index in range(ITERS):
        column_vec = lax.all_gather(direction_vec, ("row", "sub"), axis=0, tiled=True).reshape(
            row_count, quarter_len
        )
        direct = jnp.einsum("jiq,jq->i", tiles, column_vec, precision=lax.Precision.HIGHEST)
        extra = obs_error * direction_vec
        own_part = lax.psum_scatter(direct, ("col", "sub"), scatter_dimension=0, tiled=True)
        image = own_part + extra
        alpha = norm_now / lax.psum(jnp.sum(direction_vec * image), ("row", "col", "sub"))
        solution = solution + alpha * direction_vec
        residual = residual - alpha * image
        if turn_index + 1 < ITERS:
            norm_next = squares(residual)
            direction_vec = residual + norm_next / norm_now * direction_vec
            norm_now = norm_next
    return (solution, residual)


def solution(mesh):
    in_specs = (
        P(("group", "row", "sub"), None),
        P(("group", "row", "col", "sub")),
        P(("group", "row", "col", "sub")),
        P("group"),
        P("group", None),
    )
    out_specs = (P(("group", "row", "col", "sub")), P(("group", "row", "col", "sub")))
    return jax.shard_map(
        per_device, mesh=mesh, in_specs=in_specs, out_specs=out_specs, check_vma=False
    )
```

```python
import functools
import math

import jax
import jax.numpy as jnp
from jax import lax
from jax.experimental import pallas as pl
from jax.experimental.pallas import tpu as pltpu
from jax.sharding import PartitionSpec as P

ITERS = 2
LANES = 128
KEPT_BYTES = 3 * 1024 * 1024


track_width = 0.0001
exp2_rate = -math.log2(math.e) / track_width


def off_diagonal(tiles):
    return tiles * (tiles - 1) // 2


def first_slot(a, tiles):
    return a * tiles - (a * (a + 1)) // 2


def for_each_pair(reach_tiles, class_ref, action):
    tiles = class_ref.shape[0]

    def one_pair(slot, carry):
        a = jnp.int32(0)
        for row in range(1, tiles - 1):
            a = a + (slot >= first_slot(row, tiles)).astype(jnp.int32)
        b = slot - first_slot(a, tiles) + a + 1
        pl.when(class_ref[a, b] < reach_tiles)(lambda: action(slot, a, b))
        return carry

    lax.fori_loop(0, off_diagonal(tiles), one_pair, 0)


def each_pair(reach_tiles, class_ref, action):
    tiles = class_ref.shape[0]
    for a in range(tiles):
        for b in range(a + 1, tiles):
            slot = first_slot(a, tiles) + b - a - 1
            pl.when(class_ref[a, b] < reach_tiles)(functools.partial(action, slot))


def block_at(a, block_len):
    return pl.ds(pl.multiple_of(a * block_len, LANES), block_len)


def pack_kernel(row_ref, packed_ref):
    packed_ref[...] = jnp.broadcast_to(row_ref[...], packed_ref.shape)


def share_kernel(reach_tiles, class_hbm, pos_hbm, own_ref, mate_ref, kept_ref, stored_ref, *scratch):
    class_ref, pos_ref, both, turned, column, made, arrived, left = scratch
    members, total_obs = own_ref.shape
    tiles = class_ref.shape[0]
    block_len = total_obs // tiles
    kept = kept_ref.shape[0]
    pos_copy = pltpu.make_async_copy(pos_hbm, pos_ref, arrived.at[0])
    own_copy = pltpu.make_async_copy(own_ref, both.at[pl.ds(0, members), :], arrived.at[1])
    class_copy = pltpu.make_async_copy(class_hbm, class_ref, arrived.at[2])
    mate_copy = pltpu.make_async_copy(mate_ref, both.at[pl.ds(members, members), :], arrived.at[3])
    for copy in (pos_copy, own_copy, mate_copy, class_copy):
        copy.start()
    pos_copy.wait()
    spread_columns(pos_ref[...], column)
    own_copy.wait()
    turned[:, :members] = both[:members, :].T
    mate_copy.wait()
    turned[:, members:] = both[members:, :].T
    class_copy.wait()
    rows = 128

    def out_copy(slot):
        return pltpu.make_async_copy(made.at[slot], stored_ref.at[slot], left.at[slot])

    def make_tile(tile, a, b):
        rows_at, columns_at = block_at(a, block_len), block_at(b, block_len)
        right = both[:, columns_at]
        right_pos = pos_ref[:, columns_at]
        left_turned, left_column = turned.at[rows_at, :], column.at[rows_at, :]
        for begin in range(0, block_len, rows):
            part = slice(begin, begin + rows)
            product = jnp.dot(left_turned[part, :], right, preferred_element_type=jnp.float32)
            left_pos = jnp.concatenate([left_column[part, :]] * (block_len // LANES), axis=1)
            distance = left_pos - right_pos
            tile[part, :] = product * jnp.exp2(distance * distance * exp2_rate)

    def make_pair(slot, a, b):
        slot = slot + tiles - kept
        make_tile(made.at[slot], a, b)
        out_copy(slot).start()

    def make_stored(slot, carry):
        make_tile(made.at[slot], slot + kept, slot + kept)
        out_copy(slot).start()
        return carry

    def make_kept(slot, carry):
        make_tile(kept_ref.at[slot], slot, slot)
        return carry

    for_each_pair(reach_tiles, class_ref, make_pair)
    lax.fori_loop(0, tiles - kept, make_stored, 0)
    lax.fori_loop(0, kept, make_kept, 0)
    each_pair(reach_tiles, class_ref, lambda slot: out_copy(slot + tiles - kept).wait())
    for slot in range(tiles - kept):
        out_copy(slot).wait()


def spread_columns(row, column):
    for begin in range(0, column.shape[0], LANES):
        square = jnp.broadcast_to(row[:, begin : begin + LANES], (LANES, LANES))
        column[begin : begin + LANES, :] = square.T


def spread_vector(vector, column):
    for piece in range(vector.shape[0]):
        square = jnp.broadcast_to(vector[piece : piece + 1, :], (LANES, LANES))
        column[piece * LANES : (piece + 1) * LANES, :] = square.T


def apply_share(
    reach_tiles, inverse_members, class_ref, kept_ref, stored_ref, vector, column, across, sums, out_ref, ready=None
):
    tiles = class_ref.shape[0]
    kept = kept_ref.shape[0]
    block_len = kept_ref.shape[1]
    lanes = block_len // LANES
    sums[...] = jnp.zeros_like(sums)

    def add_diagonal(tile, a):
        at = block_at(a, block_len)
        factor = column.at[at, :]
        totals = [None] * lanes
        for begin in range(0, block_len, 8):
            part = slice(begin, begin + 8)
            for lane in range(lanes):
                term = tile[part, lane * LANES : (lane + 1) * LANES] * factor[part, :]
                totals[lane] = term if totals[lane] is None else totals[lane] + term
        into = sums.at[:, at]
        for lane in range(lanes):
            into[:, lane * LANES : (lane + 1) * LANES] += tile_weight(class_ref[a, a]) * totals[lane]

    def tile_weight(klass):
        return jnp.maximum(0.0, 1.0 - klass.astype(jnp.float32) / reach_tiles) * inverse_members

    def add_pair(slot, a, b):
        slot = slot + tiles - kept
        if ready is not None:
            ready(slot)
        weight = tile_weight(class_ref[a, b])
        at_a, at_b = block_at(a, block_len), block_at(b, block_len)
        tile, factor = stored_ref.at[slot], column.at[at_a, :]
        rows_b = [jnp.broadcast_to(vector[pl.ds(b * lanes + lane, 1), :], (8, LANES)) for lane in range(lanes)]
        totals = [None] * lanes
        for begin in range(0, block_len, 8):
            part = slice(begin, begin + 8)
            line = None
            for lane in range(lanes):
                here = tile[part, lane * LANES : (lane + 1) * LANES]
                term = here * factor[part, :]
                totals[lane] = term if totals[lane] is None else totals[lane] + term
                term = here * rows_b[lane]
                line = term if line is None else line + term
            across[part, :] = line
        into_a, into_b = sums.at[:, at_a], sums.at[:, at_b]
        for lane in range(lanes):
            where = slice(lane * LANES, (lane + 1) * LANES)
            into_b[:, where] += weight * totals[lane]
            turned = across[where, :].T
            folded = turned[:8, :]
            for begin in range(8, LANES, 8):
                folded = folded + turned[begin : begin + 8, :]
            into_a[:, where] += weight * folded

    def one_kept(slot, carry):
        add_diagonal(kept_ref.at[slot], slot)
        return carry

    def one_stored(slot, carry):
        if ready is not None:
            ready(slot)
        add_diagonal(stored_ref.at[slot], slot + kept)
        return carry

    lax.fori_loop(0, kept, one_kept, 0)
    lax.fori_loop(0, tiles - kept, one_stored, 0)
    for_each_pair(reach_tiles, class_ref, add_pair)
    for piece in range(tiles * lanes):
        out_ref[piece : piece + 1, :] = jnp.sum(sums[:, piece * LANES : (piece + 1) * LANES], axis=0, keepdims=True)


def first_kernel(reach_tiles, inverse_members, class_vmem, kept_ref, hbm_ref, vectors_ref, stored_ref, out_ref, *scratch):
    class_ref, vector, column, across, sums, arrived, class_arrived = scratch
    tiles = class_ref.shape[0]
    kept = kept_ref.shape[0]
    class_copy = pltpu.make_async_copy(class_vmem, class_ref, class_arrived)
    class_copy.start()

    def in_copy(slot):
        return pltpu.make_async_copy(hbm_ref.at[slot], stored_ref.at[slot], arrived.at[slot])

    for slot in range(tiles - kept):
        in_copy(slot).start()
    vector[...] = vectors_ref[:, 0, :LANES]
    spread_vector(vector, column)
    class_copy.wait()
    each_pair(reach_tiles, class_ref, lambda slot: in_copy(slot + tiles - kept).start())
    ready = lambda slot: in_copy(slot).wait()
    refs = (class_ref, kept_ref, stored_ref, vector, column, across, sums, out_ref)
    apply_share(reach_tiles, inverse_members, *refs, ready)


def total_of(x):
    return jnp.sum(jnp.sum(x, axis=0, keepdims=True), axis=1, keepdims=True)


def second_kernel(reach_tiles, inverse_members, peers, class_vmem, kept_ref, stored_ref, *refs):
    vectors_ref, parts, refs = refs[0], refs[1 : peers + 1], refs[peers + 1 :]
    sent, refs = refs[:peers], refs[peers:]
    state_ref, class_ref, direction, residual, start, column, across, sums, product, class_arrived = refs
    class_copy = pltpu.make_async_copy(class_vmem, class_ref, class_arrived)
    class_copy.start()
    innovations, obs_error = vectors_ref[:, 0, :LANES], vectors_ref[:, 0, LANES:]
    image = obs_error * innovations
    for part in parts:
        image = image + part[...]
    norm_now = total_of(innovations * innovations)
    alpha = norm_now / total_of(innovations * image)
    residual_now = innovations - alpha * image
    norm_next = total_of(residual_now * residual_now)
    direction_now = residual_now + (norm_next / norm_now) * innovations
    residual[...] = residual_now
    direction[...] = direction_now
    start[...] = alpha * innovations
    spread_vector(direction, column)
    class_copy.wait()
    shared = (class_ref, kept_ref, stored_ref, direction, column, across, sums, product)
    apply_share(reach_tiles, inverse_members, *shared)
    curvature = total_of(direction_now * product[...])
    extra = obs_error * direction_now
    own_curvature = total_of(direction_now * extra)
    row_index = lax.axis_index("row")
    within = lax.axis_index("col") * lax.axis_size("sub") + lax.axis_index("sub")
    per_row = lax.axis_size("col") * lax.axis_size("sub")
    for peer in range(peers):
        at = (row_index ^ peer) * per_row + within
        sent[peer][0:1, :] = product[pl.ds(at, 1), :]
        sent[peer][1:2, :] = jnp.broadcast_to(curvature, (1, LANES))
    own = row_index * per_row + within
    state_ref[0:1, :] = start[pl.ds(own, 1), :]
    state_ref[1:2, :] = residual[pl.ds(own, 1), :]
    state_ref[2:3, :] = direction[pl.ds(own, 1), :]
    product[...] = extra
    state_ref[3:4, :] = product[pl.ds(own, 1), :]
    state_ref[4:5, :] = jnp.broadcast_to(norm_next, (1, LANES))
    state_ref[5:6, :] = jnp.broadcast_to(own_curvature, (1, LANES))


def last_kernel(state_ref, *refs):
    parts, (solution_ref, residual_ref) = refs[:-2], refs[-2:]
    image, curvature = state_ref[3:4, :], state_ref[5:6, :]
    for part in parts:
        image = image + part[0:1, :]
        curvature = curvature + part[1:2, :]
    alpha = state_ref[4:5, :] / curvature
    solution_ref[...] = state_ref[0:1, :] + alpha * state_ref[2:3, :]
    residual_ref[...] = state_ref[1:2, :] - alpha * image


VMEM_SPEC = pl.BlockSpec(memory_space=pltpu.VMEM)
SMEM_SPEC = pl.BlockSpec(memory_space=pltpu.SMEM)
HBM_SPEC = pl.BlockSpec(memory_space=pltpu.HBM)


def in_hbm(x):
    return pltpu.with_memory_space_constraint(x, pltpu.HBM)


def swap_rows(x, mask):
    row_count = lax.axis_size("row")
    return lax.ppermute(x, "row", [(i, i ^ mask) for i in range(row_count)])


def vectors_only(anomalies, innovations, obs_error, track_pos, taper_class):
    row_count = lax.axis_size("row")
    col_count = lax.axis_size("col")
    sub_count = lax.axis_size("sub")
    local_members, total_obs = anomalies.shape
    member_total = local_members * row_count * sub_count
    inverse_members = 1.0 / (member_total - 1)
    reach_tiles = max(2, row_count // 4)
    per_row = col_count * sub_count
    devices = row_count * per_row
    pieces = total_obs // LANES
    f32 = jnp.float32

    packed = pl.pallas_call(
        pack_kernel,
        out_shape=pltpu.VMEM((devices, 1, 2 * LANES), f32),
        in_specs=[VMEM_SPEC],
        out_specs=VMEM_SPEC,
        compiler_params=pltpu.CompilerParams(vmem_limit_bytes=1024 * 1024),
        name="pack",
    )(jnp.concatenate([innovations, obs_error]).reshape(1, 2 * LANES))
    mate = lax.ppermute(anomalies, "sub", [(0, 1), (1, 0)])

    block_len = total_obs // row_count
    kept_count = min(row_count, KEPT_BYTES // (4 * block_len * block_len))
    stored_count = row_count - kept_count + off_diagonal(row_count)
    kept_shape, stored_shape = (kept_count, block_len, block_len), (stored_count, block_len, block_len)
    class_here = pltpu.SMEM(taper_class.shape, jnp.int32)
    work = [pltpu.VMEM((total_obs, LANES), f32), pltpu.VMEM((block_len, LANES), f32), pltpu.VMEM((8, total_obs), f32)]
    kept, stored = pl.pallas_call(
        functools.partial(share_kernel, reach_tiles),
        out_shape=[pltpu.VMEM(kept_shape, f32), pltpu.HBM(stored_shape, f32)],
        in_specs=[HBM_SPEC] * 4,
        out_specs=[VMEM_SPEC, HBM_SPEC],
        scratch_shapes=[
            class_here,
            pltpu.VMEM((1, total_obs), f32),
            pltpu.VMEM((2 * local_members, total_obs), anomalies.dtype),
            pltpu.VMEM((total_obs, 2 * local_members), anomalies.dtype),
            pltpu.VMEM((total_obs, LANES), f32),
            pltpu.VMEM(stored_shape, f32),
            pltpu.SemaphoreType.DMA((4,)),
            pltpu.SemaphoreType.DMA((stored_count,)),
        ],
        compiler_params=pltpu.CompilerParams(vmem_limit_bytes=24 * 1024 * 1024),
        cost_estimate=pl.CostEstimate(
            flops=4 * local_members * total_obs * total_obs,
            bytes_accessed=4 * total_obs * total_obs,
            transcendentals=total_obs * total_obs,
        ),
        name="share",
    )(in_hbm(taper_class), in_hbm(track_pos.reshape(1, total_obs)), in_hbm(anomalies), in_hbm(mate))
    vectors = lax.all_to_all(packed, ("row", "col", "sub"), split_axis=0, concat_axis=0, tiled=True)

    params = pltpu.CompilerParams(vmem_limit_bytes=8 * 1024 * 1024)
    stored, part = pl.pallas_call(
        functools.partial(first_kernel, reach_tiles, inverse_members),
        out_shape=[pltpu.VMEM(stored_shape, f32), pltpu.VMEM((pieces, LANES), f32)],
        in_specs=[VMEM_SPEC, VMEM_SPEC, HBM_SPEC, VMEM_SPEC],
        out_specs=[VMEM_SPEC, VMEM_SPEC],
        scratch_shapes=[class_here, pltpu.VMEM((pieces, LANES), f32)]
        + work
        + [pltpu.SemaphoreType.DMA((stored_count,)), pltpu.SemaphoreType.DMA(())],
        compiler_params=params,
        name="first",
    )(taper_class, kept, in_hbm(stored), vectors)
    parts = [part] + [swap_rows(part, mask) for mask in range(1, row_count)]

    *sent, state = pl.pallas_call(
        functools.partial(second_kernel, reach_tiles, inverse_members, row_count),
        out_shape=[pltpu.VMEM((8, LANES), f32) for _ in range(row_count + 1)],
        in_specs=[VMEM_SPEC] * (row_count + 4),
        out_specs=[VMEM_SPEC] * (row_count + 1),
        scratch_shapes=[class_here]
        + [pltpu.VMEM((pieces, LANES), f32)] * 3
        + work
        + [pltpu.VMEM((pieces, LANES), f32), pltpu.SemaphoreType.DMA(())],
        compiler_params=params,
        name="second",
    )(taper_class, kept, stored, vectors, *parts)
    got = [sent[0]] + [swap_rows(sent[mask], mask) for mask in reversed(range(1, row_count))]
    solution_part, residual_part = pl.pallas_call(
        last_kernel,
        out_shape=[jax.ShapeDtypeStruct((1, LANES), f32)] * 2,
        in_specs=[VMEM_SPEC] * (row_count + 1),
        out_specs=[VMEM_SPEC] * 2,
        compiler_params=pltpu.CompilerParams(vmem_limit_bytes=1024 * 1024),
        name="last",
    )(state, *got)
    return solution_part.reshape(LANES), residual_part.reshape(LANES)


def fits(anomalies, innovations, obs_error, track_pos, taper_class):
    row_count = lax.axis_size("row")
    local_members, total_obs = anomalies.shape
    share_bytes = 4 * total_obs * total_obs
    return (
        ITERS == 2
        and row_count in (2, 4)
        and lax.axis_size("sub") == 2
        and innovations.shape[0] == LANES
        and total_obs % (row_count * LANES) == 0
        and local_members % LANES == 0
        and share_bytes <= 16 * 1024 * 1024
    )


def per_device(*args):
    return vectors_only(*args) if fits(*args) else blocks(*args)


def squares(residual):
    return lax.psum(jnp.sum(residual * residual), ("row", "col", "sub"))


def blocks(anomalies, innovations, obs_error, track_pos, taper_class):
    row_count = lax.axis_size("row")
    col_count = lax.axis_size("col")
    sub_count = lax.axis_size("sub")
    row_index = lax.axis_index("row")
    col_index = lax.axis_index("col")
    local_members, total_obs = anomalies.shape
    block_len = total_obs // row_count
    quarter_len = block_len // col_count
    member_total = local_members * row_count * sub_count
    inverse_members = 1.0 / (member_total - 1)
    reach_tiles = max(2, row_count // 4)
    class_row = lax.dynamic_index_in_dim(taper_class, row_index, 0, keepdims=False)
    tile_weight = jnp.maximum(0.0, 1.0 - class_row.astype(jnp.float32) / reach_tiles)
    row_pos = lax.dynamic_slice_in_dim(track_pos, row_index * block_len, block_len, 0)
    col_pos = lax.dynamic_index_in_dim(
        track_pos.reshape(row_count, col_count, quarter_len), col_index, 1, keepdims=False
    )
    own_block = lax.all_to_all(anomalies, "row", split_axis=1, concat_axis=0, tiled=True)
    own_quarter = lax.dynamic_slice_in_dim(own_block, col_index * quarter_len, quarter_len, 1)

    def one_tile(piece, block_index, keep_factor):
        product = jnp.einsum("mi,mq->iq", own_block, piece, preferred_element_type=jnp.float32)
        column_pos = lax.dynamic_index_in_dim(col_pos, block_index, 0, keepdims=False)
        weight_here = lax.dynamic_index_in_dim(tile_weight, block_index, 0, keepdims=False)
        distance = row_pos[:, None] - column_pos[None, :]
        taper = weight_here * keep_factor * jnp.exp(-(distance * distance) / track_width)
        return product * (taper * inverse_members)

    def one_entry(entry):
        return one_tile(entry[0], entry[1], 1.0)

    piece = lax.all_gather(own_quarter[None], "row", axis=0, tiled=True)
    indices = jnp.arange(piece.shape[0], dtype=jnp.int32)
    tiles = lax.map(one_entry, (piece, indices))
    solution = jnp.zeros_like(innovations)
    residual = innovations
    direction_vec = innovations
    norm_now = squares(residual)
    for turn_index in range(ITERS):
        column_vec = lax.all_gather(direction_vec, ("row", "sub"), axis=0, tiled=True).reshape(
            row_count, quarter_len
        )
        direct = jnp.einsum("jiq,jq->i", tiles, column_vec, precision=lax.Precision.HIGHEST)
        extra = obs_error * direction_vec
        own_part = lax.psum_scatter(direct, ("col", "sub"), scatter_dimension=0, tiled=True)
        image = own_part + extra
        alpha = norm_now / lax.psum(jnp.sum(direction_vec * image), ("row", "col", "sub"))
        solution = solution + alpha * direction_vec
        residual = residual - alpha * image
        if turn_index + 1 < ITERS:
            norm_next = squares(residual)
            direction_vec = residual + norm_next / norm_now * direction_vec
            norm_now = norm_next
    return (solution, residual)


def solution(mesh):
    in_specs = (
        P(("group", "row", "sub"), None),
        P(("group", "row", "col", "sub")),
        P(("group", "row", "col", "sub")),
        P("group"),
        P("group", None),
    )
    out_specs = (P(("group", "row", "col", "sub")), P(("group", "row", "col", "sub")))
    return jax.shard_map(
        per_device, mesh=mesh, in_specs=in_specs, out_specs=out_specs, check_vma=False
    )
```

```python
import functools
import math

import jax
import jax.numpy as jnp
from jax import lax
from jax.experimental import pallas as pl
from jax.experimental.pallas import tpu as pltpu
from jax.sharding import PartitionSpec as P

ITERS = 2
LANES = 128


track_width = 0.0001
exp2_rate = -math.log2(math.e) / track_width


def off_diagonal(tiles):
    return tiles * (tiles - 1) // 2


def first_slot(a, tiles):
    return a * tiles - (a * (a + 1)) // 2


def for_each_pair(reach_tiles, class_ref, action):
    tiles = class_ref.shape[0]

    def one_pair(slot, carry):
        a = jnp.int32(0)
        for row in range(1, tiles - 1):
            a = a + (slot >= first_slot(row, tiles)).astype(jnp.int32)
        b = slot - first_slot(a, tiles) + a + 1
        pl.when(class_ref[a, b] < reach_tiles)(lambda: action(slot, a, b))
        return carry

    lax.fori_loop(0, off_diagonal(tiles), one_pair, 0)


def block_at(a, block_len):
    return pl.ds(pl.multiple_of(a * block_len, LANES), block_len)


def share_kernel(reach_tiles, class_hbm, pos_hbm, own_ref, mate_ref, share_ref, *scratch):
    class_ref, pos_ref, both, turned, column, arrived = scratch
    members, total_obs = own_ref.shape
    tiles = class_ref.shape[0]
    block_len = total_obs // tiles
    pos_copy = pltpu.make_async_copy(pos_hbm, pos_ref, arrived.at[0])
    own_copy = pltpu.make_async_copy(own_ref, both.at[pl.ds(0, members), :], arrived.at[1])
    class_copy = pltpu.make_async_copy(class_hbm, class_ref, arrived.at[2])
    for copy in (pos_copy, own_copy, class_copy):
        copy.start()
    both[members:, :] = mate_ref[...]
    turned[:, members:] = mate_ref[...].T
    pos_copy.wait()
    spread_columns(pos_ref[...], column)
    own_copy.wait()
    turned[:, :members] = both[:members, :].T
    class_copy.wait()
    rows = 128

    def make_tile(slot, a, b):
        rows_at, columns_at = block_at(a, block_len), block_at(b, block_len)
        right = both[:, columns_at]
        right_pos = pos_ref[:, columns_at]
        left_turned, left_column, tile = turned.at[rows_at, :], column.at[rows_at, :], share_ref.at[slot]
        for begin in range(0, block_len, rows):
            part = slice(begin, begin + rows)
            product = jnp.dot(left_turned[part, :], right, preferred_element_type=jnp.float32)
            left_pos = jnp.concatenate([left_column[part, :]] * (block_len // LANES), axis=1)
            distance = left_pos - right_pos
            tile[part, :] = product * jnp.exp2(distance * distance * exp2_rate)

    def make_diagonal(slot, carry):
        make_tile(slot, slot, slot)
        return carry

    lax.fori_loop(0, tiles, make_diagonal, 0)
    for_each_pair(reach_tiles, class_ref, lambda slot, a, b: make_tile(slot + tiles, a, b))


def spread_columns(row, column):
    for begin in range(0, column.shape[0], LANES):
        square = jnp.broadcast_to(row[:, begin : begin + LANES], (LANES, LANES))
        column[begin : begin + LANES, :] = square.T


def spread_vector(vector, column):
    for piece in range(vector.shape[0]):
        square = jnp.broadcast_to(vector[piece : piece + 1, :], (LANES, LANES))
        column[piece * LANES : (piece + 1) * LANES, :] = square.T


def tile_weight(klass, reach_tiles, inverse_members):
    return jnp.maximum(0.0, 1.0 - klass.astype(jnp.float32) / reach_tiles) * inverse_members


def add_sums(into, weight, totals):
    for lane, total in enumerate(totals):
        into[:, lane * LANES : (lane + 1) * LANES] += weight * total


def add_turned(into, weight, across):
    for lane in range(across.shape[0] // LANES):
        where = slice(lane * LANES, (lane + 1) * LANES)
        turned = across[where, :].T
        folded = turned[:8, :]
        for begin in range(8, LANES, 8):
            folded = folded + turned[begin : begin + 8, :]
        into[:, where] += weight * folded


def fold_sums(sums, out_ref):
    for piece in range(sums.shape[1] // LANES):
        out_ref[piece : piece + 1, :] = jnp.sum(sums[:, piece * LANES : (piece + 1) * LANES], axis=0, keepdims=True)


def apply_share(reach_tiles, inverse_members, class_ref, share_ref, vector, column, across, sums, out_ref):
    tiles = class_ref.shape[0]
    block_len = share_ref.shape[1]
    lanes = block_len // LANES
    sums[...] = jnp.zeros_like(sums)

    def add_diagonal(a, carry):
        at = block_at(a, block_len)
        tile, factor = share_ref.at[a], column.at[at, :]
        totals = [None] * lanes
        for begin in range(0, block_len, 8):
            part = slice(begin, begin + 8)
            for lane in range(lanes):
                term = tile[part, lane * LANES : (lane + 1) * LANES] * factor[part, :]
                totals[lane] = term if totals[lane] is None else totals[lane] + term
        add_sums(sums.at[:, at], tile_weight(class_ref[a, a], reach_tiles, inverse_members), totals)
        return carry

    def add_pair(slot, a, b):
        weight = tile_weight(class_ref[a, b], reach_tiles, inverse_members)
        at_a, at_b = block_at(a, block_len), block_at(b, block_len)
        tile, factor = share_ref.at[slot + tiles], column.at[at_a, :]
        rows_b = [jnp.broadcast_to(vector[pl.ds(b * lanes + lane, 1), :], (8, LANES)) for lane in range(lanes)]
        totals = [None] * lanes
        for begin in range(0, block_len, 8):
            part = slice(begin, begin + 8)
            line = None
            for lane in range(lanes):
                here = tile[part, lane * LANES : (lane + 1) * LANES]
                term = here * factor[part, :]
                totals[lane] = term if totals[lane] is None else totals[lane] + term
                term = here * rows_b[lane]
                line = term if line is None else line + term
            across[part, :] = line
        add_sums(sums.at[:, at_b], weight, totals)
        add_turned(sums.at[:, at_a], weight, across)

    lax.fori_loop(0, tiles, add_diagonal, 0)
    for_each_pair(reach_tiles, class_ref, add_pair)
    fold_sums(sums, out_ref)


def place():
    sub_count = lax.axis_size("sub")
    within = lax.axis_index("col") * sub_count + lax.axis_index("sub")
    return lax.axis_index("row"), within, lax.axis_size("col") * sub_count


def first_kernel(reach_tiles, inverse_members, masks, class_vmem, share_ref, error_ref, *refs):
    tiles = class_vmem.shape[0]
    chunks, refs = refs[:tiles], refs[tiles:]
    out_ref, class_ref, vector, column, across, sums, class_arrived = refs
    class_copy = pltpu.make_async_copy(class_vmem, class_ref, class_arrived)
    class_copy.start()
    row_index, within, per_row = place()
    block_len = share_ref.shape[1]
    lanes = block_len // LANES
    pieces = tiles * lanes
    for mask, chunk in zip(masks, chunks):
        vector[pl.ds(row_index ^ mask, 1), :] = chunk[...]
    spread_vector(vector, column)
    sums[...] = jnp.zeros_like(sums)
    chunk_at = pl.ds(pl.multiple_of(within * LANES, LANES), LANES)
    class_copy.wait()

    def sums_of_rows(tile, a):
        strip, factor = tile.at[chunk_at, :], column.at[pl.ds(pl.multiple_of(a * LANES, LANES), LANES), :]
        totals = [None] * lanes
        for begin in range(0, LANES, 8):
            part = slice(begin, begin + 8)
            for lane in range(lanes):
                term = strip[part, lane * LANES : (lane + 1) * LANES] * factor[part, :]
                totals[lane] = term if totals[lane] is None else totals[lane] + term
        return totals

    def add_diagonal(a, carry):
        weight = tile_weight(class_ref[a, a], reach_tiles, inverse_members)
        add_sums(sums.at[:, block_at(a, block_len)], weight, sums_of_rows(share_ref.at[a], a))
        return carry

    def add_pair(slot, a, b):
        weight = tile_weight(class_ref[a, b], reach_tiles, inverse_members)
        tile = share_ref.at[slot + tiles]
        add_sums(sums.at[:, block_at(b, block_len)], weight, sums_of_rows(tile, a))
        across[...] = tile[:, chunk_at] * vector[pl.ds(b, 1), :]
        add_turned(sums.at[:, block_at(a, block_len)], weight, across)

    lax.fori_loop(0, tiles, add_diagonal, 0)
    for_each_pair(reach_tiles, class_ref, add_pair)
    fold_sums(sums, out_ref)
    own = row_index * per_row + within
    out_ref[pl.ds(own, 1), :] += error_ref[...] * chunks[0][...]
    out_ref[pieces : pieces + tiles, :] = vector[...]
    out_ref[pieces + tiles : pieces + tiles + 1, :] = error_ref[...]


def middle_kernel(pieces, *refs):
    parts, out_ref = refs[:-1], refs[-1]
    total = parts[0][:pieces, :]
    for part in parts[1:]:
        total = total + part[:pieces, :]
    out_ref[...] = total


def gather_kernel(tiles, masks, *refs):
    parts, (innovations_ref, error_ref) = refs[:-2], refs[-2:]
    _, within, per_row = place()
    pieces = innovations_ref.shape[0]
    for mask, part in zip(masks, parts):
        there = within ^ mask
        for a in range(tiles):
            innovations_ref[pl.ds(a * per_row + there, 1), :] = part[pieces + a : pieces + a + 1, :]
        error_ref[pl.ds(there, 1), :] = part[pieces + tiles : pieces + tiles + 1, :]


def total_of(x):
    return jnp.sum(jnp.sum(x, axis=0, keepdims=True), axis=1, keepdims=True)


def second_kernel(reach_tiles, inverse_members, peers, class_vmem, share_ref, innovations_ref, error_ref, *refs):
    parts, refs = refs[:peers], refs[peers:]
    sent, refs = refs[:peers], refs[peers:]
    state_ref, class_ref, direction, residual, start, column, across, sums, product, class_arrived = refs
    class_copy = pltpu.make_async_copy(class_vmem, class_ref, class_arrived)
    class_copy.start()
    row_index, within, per_row = place()
    innovations = innovations_ref[...]
    image = parts[0][...]
    for part in parts[1:]:
        image = image + part[...]
    norm_now = total_of(innovations * innovations)
    alpha = norm_now / total_of(innovations * image)
    residual_now = innovations - alpha * image
    norm_next = total_of(residual_now * residual_now)
    direction_now = residual_now + (norm_next / norm_now) * innovations
    residual[...] = residual_now
    direction[...] = direction_now
    start[...] = alpha * innovations
    spread_vector(direction, column)
    class_copy.wait()
    shared = (class_ref, share_ref, direction, column, across, sums, product)
    apply_share(reach_tiles, inverse_members, *shared)
    of_row = direction[pl.ds(row_index * per_row, per_row), :]
    curvature = total_of(direction_now * product[...]) + total_of(error_ref[...] * of_row * of_row)
    for peer in range(peers):
        at = (row_index ^ peer) * per_row + within
        sent[peer][0:1, :] = product[pl.ds(at, 1), :]
        sent[peer][1:2, :] = jnp.broadcast_to(curvature, (1, LANES))
    own = pl.ds(row_index * per_row + within, 1)
    state_ref[0:1, :] = start[own, :]
    state_ref[1:2, :] = residual[own, :]
    state_ref[2:3, :] = direction[own, :]
    state_ref[3:4, :] = error_ref[pl.ds(within, 1), :] * direction[own, :]
    state_ref[4:5, :] = jnp.broadcast_to(norm_next, (1, LANES))


def last_kernel(state_ref, *refs):
    parts, (solution_ref, residual_ref) = refs[:-2], refs[-2:]
    image = state_ref[3:4, :] + parts[0][0:1, :]
    curvature = parts[0][1:2, :]
    for part in parts[1:]:
        image = image + part[0:1, :]
        curvature = curvature + part[1:2, :]
    alpha = state_ref[4:5, :] / curvature
    solution_ref[...] = state_ref[0:1, :] + alpha * state_ref[2:3, :]
    residual_ref[...] = state_ref[1:2, :] - alpha * image


VMEM_SPEC = pl.BlockSpec(memory_space=pltpu.VMEM)
SMEM_SPEC = pl.BlockSpec(memory_space=pltpu.SMEM)
HBM_SPEC = pl.BlockSpec(memory_space=pltpu.HBM)


def in_hbm(x):
    return pltpu.with_memory_space_constraint(x, pltpu.HBM)


def exchange(axes, masks, values):
    count = math.prod(lax.axis_size(axis) for axis in axes)
    return [
        lax.ppermute(value, axes, [(i, i ^ mask) for i in range(count)]) if mask else value
        for mask, value in zip(masks, values)
    ]


def nearest_first(count):
    return tuple(range(count))


def farthest_first(count):
    return (0,) + tuple(range(count - 1, 0, -1))


def vectors_only(anomalies, innovations, obs_error, track_pos, taper_class):
    row_count = lax.axis_size("row")
    sub_count = lax.axis_size("sub")
    per_row = lax.axis_size("col") * sub_count
    local_members, total_obs = anomalies.shape
    member_total = local_members * row_count * sub_count
    inverse_members = 1.0 / (member_total - 1)
    reach_tiles = max(2, row_count // 4)
    pieces = total_obs // LANES
    block_len = total_obs // row_count
    f32 = jnp.float32
    row, here = ("row",), ("col", "sub")
    params = pltpu.CompilerParams(vmem_limit_bytes=16 * 1024 * 1024)

    mate = lax.ppermute(anomalies, "sub", [(0, 1), (1, 0)])
    chunk = innovations.reshape(1, LANES)
    chunk_order = farthest_first(row_count)
    chunks = exchange(row, chunk_order, [chunk] * row_count)

    class_here = pltpu.SMEM(taper_class.shape, jnp.int32)
    work = [pltpu.VMEM((block_len, LANES), f32), pltpu.VMEM((8, total_obs), f32)]
    share = pl.pallas_call(
        functools.partial(share_kernel, reach_tiles),
        out_shape=pltpu.VMEM((row_count + off_diagonal(row_count), block_len, block_len), f32),
        in_specs=[HBM_SPEC] * 3 + [VMEM_SPEC],
        out_specs=VMEM_SPEC,
        scratch_shapes=[
            class_here,
            pltpu.VMEM((1, total_obs), f32),
            pltpu.VMEM((2 * local_members, total_obs), anomalies.dtype),
            pltpu.VMEM((total_obs, 2 * local_members), anomalies.dtype),
            pltpu.VMEM((total_obs, LANES), f32),
            pltpu.SemaphoreType.DMA((3,)),
        ],
        compiler_params=params,
        cost_estimate=pl.CostEstimate(
            flops=4 * local_members * total_obs * total_obs,
            bytes_accessed=4 * total_obs * total_obs,
            transcendentals=total_obs * total_obs,
        ),
        name="share",
    )(in_hbm(taper_class), in_hbm(track_pos.reshape(1, total_obs)), in_hbm(anomalies), mate)

    payload = pl.pallas_call(
        functools.partial(first_kernel, reach_tiles, inverse_members, chunk_order),
        out_shape=pltpu.VMEM((pieces + 8, LANES), f32),
        in_specs=[VMEM_SPEC] * (row_count + 3),
        out_specs=VMEM_SPEC,
        scratch_shapes=[class_here, pltpu.VMEM((row_count, LANES), f32), pltpu.VMEM((row_count * LANES, LANES), f32)]
        + work
        + [pltpu.SemaphoreType.DMA(())],
        compiler_params=params,
        name="first",
    )(taper_class, share, obs_error.reshape(1, LANES), *chunks)
    payload_order = farthest_first(per_row)
    payloads = exchange(here, payload_order, [payload] * per_row)
    part = pl.pallas_call(
        functools.partial(middle_kernel, pieces),
        out_shape=pltpu.VMEM((pieces, LANES), f32),
        in_specs=[VMEM_SPEC] * per_row,
        out_specs=VMEM_SPEC,
        compiler_params=params,
        name="middle",
    )(*payloads)
    parts = exchange(row, farthest_first(row_count), [part] * row_count)
    whole, error = pl.pallas_call(
        functools.partial(gather_kernel, row_count, payload_order),
        out_shape=[pltpu.VMEM((pieces, LANES), f32), pltpu.VMEM((per_row, LANES), f32)],
        in_specs=[VMEM_SPEC] * per_row,
        out_specs=[VMEM_SPEC] * 2,
        compiler_params=params,
        name="gather",
    )(*payloads)

    *sent, state = pl.pallas_call(
        functools.partial(second_kernel, reach_tiles, inverse_members, row_count),
        out_shape=[pltpu.VMEM((8, LANES), f32) for _ in range(row_count + 1)],
        in_specs=[VMEM_SPEC] * (row_count + 4),
        out_specs=[VMEM_SPEC] * (row_count + 1),
        scratch_shapes=[class_here]
        + [pltpu.VMEM((pieces, LANES), f32)] * 3
        + [pltpu.VMEM((total_obs, LANES), f32)]
        + work
        + [pltpu.VMEM((pieces, LANES), f32), pltpu.SemaphoreType.DMA(())],
        compiler_params=params,
        name="second",
    )(taper_class, share, whole, error, *parts)
    last_order = farthest_first(row_count)
    got = exchange(row, last_order, [sent[mask] for mask in last_order])
    solution_part, residual_part = pl.pallas_call(
        last_kernel,
        out_shape=[jax.ShapeDtypeStruct((1, LANES), f32)] * 2,
        in_specs=[VMEM_SPEC] * (row_count + 1),
        out_specs=[VMEM_SPEC] * 2,
        compiler_params=pltpu.CompilerParams(vmem_limit_bytes=1024 * 1024),
        name="last",
    )(state, *got)
    return solution_part.reshape(LANES), residual_part.reshape(LANES)


def fits(anomalies, innovations, obs_error, track_pos, taper_class):
    row_count = lax.axis_size("row")
    per_row = lax.axis_size("col") * lax.axis_size("sub")
    local_members, total_obs = anomalies.shape
    block_len = total_obs // row_count
    share_bytes = 4 * (row_count + off_diagonal(row_count)) * block_len * block_len
    return (
        ITERS == 2
        and row_count in (2, 4)
        and per_row in (2, 4)
        and lax.axis_size("sub") == 2
        and innovations.shape[0] == LANES
        and total_obs == row_count * per_row * LANES
        and local_members % LANES == 0
        and share_bytes <= 16 * 1024 * 1024
    )


def per_device(*args):
    return vectors_only(*args) if fits(*args) else blocks(*args)


def squares(residual):
    return lax.psum(jnp.sum(residual * residual), ("row", "col", "sub"))


def blocks(anomalies, innovations, obs_error, track_pos, taper_class):
    row_count = lax.axis_size("row")
    col_count = lax.axis_size("col")
    sub_count = lax.axis_size("sub")
    row_index = lax.axis_index("row")
    col_index = lax.axis_index("col")
    local_members, total_obs = anomalies.shape
    block_len = total_obs // row_count
    quarter_len = block_len // col_count
    member_total = local_members * row_count * sub_count
    inverse_members = 1.0 / (member_total - 1)
    reach_tiles = max(2, row_count // 4)
    class_row = lax.dynamic_index_in_dim(taper_class, row_index, 0, keepdims=False)
    tile_weight = jnp.maximum(0.0, 1.0 - class_row.astype(jnp.float32) / reach_tiles)
    row_pos = lax.dynamic_slice_in_dim(track_pos, row_index * block_len, block_len, 0)
    col_pos = lax.dynamic_index_in_dim(
        track_pos.reshape(row_count, col_count, quarter_len), col_index, 1, keepdims=False
    )
    own_block = lax.all_to_all(anomalies, "row", split_axis=1, concat_axis=0, tiled=True)
    own_quarter = lax.dynamic_slice_in_dim(own_block, col_index * quarter_len, quarter_len, 1)

    def one_tile(piece, block_index, keep_factor):
        product = jnp.einsum("mi,mq->iq", own_block, piece, preferred_element_type=jnp.float32)
        column_pos = lax.dynamic_index_in_dim(col_pos, block_index, 0, keepdims=False)
        weight_here = lax.dynamic_index_in_dim(tile_weight, block_index, 0, keepdims=False)
        distance = row_pos[:, None] - column_pos[None, :]
        taper = weight_here * keep_factor * jnp.exp(-(distance * distance) / track_width)
        return product * (taper * inverse_members)

    def one_entry(entry):
        return one_tile(entry[0], entry[1], 1.0)

    piece = lax.all_gather(own_quarter[None], "row", axis=0, tiled=True)
    indices = jnp.arange(piece.shape[0], dtype=jnp.int32)
    tiles = lax.map(one_entry, (piece, indices))
    solution = jnp.zeros_like(innovations)
    residual = innovations
    direction_vec = innovations
    norm_now = squares(residual)
    for turn_index in range(ITERS):
        column_vec = lax.all_gather(direction_vec, ("row", "sub"), axis=0, tiled=True).reshape(
            row_count, quarter_len
        )
        direct = jnp.einsum("jiq,jq->i", tiles, column_vec, precision=lax.Precision.HIGHEST)
        extra = obs_error * direction_vec
        own_part = lax.psum_scatter(direct, ("col", "sub"), scatter_dimension=0, tiled=True)
        image = own_part + extra
        alpha = norm_now / lax.psum(jnp.sum(direction_vec * image), ("row", "col", "sub"))
        solution = solution + alpha * direction_vec
        residual = residual - alpha * image
        if turn_index + 1 < ITERS:
            norm_next = squares(residual)
            direction_vec = residual + norm_next / norm_now * direction_vec
            norm_now = norm_next
    return (solution, residual)


def solution(mesh):
    in_specs = (
        P(("group", "row", "sub"), None),
        P(("group", "row", "col", "sub")),
        P(("group", "row", "col", "sub")),
        P("group"),
        P("group", None),
    )
    out_specs = (P(("group", "row", "col", "sub")), P(("group", "row", "col", "sub")))
    return jax.shard_map(
        per_device, mesh=mesh, in_specs=in_specs, out_specs=out_specs, check_vma=False
    )
```

```python
import functools
import math

import jax
import jax.numpy as jnp
from jax import lax
from jax.experimental import pallas as pl
from jax.experimental.pallas import tpu as pltpu
from jax.sharding import PartitionSpec as P

ITERS = 2
LANES = 128


track_width = 0.0001
exp2_rate = -math.log2(math.e) / track_width


def off_diagonal(tiles):
    return tiles * (tiles - 1) // 2


def first_slot(a, tiles):
    return a * tiles - (a * (a + 1)) // 2


def for_each_pair(reach_tiles, class_ref, action):
    tiles = class_ref.shape[0]

    def one_pair(slot, carry):
        a = jnp.int32(0)
        for row in range(1, tiles - 1):
            a = a + (slot >= first_slot(row, tiles)).astype(jnp.int32)
        b = slot - first_slot(a, tiles) + a + 1
        pl.when(class_ref[a, b] < reach_tiles)(lambda: action(slot, a, b))
        return carry

    lax.fori_loop(0, off_diagonal(tiles), one_pair, 0)


def block_at(a, block_len):
    return pl.ds(pl.multiple_of(a * block_len, LANES), block_len)


def share_kernel(
    reach_tiles, class_hbm, pos_hbm, chunk_hbm, error_hbm, own_ref, mate_ref, share_ref, class_ref, chunk_ref, error_ref,
    *scratch
):
    pos_ref, both, turned, column, arrived = scratch
    members, total_obs = own_ref.shape
    tiles = class_ref.shape[0]
    block_len = total_obs // tiles
    pos_copy = pltpu.make_async_copy(pos_hbm, pos_ref, arrived.at[0])
    own_copy = pltpu.make_async_copy(own_ref, both.at[pl.ds(0, members), :], arrived.at[1])
    class_copy = pltpu.make_async_copy(class_hbm, class_ref, arrived.at[2])
    chunk_copy = pltpu.make_async_copy(chunk_hbm, chunk_ref, arrived.at[3])
    error_copy = pltpu.make_async_copy(error_hbm, error_ref, arrived.at[4])
    for copy in (pos_copy, own_copy, class_copy, chunk_copy, error_copy):
        copy.start()
    both[members:, :] = mate_ref[...]
    turned[:, members:] = mate_ref[...].T
    pos_copy.wait()
    spread_columns(pos_ref[...], column)
    own_copy.wait()
    turned[:, :members] = both[:members, :].T
    for copy in (class_copy, chunk_copy, error_copy):
        copy.wait()
    rows = 128

    def make_tile(slot, a, b):
        rows_at, columns_at = block_at(a, block_len), block_at(b, block_len)
        right = both[:, columns_at]
        right_pos = pos_ref[:, columns_at]
        left_turned, left_column, tile = turned.at[rows_at, :], column.at[rows_at, :], share_ref.at[slot]
        for begin in range(0, block_len, rows):
            part = slice(begin, begin + rows)
            product = jnp.dot(left_turned[part, :], right, preferred_element_type=jnp.float32)
            left_pos = jnp.concatenate([left_column[part, :]] * (block_len // LANES), axis=1)
            distance = left_pos - right_pos
            tile[part, :] = product * jnp.exp2(distance * distance * exp2_rate)

    def make_diagonal(slot, carry):
        make_tile(slot, slot, slot)
        return carry

    lax.fori_loop(0, tiles, make_diagonal, 0)
    for_each_pair(reach_tiles, class_ref, lambda slot, a, b: make_tile(slot + tiles, a, b))


def spread_columns(row, column):
    for begin in range(0, column.shape[0], LANES):
        square = jnp.broadcast_to(row[:, begin : begin + LANES], (LANES, LANES))
        column[begin : begin + LANES, :] = square.T


def spread_vector(vector, column):
    for piece in range(vector.shape[0]):
        square = jnp.broadcast_to(vector[piece : piece + 1, :], (LANES, LANES))
        column[piece * LANES : (piece + 1) * LANES, :] = square.T


def tile_weight(klass, reach_tiles, inverse_members):
    return jnp.maximum(0.0, 1.0 - klass.astype(jnp.float32) / reach_tiles) * inverse_members


def add_sums(into, weight, totals):
    for lane, total in enumerate(totals):
        into[:, lane * LANES : (lane + 1) * LANES] += weight * total


def add_turned(into, weight, across):
    for lane in range(across.shape[0] // LANES):
        where = slice(lane * LANES, (lane + 1) * LANES)
        turned = across[where, :].T
        folded = turned[:8, :]
        for begin in range(8, LANES, 8):
            folded = folded + turned[begin : begin + 8, :]
        into[:, where] += weight * folded


def fold_sums(sums, out_ref):
    for piece in range(sums.shape[1] // LANES):
        out_ref[piece : piece + 1, :] = jnp.sum(sums[:, piece * LANES : (piece + 1) * LANES], axis=0, keepdims=True)


def apply_share(reach_tiles, inverse_members, class_ref, share_ref, vector, column, across, sums, out_ref):
    tiles = class_ref.shape[0]
    block_len = share_ref.shape[1]
    lanes = block_len // LANES
    sums[...] = jnp.zeros_like(sums)

    def add_diagonal(a, carry):
        at = block_at(a, block_len)
        tile, factor = share_ref.at[a], column.at[at, :]
        totals = [None] * lanes
        for begin in range(0, block_len, 8):
            part = slice(begin, begin + 8)
            for lane in range(lanes):
                term = tile[part, lane * LANES : (lane + 1) * LANES] * factor[part, :]
                totals[lane] = term if totals[lane] is None else totals[lane] + term
        add_sums(sums.at[:, at], tile_weight(class_ref[a, a], reach_tiles, inverse_members), totals)
        return carry

    def add_pair(slot, a, b):
        weight = tile_weight(class_ref[a, b], reach_tiles, inverse_members)
        at_a, at_b = block_at(a, block_len), block_at(b, block_len)
        tile, factor = share_ref.at[slot + tiles], column.at[at_a, :]
        rows_b = [jnp.broadcast_to(vector[pl.ds(b * lanes + lane, 1), :], (8, LANES)) for lane in range(lanes)]
        totals = [None] * lanes
        for begin in range(0, block_len, 8):
            part = slice(begin, begin + 8)
            line = None
            for lane in range(lanes):
                here = tile[part, lane * LANES : (lane + 1) * LANES]
                term = here * factor[part, :]
                totals[lane] = term if totals[lane] is None else totals[lane] + term
                term = here * rows_b[lane]
                line = term if line is None else line + term
            across[part, :] = line
        add_sums(sums.at[:, at_b], weight, totals)
        add_turned(sums.at[:, at_a], weight, across)

    lax.fori_loop(0, tiles, add_diagonal, 0)
    for_each_pair(reach_tiles, class_ref, add_pair)
    fold_sums(sums, out_ref)


def place():
    sub_count = lax.axis_size("sub")
    within = lax.axis_index("col") * sub_count + lax.axis_index("sub")
    return lax.axis_index("row"), within, lax.axis_size("col") * sub_count


def first_kernel(reach_tiles, inverse_members, masks, class_ref, share_ref, error_ref, *refs):
    tiles = class_ref.shape[0]
    chunks, refs = refs[:tiles], refs[tiles:]
    out_ref, vector, column, across, sums = refs
    row_index, within, per_row = place()
    block_len = share_ref.shape[1]
    lanes = block_len // LANES
    pieces = tiles * lanes
    for mask, chunk in zip(masks, chunks):
        vector[pl.ds(row_index ^ mask, 1), :] = chunk[...]
    spread_vector(vector, column)
    sums[...] = jnp.zeros_like(sums)
    chunk_at = pl.ds(pl.multiple_of(within * LANES, LANES), LANES)

    def sums_of_rows(tile, a):
        strip, factor = tile.at[chunk_at, :], column.at[pl.ds(pl.multiple_of(a * LANES, LANES), LANES), :]
        totals = [None] * lanes
        for begin in range(0, LANES, 8):
            part = slice(begin, begin + 8)
            for lane in range(lanes):
                term = strip[part, lane * LANES : (lane + 1) * LANES] * factor[part, :]
                totals[lane] = term if totals[lane] is None else totals[lane] + term
        return totals

    def add_diagonal(a, carry):
        weight = tile_weight(class_ref[a, a], reach_tiles, inverse_members)
        add_sums(sums.at[:, block_at(a, block_len)], weight, sums_of_rows(share_ref.at[a], a))
        return carry

    def add_pair(slot, a, b):
        weight = tile_weight(class_ref[a, b], reach_tiles, inverse_members)
        tile = share_ref.at[slot + tiles]
        add_sums(sums.at[:, block_at(b, block_len)], weight, sums_of_rows(tile, a))
        across[...] = tile[:, chunk_at] * vector[pl.ds(b, 1), :]
        add_turned(sums.at[:, block_at(a, block_len)], weight, across)

    lax.fori_loop(0, tiles, add_diagonal, 0)
    for_each_pair(reach_tiles, class_ref, add_pair)
    fold_sums(sums, out_ref)
    own = row_index * per_row + within
    out_ref[pl.ds(own, 1), :] += error_ref[...] * chunks[0][...]
    out_ref[pieces : pieces + tiles, :] = vector[...]
    out_ref[pieces + tiles : pieces + tiles + 1, :] = error_ref[...]


def middle_kernel(pieces, *refs):
    parts, out_ref = refs[:-1], refs[-1]
    total = parts[0][:pieces, :]
    for part in parts[1:]:
        total = total + part[:pieces, :]
    out_ref[...] = total


def gather_kernel(tiles, masks, *refs):
    parts, (innovations_ref, error_ref) = refs[:-2], refs[-2:]
    _, within, per_row = place()
    pieces = innovations_ref.shape[0]
    for mask, part in zip(masks, parts):
        there = within ^ mask
        for a in range(tiles):
            innovations_ref[pl.ds(a * per_row + there, 1), :] = part[pieces + a : pieces + a + 1, :]
        error_ref[pl.ds(there, 1), :] = part[pieces + tiles : pieces + tiles + 1, :]


def total_of(x):
    return jnp.sum(jnp.sum(x, axis=0, keepdims=True), axis=1, keepdims=True)


def second_kernel(reach_tiles, inverse_members, peers, class_ref, share_ref, innovations_ref, error_ref, *refs):
    parts, refs = refs[:peers], refs[peers:]
    sent, refs = refs[:peers], refs[peers:]
    state_ref, direction, residual, start, column, across, sums, product = refs
    row_index, within, per_row = place()
    innovations = innovations_ref[...]
    image = parts[0][...]
    for part in parts[1:]:
        image = image + part[...]
    norm_now = total_of(innovations * innovations)
    alpha = norm_now / total_of(innovations * image)
    residual_now = innovations - alpha * image
    norm_next = total_of(residual_now * residual_now)
    direction_now = residual_now + (norm_next / norm_now) * innovations
    residual[...] = residual_now
    direction[...] = direction_now
    start[...] = alpha * innovations
    spread_vector(direction, column)
    shared = (class_ref, share_ref, direction, column, across, sums, product)
    apply_share(reach_tiles, inverse_members, *shared)
    of_row = direction[pl.ds(row_index * per_row, per_row), :]
    curvature = total_of(direction_now * product[...]) + total_of(error_ref[...] * of_row * of_row)
    for peer in range(peers):
        at = (row_index ^ peer) * per_row + within
        sent[peer][0:1, :] = product[pl.ds(at, 1), :]
        sent[peer][1:2, :] = jnp.broadcast_to(curvature, (1, LANES))
    own = pl.ds(row_index * per_row + within, 1)
    state_ref[0:1, :] = start[own, :]
    state_ref[1:2, :] = residual[own, :]
    state_ref[2:3, :] = direction[own, :]
    state_ref[3:4, :] = error_ref[pl.ds(within, 1), :] * direction[own, :]
    state_ref[4:5, :] = jnp.broadcast_to(norm_next, (1, LANES))


def last_kernel(state_ref, *refs):
    parts, (solution_ref, residual_ref) = refs[:-2], refs[-2:]
    image = state_ref[3:4, :] + parts[0][0:1, :]
    curvature = parts[0][1:2, :]
    for part in parts[1:]:
        image = image + part[0:1, :]
        curvature = curvature + part[1:2, :]
    alpha = state_ref[4:5, :] / curvature
    solution_ref[...] = state_ref[0:1, :] + alpha * state_ref[2:3, :]
    residual_ref[...] = state_ref[1:2, :] - alpha * image


VMEM_SPEC = pl.BlockSpec(memory_space=pltpu.VMEM)
SMEM_SPEC = pl.BlockSpec(memory_space=pltpu.SMEM)
HBM_SPEC = pl.BlockSpec(memory_space=pltpu.HBM)


def in_hbm(x):
    return pltpu.with_memory_space_constraint(x, pltpu.HBM)


def exchange(axes, masks, values):
    count = math.prod(lax.axis_size(axis) for axis in axes)
    return [
        lax.ppermute(value, axes, [(i, i ^ mask) for i in range(count)]) if mask else value
        for mask, value in zip(masks, values)
    ]


def nearest_first(count):
    return tuple(range(count))


def farthest_first(count):
    return (0,) + tuple(range(count - 1, 0, -1))


def vectors_only(anomalies, innovations, obs_error, track_pos, taper_class):
    row_count = lax.axis_size("row")
    sub_count = lax.axis_size("sub")
    per_row = lax.axis_size("col") * sub_count
    local_members, total_obs = anomalies.shape
    member_total = local_members * row_count * sub_count
    inverse_members = 1.0 / (member_total - 1)
    reach_tiles = max(2, row_count // 4)
    pieces = total_obs // LANES
    block_len = total_obs // row_count
    f32 = jnp.float32
    row, here = ("row",), ("col", "sub")
    params = pltpu.CompilerParams(vmem_limit_bytes=16 * 1024 * 1024)

    mate = lax.ppermute(anomalies, "sub", [(0, 1), (1, 0)])
    chunk = innovations.reshape(1, LANES)
    error = obs_error.reshape(1, LANES)
    chunk_order = farthest_first(row_count)
    chunks = exchange(row, chunk_order, [chunk] * row_count)

    work = [pltpu.VMEM((block_len, LANES), f32), pltpu.VMEM((8, total_obs), f32)]
    share, classes, own_chunk, own_error = pl.pallas_call(
        functools.partial(share_kernel, reach_tiles),
        out_shape=[
            pltpu.VMEM((row_count + off_diagonal(row_count), block_len, block_len), f32),
            pltpu.SMEM(taper_class.shape, jnp.int32),
            pltpu.VMEM((1, LANES), f32),
            pltpu.VMEM((1, LANES), f32),
        ],
        in_specs=[HBM_SPEC] * 5 + [VMEM_SPEC],
        out_specs=[VMEM_SPEC, SMEM_SPEC, VMEM_SPEC, VMEM_SPEC],
        scratch_shapes=[
            pltpu.VMEM((1, total_obs), f32),
            pltpu.VMEM((2 * local_members, total_obs), anomalies.dtype),
            pltpu.VMEM((total_obs, 2 * local_members), anomalies.dtype),
            pltpu.VMEM((total_obs, LANES), f32),
            pltpu.SemaphoreType.DMA((5,)),
        ],
        compiler_params=params,
        cost_estimate=pl.CostEstimate(
            flops=4 * local_members * total_obs * total_obs,
            bytes_accessed=4 * total_obs * total_obs,
            transcendentals=total_obs * total_obs,
        ),
        name="share",
    )(*[in_hbm(x) for x in (taper_class, track_pos.reshape(1, total_obs), chunk, error, anomalies)], mate)

    payload = pl.pallas_call(
        functools.partial(first_kernel, reach_tiles, inverse_members, chunk_order),
        out_shape=pltpu.VMEM((pieces + 8, LANES), f32),
        in_specs=[SMEM_SPEC] + [VMEM_SPEC] * (row_count + 2),
        out_specs=VMEM_SPEC,
        scratch_shapes=[pltpu.VMEM((row_count, LANES), f32), pltpu.VMEM((row_count * LANES, LANES), f32)]
        + work,
        compiler_params=params,
        name="first",
    )(classes, share, own_error, own_chunk, *chunks[1:])
    payload_order = farthest_first(per_row)
    payloads = exchange(here, payload_order, [payload] * per_row)
    part = pl.pallas_call(
        functools.partial(middle_kernel, pieces),
        out_shape=pltpu.VMEM((pieces, LANES), f32),
        in_specs=[VMEM_SPEC] * per_row,
        out_specs=VMEM_SPEC,
        compiler_params=params,
        name="middle",
    )(*payloads)
    parts = exchange(row, farthest_first(row_count), [part] * row_count)
    whole, error = pl.pallas_call(
        functools.partial(gather_kernel, row_count, payload_order),
        out_shape=[pltpu.VMEM((pieces, LANES), f32), pltpu.VMEM((per_row, LANES), f32)],
        in_specs=[VMEM_SPEC] * per_row,
        out_specs=[VMEM_SPEC] * 2,
        compiler_params=params,
        name="gather",
    )(*payloads)

    *sent, state = pl.pallas_call(
        functools.partial(second_kernel, reach_tiles, inverse_members, row_count),
        out_shape=[pltpu.VMEM((8, LANES), f32) for _ in range(row_count + 1)],
        in_specs=[SMEM_SPEC] + [VMEM_SPEC] * (row_count + 3),
        out_specs=[VMEM_SPEC] * (row_count + 1),
        scratch_shapes=[pltpu.VMEM((pieces, LANES), f32)] * 3
        + [pltpu.VMEM((total_obs, LANES), f32)]
        + work
        + [pltpu.VMEM((pieces, LANES), f32)],
        compiler_params=params,
        name="second",
    )(classes, share, whole, error, *parts)
    last_order = farthest_first(row_count)
    got = exchange(row, last_order, [sent[mask] for mask in last_order])
    solution_part, residual_part = pl.pallas_call(
        last_kernel,
        out_shape=[jax.ShapeDtypeStruct((1, LANES), f32)] * 2,
        in_specs=[VMEM_SPEC] * (row_count + 1),
        out_specs=[VMEM_SPEC] * 2,
        compiler_params=pltpu.CompilerParams(vmem_limit_bytes=1024 * 1024),
        name="last",
    )(state, *got)
    return solution_part.reshape(LANES), residual_part.reshape(LANES)


def fits(anomalies, innovations, obs_error, track_pos, taper_class):
    row_count = lax.axis_size("row")
    per_row = lax.axis_size("col") * lax.axis_size("sub")
    local_members, total_obs = anomalies.shape
    block_len = total_obs // row_count
    share_bytes = 4 * (row_count + off_diagonal(row_count)) * block_len * block_len
    return (
        ITERS == 2
        and row_count in (2, 4)
        and per_row in (2, 4)
        and lax.axis_size("sub") == 2
        and innovations.shape[0] == LANES
        and total_obs == row_count * per_row * LANES
        and local_members % LANES == 0
        and share_bytes <= 16 * 1024 * 1024
    )


def per_device(*args):
    return vectors_only(*args) if fits(*args) else blocks(*args)


def squares(residual):
    return lax.psum(jnp.sum(residual * residual), ("row", "col", "sub"))


def blocks(anomalies, innovations, obs_error, track_pos, taper_class):
    row_count = lax.axis_size("row")
    col_count = lax.axis_size("col")
    sub_count = lax.axis_size("sub")
    row_index = lax.axis_index("row")
    col_index = lax.axis_index("col")
    local_members, total_obs = anomalies.shape
    block_len = total_obs // row_count
    quarter_len = block_len // col_count
    member_total = local_members * row_count * sub_count
    inverse_members = 1.0 / (member_total - 1)
    reach_tiles = max(2, row_count // 4)
    class_row = lax.dynamic_index_in_dim(taper_class, row_index, 0, keepdims=False)
    tile_weight = jnp.maximum(0.0, 1.0 - class_row.astype(jnp.float32) / reach_tiles)
    row_pos = lax.dynamic_slice_in_dim(track_pos, row_index * block_len, block_len, 0)
    col_pos = lax.dynamic_index_in_dim(
        track_pos.reshape(row_count, col_count, quarter_len), col_index, 1, keepdims=False
    )
    own_block = lax.all_to_all(anomalies, "row", split_axis=1, concat_axis=0, tiled=True)
    own_quarter = lax.dynamic_slice_in_dim(own_block, col_index * quarter_len, quarter_len, 1)

    def one_tile(piece, block_index, keep_factor):
        product = jnp.einsum("mi,mq->iq", own_block, piece, preferred_element_type=jnp.float32)
        column_pos = lax.dynamic_index_in_dim(col_pos, block_index, 0, keepdims=False)
        weight_here = lax.dynamic_index_in_dim(tile_weight, block_index, 0, keepdims=False)
        distance = row_pos[:, None] - column_pos[None, :]
        taper = weight_here * keep_factor * jnp.exp(-(distance * distance) / track_width)
        return product * (taper * inverse_members)

    def one_entry(entry):
        return one_tile(entry[0], entry[1], 1.0)

    piece = lax.all_gather(own_quarter[None], "row", axis=0, tiled=True)
    indices = jnp.arange(piece.shape[0], dtype=jnp.int32)
    tiles = lax.map(one_entry, (piece, indices))
    solution = jnp.zeros_like(innovations)
    residual = innovations
    direction_vec = innovations
    norm_now = squares(residual)
    for turn_index in range(ITERS):
        column_vec = lax.all_gather(direction_vec, ("row", "sub"), axis=0, tiled=True).reshape(
            row_count, quarter_len
        )
        direct = jnp.einsum("jiq,jq->i", tiles, column_vec, precision=lax.Precision.HIGHEST)
        extra = obs_error * direction_vec
        own_part = lax.psum_scatter(direct, ("col", "sub"), scatter_dimension=0, tiled=True)
        image = own_part + extra
        alpha = norm_now / lax.psum(jnp.sum(direction_vec * image), ("row", "col", "sub"))
        solution = solution + alpha * direction_vec
        residual = residual - alpha * image
        if turn_index + 1 < ITERS:
            norm_next = squares(residual)
            direction_vec = residual + norm_next / norm_now * direction_vec
            norm_now = norm_next
    return (solution, residual)


def solution(mesh):
    in_specs = (
        P(("group", "row", "sub"), None),
        P(("group", "row", "col", "sub")),
        P(("group", "row", "col", "sub")),
        P("group"),
        P("group", None),
    )
    out_specs = (P(("group", "row", "col", "sub")), P(("group", "row", "col", "sub")))
    return jax.shard_map(
        per_device, mesh=mesh, in_specs=in_specs, out_specs=out_specs, check_vma=False
    )
```

```python
import functools
import math

import jax
import jax.numpy as jnp
from jax import lax
from jax.experimental import pallas as pl
from jax.experimental.pallas import tpu as pltpu
from jax.sharding import PartitionSpec as P

ITERS = 2
LANES = 128


track_width = 0.0001
exp2_rate = -math.log2(math.e) / track_width


def off_diagonal(tiles):
    return tiles * (tiles - 1) // 2


def first_slot(a, tiles):
    return a * tiles - (a * (a + 1)) // 2


def for_each_pair(reach_tiles, class_ref, action):
    tiles = class_ref.shape[0]

    def one_pair(slot, carry):
        a = jnp.int32(0)
        for row in range(1, tiles - 1):
            a = a + (slot >= first_slot(row, tiles)).astype(jnp.int32)
        b = slot - first_slot(a, tiles) + a + 1
        pl.when(class_ref[a, b] < reach_tiles)(lambda: action(slot, a, b))
        return carry

    lax.fori_loop(0, off_diagonal(tiles), one_pair, 0)


def block_at(a, block_len):
    return pl.ds(pl.multiple_of(a * block_len, LANES), block_len)


def make_part(target, left_turned, right, left_column, right_pos):
    product = jnp.dot(left_turned, right, preferred_element_type=jnp.float32)
    left_pos = jnp.concatenate([left_column] * (right_pos.shape[1] // LANES), axis=1)
    distance = left_pos - right_pos
    target[...] = product * jnp.exp2(distance * distance * exp2_rate)


def turn_kernel(mate_ref, turned_ref):
    turned_ref[...] = mate_ref[...].T


def strips_kernel(
    reach_tiles, class_hbm, pos_ref, own_ref, mate_ref, turned_mate_ref, row_strips, column_strips, class_ref, both,
    turned, column, arrived,
):
    members, total_obs = own_ref.shape
    tiles = class_ref.shape[0]
    block_len = total_obs // tiles
    class_copy = pltpu.make_async_copy(class_hbm, class_ref, arrived)
    class_copy.start()
    both[:members, :] = own_ref[...]
    both[members:, :] = mate_ref[...]
    turned[:, :members] = own_ref[...].T
    turned[:, members:] = turned_mate_ref[...]
    spread_columns(pos_ref[...], column)
    _, within, _ = place()

    def chunk_of(a):
        return pl.ds(pl.multiple_of(a * block_len + within * LANES, LANES), LANES)

    def row_strip(target, a, b):
        at, columns_at = chunk_of(a), block_at(b, block_len)
        make_part(target, turned[at, :], both[:, columns_at], column[at, :], pos_ref[:, columns_at])

    def make_diagonal(slot, carry):
        row_strip(row_strips.at[slot], slot, slot)
        return carry

    def make_pair(slot, a, b):
        row_strip(row_strips.at[slot + tiles], a, b)
        at, columns_at = block_at(a, block_len), chunk_of(b)
        make_part(column_strips.at[slot], turned[at, :], both[:, columns_at], column[at, :], pos_ref[:, columns_at])

    lax.fori_loop(0, tiles, make_diagonal, 0)
    class_copy.wait()
    for_each_pair(reach_tiles, class_ref, make_pair)


def share_kernel(reach_tiles, class_ref, pos_ref, both, turned, column, row_strips, share_ref):
    tiles = class_ref.shape[0]
    block_len = share_ref.shape[1]
    _, within, per_row = place()

    def make_tile(slot, a, b):
        tile, columns_at = share_ref.at[slot], block_at(b, block_len)
        right, right_pos = both[:, columns_at], pos_ref[:, columns_at]
        here = pl.ds(pl.multiple_of(within * LANES, LANES), LANES)
        tile[here, :] = row_strips[slot]
        for turn in range(1, per_row):
            begin = lax.rem(within + turn, per_row) * LANES
            here = pl.ds(pl.multiple_of(begin, LANES), LANES)
            at = pl.ds(pl.multiple_of(a * block_len + begin, LANES), LANES)
            make_part(tile.at[here, :], turned[at, :], right, column[at, :], right_pos)

    def make_diagonal(slot, carry):
        make_tile(slot, slot, slot)
        return carry

    lax.fori_loop(0, tiles, make_diagonal, 0)
    for_each_pair(reach_tiles, class_ref, lambda slot, a, b: make_tile(slot + tiles, a, b))


def spread_columns(row, column):
    for begin in range(0, column.shape[0], LANES):
        square = jnp.broadcast_to(row[:, begin : begin + LANES], (LANES, LANES))
        column[begin : begin + LANES, :] = square.T


def spread_vector(vector, column):
    for piece in range(vector.shape[0]):
        square = jnp.broadcast_to(vector[piece : piece + 1, :], (LANES, LANES))
        column[piece * LANES : (piece + 1) * LANES, :] = square.T


def tile_weight(klass, reach_tiles, inverse_members):
    return jnp.maximum(0.0, 1.0 - klass.astype(jnp.float32) / reach_tiles) * inverse_members


def add_sums(into, weight, totals):
    for lane, total in enumerate(totals):
        into[:, lane * LANES : (lane + 1) * LANES] += weight * total


def add_turned(into, weight, across):
    for lane in range(across.shape[0] // LANES):
        where = slice(lane * LANES, (lane + 1) * LANES)
        turned = across[where, :].T
        folded = turned[:8, :]
        for begin in range(8, LANES, 8):
            folded = folded + turned[begin : begin + 8, :]
        into[:, where] += weight * folded


def fold_sums(sums, out_ref):
    for piece in range(sums.shape[1] // LANES):
        out_ref[piece : piece + 1, :] = jnp.sum(sums[:, piece * LANES : (piece + 1) * LANES], axis=0, keepdims=True)


def apply_share(reach_tiles, inverse_members, class_ref, share_ref, vector, column, across, sums, out_ref):
    tiles = class_ref.shape[0]
    block_len = share_ref.shape[1]
    lanes = block_len // LANES
    sums[...] = jnp.zeros_like(sums)

    def add_diagonal(a, carry):
        at = block_at(a, block_len)
        tile, factor = share_ref.at[a], column.at[at, :]
        totals = [None] * lanes
        for begin in range(0, block_len, 8):
            part = slice(begin, begin + 8)
            for lane in range(lanes):
                term = tile[part, lane * LANES : (lane + 1) * LANES] * factor[part, :]
                totals[lane] = term if totals[lane] is None else totals[lane] + term
        add_sums(sums.at[:, at], tile_weight(class_ref[a, a], reach_tiles, inverse_members), totals)
        return carry

    def add_pair(slot, a, b):
        weight = tile_weight(class_ref[a, b], reach_tiles, inverse_members)
        at_a, at_b = block_at(a, block_len), block_at(b, block_len)
        tile, factor = share_ref.at[slot + tiles], column.at[at_a, :]
        rows_b = [jnp.broadcast_to(vector[pl.ds(b * lanes + lane, 1), :], (8, LANES)) for lane in range(lanes)]
        totals = [None] * lanes
        for begin in range(0, block_len, 8):
            part = slice(begin, begin + 8)
            line = None
            for lane in range(lanes):
                here = tile[part, lane * LANES : (lane + 1) * LANES]
                term = here * factor[part, :]
                totals[lane] = term if totals[lane] is None else totals[lane] + term
                term = here * rows_b[lane]
                line = term if line is None else line + term
            across[part, :] = line
        add_sums(sums.at[:, at_b], weight, totals)
        add_turned(sums.at[:, at_a], weight, across)

    lax.fori_loop(0, tiles, add_diagonal, 0)
    for_each_pair(reach_tiles, class_ref, add_pair)
    fold_sums(sums, out_ref)


def place():
    sub_count = lax.axis_size("sub")
    within = lax.axis_index("col") * sub_count + lax.axis_index("sub")
    return lax.axis_index("row"), within, lax.axis_size("col") * sub_count


def first_kernel(reach_tiles, inverse_members, masks, class_ref, row_strips, column_strips, error_ref, *refs):
    tiles = class_ref.shape[0]
    chunks, refs = refs[:tiles], refs[tiles:]
    out_ref, vector, column, across, sums = refs
    row_index, within, per_row = place()
    block_len = row_strips.shape[2]
    lanes = block_len // LANES
    pieces = tiles * lanes
    for mask, chunk in zip(masks, chunks):
        vector[pl.ds(row_index ^ mask, 1), :] = chunk[...]
    spread_vector(vector, column)
    sums[...] = jnp.zeros_like(sums)

    def sums_of_rows(strip, a):
        factor = column.at[pl.ds(pl.multiple_of(a * LANES, LANES), LANES), :]
        totals = [None] * lanes
        for begin in range(0, LANES, 8):
            part = slice(begin, begin + 8)
            for lane in range(lanes):
                term = strip[part, lane * LANES : (lane + 1) * LANES] * factor[part, :]
                totals[lane] = term if totals[lane] is None else totals[lane] + term
        return totals

    def add_diagonal(a, carry):
        weight = tile_weight(class_ref[a, a], reach_tiles, inverse_members)
        add_sums(sums.at[:, block_at(a, block_len)], weight, sums_of_rows(row_strips.at[a], a))
        return carry

    def add_pair(slot, a, b):
        weight = tile_weight(class_ref[a, b], reach_tiles, inverse_members)
        add_sums(sums.at[:, block_at(b, block_len)], weight, sums_of_rows(row_strips.at[slot + tiles], a))
        across[...] = column_strips[slot] * vector[pl.ds(b, 1), :]
        add_turned(sums.at[:, block_at(a, block_len)], weight, across)

    lax.fori_loop(0, tiles, add_diagonal, 0)
    for_each_pair(reach_tiles, class_ref, add_pair)
    fold_sums(sums, out_ref)
    own = row_index * per_row + within
    out_ref[pl.ds(own, 1), :] += error_ref[...] * chunks[0][...]
    out_ref[pieces : pieces + tiles, :] = vector[...]
    out_ref[pieces + tiles : pieces + tiles + 1, :] = error_ref[...]


def middle_kernel(pieces, *refs):
    parts, out_ref = refs[:-1], refs[-1]
    total = parts[0][:pieces, :]
    for part in parts[1:]:
        total = total + part[:pieces, :]
    out_ref[...] = total


def gather_kernel(tiles, masks, *refs):
    parts, (innovations_ref, error_ref) = refs[:-2], refs[-2:]
    _, within, per_row = place()
    pieces = innovations_ref.shape[0]
    for mask, part in zip(masks, parts):
        there = within ^ mask
        for a in range(tiles):
            innovations_ref[pl.ds(a * per_row + there, 1), :] = part[pieces + a : pieces + a + 1, :]
        error_ref[pl.ds(there, 1), :] = part[pieces + tiles : pieces + tiles + 1, :]


def total_of(x):
    return jnp.sum(jnp.sum(x, axis=0, keepdims=True), axis=1, keepdims=True)


def second_kernel(reach_tiles, inverse_members, peers, class_ref, share_ref, innovations_ref, error_ref, *refs):
    parts, refs = refs[:peers], refs[peers:]
    sent, refs = refs[:peers], refs[peers:]
    state_ref, direction, residual, start, column, across, sums, product = refs
    row_index, within, per_row = place()
    innovations = innovations_ref[...]
    image = parts[0][...]
    for part in parts[1:]:
        image = image + part[...]
    norm_now = total_of(innovations * innovations)
    alpha = norm_now / total_of(innovations * image)
    residual_now = innovations - alpha * image
    norm_next = total_of(residual_now * residual_now)
    direction_now = residual_now + (norm_next / norm_now) * innovations
    residual[...] = residual_now
    direction[...] = direction_now
    start[...] = alpha * innovations
    spread_vector(direction, column)
    shared = (class_ref, share_ref, direction, column, across, sums, product)
    apply_share(reach_tiles, inverse_members, *shared)
    of_row = direction[pl.ds(row_index * per_row, per_row), :]
    curvature = total_of(direction_now * product[...]) + total_of(error_ref[...] * of_row * of_row)
    for peer in range(peers):
        at = (row_index ^ peer) * per_row + within
        sent[peer][0:1, :] = product[pl.ds(at, 1), :]
        sent[peer][1:2, :] = jnp.broadcast_to(curvature, (1, LANES))
    own = pl.ds(row_index * per_row + within, 1)
    state_ref[0:1, :] = start[own, :]
    state_ref[1:2, :] = residual[own, :]
    state_ref[2:3, :] = direction[own, :]
    state_ref[3:4, :] = error_ref[pl.ds(within, 1), :] * direction[own, :]
    state_ref[4:5, :] = jnp.broadcast_to(norm_next, (1, LANES))


def last_kernel(state_ref, *refs):
    parts, (solution_ref, residual_ref) = refs[:-2], refs[-2:]
    image = state_ref[3:4, :] + parts[0][0:1, :]
    curvature = parts[0][1:2, :]
    for part in parts[1:]:
        image = image + part[0:1, :]
        curvature = curvature + part[1:2, :]
    alpha = state_ref[4:5, :] / curvature
    solution_ref[...] = state_ref[0:1, :] + alpha * state_ref[2:3, :]
    residual_ref[...] = state_ref[1:2, :] - alpha * image


VMEM_SPEC = pl.BlockSpec(memory_space=pltpu.VMEM)
SMEM_SPEC = pl.BlockSpec(memory_space=pltpu.SMEM)
HBM_SPEC = pl.BlockSpec(memory_space=pltpu.HBM)


def in_hbm(x):
    return pltpu.with_memory_space_constraint(x, pltpu.HBM)


def exchange(axes, masks, values):
    count = math.prod(lax.axis_size(axis) for axis in axes)
    return [
        lax.ppermute(value, axes, [(i, i ^ mask) for i in range(count)]) if mask else value
        for mask, value in zip(masks, values)
    ]


def nearest_first(count):
    return tuple(range(count))


def farthest_first(count):
    return (0,) + tuple(range(count - 1, 0, -1))


def vectors_only(anomalies, innovations, obs_error, track_pos, taper_class):
    row_count = lax.axis_size("row")
    sub_count = lax.axis_size("sub")
    per_row = lax.axis_size("col") * sub_count
    local_members, total_obs = anomalies.shape
    member_total = local_members * row_count * sub_count
    inverse_members = 1.0 / (member_total - 1)
    reach_tiles = max(2, row_count // 4)
    pieces = total_obs // LANES
    block_len = total_obs // row_count
    f32 = jnp.float32
    row, here = ("row",), ("col", "sub")
    params = pltpu.CompilerParams(vmem_limit_bytes=16 * 1024 * 1024)

    mate = lax.ppermute(anomalies, "sub", [(0, 1), (1, 0)])
    chunk = innovations.reshape(1, LANES)
    error = obs_error.reshape(1, LANES)
    chunk_order = nearest_first(row_count)
    chunks = exchange(row, chunk_order, [chunk] * row_count)

    work = [pltpu.VMEM((block_len, LANES), f32), pltpu.VMEM((8, total_obs), f32)]
    pairs = off_diagonal(row_count)
    part_elements = (row_count + pairs) * block_len * block_len
    mate_bytes = anomalies.size * anomalies.dtype.itemsize
    turned_mate = pl.pallas_call(
        turn_kernel,
        out_shape=pltpu.VMEM((total_obs, local_members), anomalies.dtype),
        in_specs=[VMEM_SPEC],
        out_specs=VMEM_SPEC,
        compiler_params=params,
        cost_estimate=pl.CostEstimate(flops=4 * local_members * total_obs * total_obs, bytes_accessed=16 * mate_bytes, transcendentals=0),
        name="turn",
    )(mate)
    positions = track_pos.reshape(1, total_obs)
    strips, strip_columns, classes, both, turned, column = pl.pallas_call(
        functools.partial(strips_kernel, reach_tiles),
        out_shape=[
            pltpu.VMEM((row_count + pairs, LANES, block_len), f32),
            pltpu.VMEM((pairs, block_len, LANES), f32),
            pltpu.SMEM(taper_class.shape, jnp.int32),
            pltpu.VMEM((2 * local_members, total_obs), anomalies.dtype),
            pltpu.VMEM((total_obs, 2 * local_members), anomalies.dtype),
            pltpu.VMEM((total_obs, LANES), f32),
        ],
        in_specs=[HBM_SPEC] + [VMEM_SPEC] * 4,
        out_specs=[VMEM_SPEC] * 2 + [SMEM_SPEC] + [VMEM_SPEC] * 3,
        scratch_shapes=[pltpu.SemaphoreType.DMA(())],
        compiler_params=params,
        cost_estimate=pl.CostEstimate(
            flops=2 * local_members * part_elements,
            bytes_accessed=2 * part_elements,
            transcendentals=part_elements // 2,
        ),
        name="strips",
    )(in_hbm(taper_class), positions, anomalies, mate, turned_mate)

    payload = pl.pallas_call(
        functools.partial(first_kernel, reach_tiles, inverse_members, chunk_order),
        out_shape=pltpu.VMEM((pieces + 8, LANES), f32),
        in_specs=[SMEM_SPEC] + [VMEM_SPEC] * (row_count + 3),
        out_specs=VMEM_SPEC,
        scratch_shapes=[pltpu.VMEM((row_count, LANES), f32), pltpu.VMEM((row_count * LANES, LANES), f32)]
        + work,
        compiler_params=params,
        name="first",
    )(classes, strips, strip_columns, error, *chunks)
    payload_order = nearest_first(per_row)
    payloads = exchange(here, payload_order, [payload] * per_row)
    part = pl.pallas_call(
        functools.partial(middle_kernel, pieces),
        out_shape=pltpu.VMEM((pieces, LANES), f32),
        in_specs=[VMEM_SPEC] * per_row,
        out_specs=VMEM_SPEC,
        compiler_params=params,
        name="middle",
    )(*payloads)
    parts = exchange(row, nearest_first(row_count), [part] * row_count)
    whole, error = pl.pallas_call(
        functools.partial(gather_kernel, row_count, payload_order),
        out_shape=[pltpu.VMEM((pieces, LANES), f32), pltpu.VMEM((per_row, LANES), f32)],
        in_specs=[VMEM_SPEC] * per_row,
        out_specs=[VMEM_SPEC] * 2,
        compiler_params=params,
        name="gather",
    )(*payloads)

    share = pl.pallas_call(
        functools.partial(share_kernel, reach_tiles),
        out_shape=pltpu.VMEM((row_count + pairs, block_len, block_len), f32),
        in_specs=[SMEM_SPEC] + [VMEM_SPEC] * 5,
        out_specs=VMEM_SPEC,
        compiler_params=params,
        cost_estimate=pl.CostEstimate(
            flops=4 * local_members * part_elements,
            bytes_accessed=4 * part_elements,
            transcendentals=part_elements,
        ),
        name="share",
    )(classes, positions, both, turned, column, strips)
    *sent, state = pl.pallas_call(
        functools.partial(second_kernel, reach_tiles, inverse_members, row_count),
        out_shape=[pltpu.VMEM((8, LANES), f32) for _ in range(row_count + 1)],
        in_specs=[SMEM_SPEC] + [VMEM_SPEC] * (row_count + 3),
        out_specs=[VMEM_SPEC] * (row_count + 1),
        scratch_shapes=[pltpu.VMEM((pieces, LANES), f32)] * 3
        + [pltpu.VMEM((total_obs, LANES), f32)]
        + work
        + [pltpu.VMEM((pieces, LANES), f32)],
        compiler_params=params,
        name="second",
    )(classes, share, whole, error, *parts)
    last_order = farthest_first(row_count)
    got = exchange(row, last_order, [sent[mask] for mask in last_order])
    solution_part, residual_part = pl.pallas_call(
        last_kernel,
        out_shape=[jax.ShapeDtypeStruct((1, LANES), f32)] * 2,
        in_specs=[VMEM_SPEC] * (row_count + 1),
        out_specs=[VMEM_SPEC] * 2,
        compiler_params=pltpu.CompilerParams(vmem_limit_bytes=1024 * 1024),
        name="last",
    )(state, *got)
    return solution_part.reshape(LANES), residual_part.reshape(LANES)


def fits(anomalies, innovations, obs_error, track_pos, taper_class):
    row_count = lax.axis_size("row")
    per_row = lax.axis_size("col") * lax.axis_size("sub")
    local_members, total_obs = anomalies.shape
    block_len = total_obs // row_count
    share_bytes = 4 * (row_count + off_diagonal(row_count)) * block_len * block_len
    return (
        ITERS == 2
        and row_count in (2, 4)
        and per_row in (2, 4)
        and lax.axis_size("sub") == 2
        and innovations.shape[0] == LANES
        and total_obs == row_count * per_row * LANES
        and local_members % LANES == 0
        and share_bytes <= 16 * 1024 * 1024
    )


def per_device(*args):
    return vectors_only(*args) if fits(*args) else blocks(*args)


def squares(residual):
    return lax.psum(jnp.sum(residual * residual), ("row", "col", "sub"))


def blocks(anomalies, innovations, obs_error, track_pos, taper_class):
    row_count = lax.axis_size("row")
    col_count = lax.axis_size("col")
    sub_count = lax.axis_size("sub")
    row_index = lax.axis_index("row")
    col_index = lax.axis_index("col")
    local_members, total_obs = anomalies.shape
    block_len = total_obs // row_count
    quarter_len = block_len // col_count
    member_total = local_members * row_count * sub_count
    inverse_members = 1.0 / (member_total - 1)
    reach_tiles = max(2, row_count // 4)
    class_row = lax.dynamic_index_in_dim(taper_class, row_index, 0, keepdims=False)
    tile_weight = jnp.maximum(0.0, 1.0 - class_row.astype(jnp.float32) / reach_tiles)
    row_pos = lax.dynamic_slice_in_dim(track_pos, row_index * block_len, block_len, 0)
    col_pos = lax.dynamic_index_in_dim(
        track_pos.reshape(row_count, col_count, quarter_len), col_index, 1, keepdims=False
    )
    own_block = lax.all_to_all(anomalies, "row", split_axis=1, concat_axis=0, tiled=True)
    own_quarter = lax.dynamic_slice_in_dim(own_block, col_index * quarter_len, quarter_len, 1)

    def one_tile(piece, block_index, keep_factor):
        product = jnp.einsum("mi,mq->iq", own_block, piece, preferred_element_type=jnp.float32)
        column_pos = lax.dynamic_index_in_dim(col_pos, block_index, 0, keepdims=False)
        weight_here = lax.dynamic_index_in_dim(tile_weight, block_index, 0, keepdims=False)
        distance = row_pos[:, None] - column_pos[None, :]
        taper = weight_here * keep_factor * jnp.exp(-(distance * distance) / track_width)
        return product * (taper * inverse_members)

    def one_entry(entry):
        return one_tile(entry[0], entry[1], 1.0)

    piece = lax.all_gather(own_quarter[None], "row", axis=0, tiled=True)
    indices = jnp.arange(piece.shape[0], dtype=jnp.int32)
    tiles = lax.map(one_entry, (piece, indices))
    solution = jnp.zeros_like(innovations)
    residual = innovations
    direction_vec = innovations
    norm_now = squares(residual)
    for turn_index in range(ITERS):
        column_vec = lax.all_gather(direction_vec, ("row", "sub"), axis=0, tiled=True).reshape(
            row_count, quarter_len
        )
        direct = jnp.einsum("jiq,jq->i", tiles, column_vec, precision=lax.Precision.HIGHEST)
        extra = obs_error * direction_vec
        own_part = lax.psum_scatter(direct, ("col", "sub"), scatter_dimension=0, tiled=True)
        image = own_part + extra
        alpha = norm_now / lax.psum(jnp.sum(direction_vec * image), ("row", "col", "sub"))
        solution = solution + alpha * direction_vec
        residual = residual - alpha * image
        if turn_index + 1 < ITERS:
            norm_next = squares(residual)
            direction_vec = residual + norm_next / norm_now * direction_vec
            norm_now = norm_next
    return (solution, residual)


def solution(mesh):
    in_specs = (
        P(("group", "row", "sub"), None),
        P(("group", "row", "col", "sub")),
        P(("group", "row", "col", "sub")),
        P("group"),
        P("group", None),
    )
    out_specs = (P(("group", "row", "col", "sub")), P(("group", "row", "col", "sub")))
    return jax.shard_map(
        per_device, mesh=mesh, in_specs=in_specs, out_specs=out_specs, check_vma=False
    )
```

```python
import functools
import math

import jax
import jax.numpy as jnp
from jax import lax
from jax.experimental import pallas as pl
from jax.experimental.pallas import tpu as pltpu
from jax.sharding import PartitionSpec as P

ITERS = 2
LANES = 128


track_width = 0.0001
exp2_rate = -math.log2(math.e) / track_width


def off_diagonal(tiles):
    return tiles * (tiles - 1) // 2


def first_slot(a, tiles):
    return a * tiles - (a * (a + 1)) // 2


def for_each_pair(reach_tiles, class_ref, action):
    tiles = class_ref.shape[0]

    def one_pair(slot, carry):
        a = jnp.int32(0)
        for row in range(1, tiles - 1):
            a = a + (slot >= first_slot(row, tiles)).astype(jnp.int32)
        b = slot - first_slot(a, tiles) + a + 1
        pl.when(class_ref[a, b] < reach_tiles)(lambda: action(slot, a, b))
        return carry

    lax.fori_loop(0, off_diagonal(tiles), one_pair, 0)


def block_at(a, block_len):
    return pl.ds(pl.multiple_of(a * block_len, LANES), block_len)


def make_part(target, left_turned, right, left_column, right_pos):
    product = jnp.dot(left_turned, right, preferred_element_type=jnp.float32)
    left_pos = jnp.concatenate([left_column] * (right_pos.shape[1] // LANES), axis=1)
    distance = left_pos - right_pos
    target[...] = product * jnp.exp2(distance * distance * exp2_rate)


def turn_kernel(mate_ref, turned_ref):
    turned_ref[...] = mate_ref[...].T


def strips_kernel(
    reach_tiles, class_hbm, pos_ref, own_ref, mate_ref, turned_mate_ref, row_strips, column_strips, class_ref, both,
    turned, column, arrived,
):
    members, total_obs = own_ref.shape
    tiles = class_ref.shape[0]
    block_len = total_obs // tiles
    class_copy = pltpu.make_async_copy(class_hbm, class_ref, arrived)
    class_copy.start()
    both[:members, :] = own_ref[...]
    both[members:, :] = mate_ref[...]
    turned[:, :members] = own_ref[...].T
    turned[:, members:] = turned_mate_ref[...]
    spread_columns(pos_ref[...], column)
    _, within, _ = place()

    def chunk_of(a):
        return pl.ds(pl.multiple_of(a * block_len + within * LANES, LANES), LANES)

    def row_strip(target, a, b):
        at, columns_at = chunk_of(a), block_at(b, block_len)
        make_part(target, turned[at, :], both[:, columns_at], column[at, :], pos_ref[:, columns_at])

    def make_pair(slot, a, b):
        row_strip(row_strips.at[slot + tiles], a, b)
        at, columns_at = block_at(a, block_len), chunk_of(b)
        make_part(column_strips.at[slot], turned[at, :], both[:, columns_at], column[at, :], pos_ref[:, columns_at])

    for slot in range(tiles):
        row_strip(row_strips.at[slot], slot, slot)
    class_copy.wait()
    for_each_pair(reach_tiles, class_ref, make_pair)


def share_kernel(reach_tiles, class_ref, pos_ref, both, turned, column, row_strips, share_ref):
    tiles = class_ref.shape[0]
    block_len = share_ref.shape[1]
    _, within, per_row = place()

    def make_tile(slot, a, b):
        tile, columns_at = share_ref.at[slot], block_at(b, block_len)
        right, right_pos = both[:, columns_at], pos_ref[:, columns_at]
        here = pl.ds(pl.multiple_of(within * LANES, LANES), LANES)
        tile[here, :] = row_strips[slot]
        for turn in range(1, per_row):
            begin = lax.rem(within + turn, per_row) * LANES
            here = pl.ds(pl.multiple_of(begin, LANES), LANES)
            at = pl.ds(pl.multiple_of(a * block_len + begin, LANES), LANES)
            make_part(tile.at[here, :], turned[at, :], right, column[at, :], right_pos)

    def make_diagonal(slot, carry):
        make_tile(slot, slot, slot)
        return carry

    lax.fori_loop(0, tiles, make_diagonal, 0)
    for_each_pair(reach_tiles, class_ref, lambda slot, a, b: make_tile(slot + tiles, a, b))


def spread_columns(row, column):
    for begin in range(0, column.shape[0], LANES):
        square = jnp.broadcast_to(row[:, begin : begin + LANES], (LANES, LANES))
        column[begin : begin + LANES, :] = square.T


def spread_vector(vector, column):
    for piece in range(vector.shape[0]):
        square = jnp.broadcast_to(vector[piece : piece + 1, :], (LANES, LANES))
        column[piece * LANES : (piece + 1) * LANES, :] = square.T


def tile_weight(klass, reach_tiles, inverse_members):
    return jnp.maximum(0.0, 1.0 - klass.astype(jnp.float32) / reach_tiles) * inverse_members


def add_sums(into, weight, totals):
    for lane, total in enumerate(totals):
        into[:, lane * LANES : (lane + 1) * LANES] += weight * total


def add_turned(into, weight, across):
    for lane in range(across.shape[0] // LANES):
        where = slice(lane * LANES, (lane + 1) * LANES)
        turned = across[where, :].T
        folded = turned[:8, :]
        for begin in range(8, LANES, 8):
            folded = folded + turned[begin : begin + 8, :]
        into[:, where] += weight * folded


def fold_sums(sums, out_ref):
    for piece in range(sums.shape[1] // LANES):
        out_ref[piece : piece + 1, :] = jnp.sum(sums[:, piece * LANES : (piece + 1) * LANES], axis=0, keepdims=True)


def apply_share(reach_tiles, inverse_members, class_ref, share_ref, vector, column, across, sums, out_ref):
    tiles = class_ref.shape[0]
    block_len = share_ref.shape[1]
    lanes = block_len // LANES
    sums[...] = jnp.zeros_like(sums)

    def add_diagonal(a, carry):
        at = block_at(a, block_len)
        tile, factor = share_ref.at[a], column.at[at, :]
        totals = [None] * lanes
        for begin in range(0, block_len, 8):
            part = slice(begin, begin + 8)
            for lane in range(lanes):
                term = tile[part, lane * LANES : (lane + 1) * LANES] * factor[part, :]
                totals[lane] = term if totals[lane] is None else totals[lane] + term
        add_sums(sums.at[:, at], tile_weight(class_ref[a, a], reach_tiles, inverse_members), totals)
        return carry

    def add_pair(slot, a, b):
        weight = tile_weight(class_ref[a, b], reach_tiles, inverse_members)
        at_a, at_b = block_at(a, block_len), block_at(b, block_len)
        tile, factor = share_ref.at[slot + tiles], column.at[at_a, :]
        rows_b = [jnp.broadcast_to(vector[pl.ds(b * lanes + lane, 1), :], (8, LANES)) for lane in range(lanes)]
        totals = [None] * lanes
        for begin in range(0, block_len, 8):
            part = slice(begin, begin + 8)
            line = None
            for lane in range(lanes):
                here = tile[part, lane * LANES : (lane + 1) * LANES]
                term = here * factor[part, :]
                totals[lane] = term if totals[lane] is None else totals[lane] + term
                term = here * rows_b[lane]
                line = term if line is None else line + term
            across[part, :] = line
        add_sums(sums.at[:, at_b], weight, totals)
        add_turned(sums.at[:, at_a], weight, across)

    lax.fori_loop(0, tiles, add_diagonal, 0)
    for_each_pair(reach_tiles, class_ref, add_pair)
    fold_sums(sums, out_ref)


def place():
    sub_count = lax.axis_size("sub")
    within = lax.axis_index("col") * sub_count + lax.axis_index("sub")
    return lax.axis_index("row"), within, lax.axis_size("col") * sub_count


def first_kernel(reach_tiles, inverse_members, masks, class_ref, row_strips, column_strips, error_ref, *refs):
    tiles = class_ref.shape[0]
    chunks, refs = refs[:tiles], refs[tiles:]
    out_ref, vector, column, across, sums = refs
    row_index, within, per_row = place()
    block_len = row_strips.shape[2]
    lanes = block_len // LANES
    pieces = tiles * lanes
    for mask, chunk in zip(masks, chunks):
        vector[pl.ds(row_index ^ mask, 1), :] = chunk[...]
    spread_vector(vector, column)
    sums[...] = jnp.zeros_like(sums)

    def sums_of_rows(strip, a):
        factor = column.at[pl.ds(pl.multiple_of(a * LANES, LANES), LANES), :]
        totals = [None] * lanes
        for begin in range(0, LANES, 8):
            part = slice(begin, begin + 8)
            for lane in range(lanes):
                term = strip[part, lane * LANES : (lane + 1) * LANES] * factor[part, :]
                totals[lane] = term if totals[lane] is None else totals[lane] + term
        return totals

    def add_pair(slot, a, b):
        weight = tile_weight(class_ref[a, b], reach_tiles, inverse_members)
        add_sums(sums.at[:, block_at(b, block_len)], weight, sums_of_rows(row_strips.at[slot + tiles], a))
        across[...] = column_strips[slot] * vector[pl.ds(b, 1), :]
        add_turned(sums.at[:, block_at(a, block_len)], weight, across)

    for a in range(tiles):
        weight = tile_weight(class_ref[a, a], reach_tiles, inverse_members)
        add_sums(sums.at[:, a * block_len : (a + 1) * block_len], weight, sums_of_rows(row_strips.at[a], a))
    for_each_pair(reach_tiles, class_ref, add_pair)
    fold_sums(sums, out_ref)
    own = row_index * per_row + within
    out_ref[pl.ds(own, 1), :] += error_ref[...] * chunks[0][...]
    out_ref[pieces : pieces + tiles, :] = vector[...]
    out_ref[pieces + tiles : pieces + tiles + 1, :] = error_ref[...]


def middle_kernel(pieces, *refs):
    parts, out_ref = refs[:-1], refs[-1]
    total = parts[0][:pieces, :]
    for part in parts[1:]:
        total = total + part[:pieces, :]
    out_ref[...] = total


def gather_kernel(tiles, masks, *refs):
    parts, (innovations_ref, error_ref) = refs[:-2], refs[-2:]
    _, within, per_row = place()
    pieces = innovations_ref.shape[0]
    for mask, part in zip(masks, parts):
        there = within ^ mask
        for a in range(tiles):
            innovations_ref[pl.ds(a * per_row + there, 1), :] = part[pieces + a : pieces + a + 1, :]
        error_ref[pl.ds(there, 1), :] = part[pieces + tiles : pieces + tiles + 1, :]


def total_of(x):
    return jnp.sum(jnp.sum(x, axis=0, keepdims=True), axis=1, keepdims=True)


def second_kernel(reach_tiles, inverse_members, peers, class_ref, share_ref, innovations_ref, error_ref, *refs):
    parts, refs = refs[:peers], refs[peers:]
    sent, refs = refs[:peers], refs[peers:]
    state_ref, direction, residual, start, column, across, sums, product = refs
    row_index, within, per_row = place()
    innovations = innovations_ref[...]
    image = parts[0][...]
    for part in parts[1:]:
        image = image + part[...]
    norm_now = total_of(innovations * innovations)
    alpha = norm_now / total_of(innovations * image)
    residual_now = innovations - alpha * image
    norm_next = total_of(residual_now * residual_now)
    direction_now = residual_now + (norm_next / norm_now) * innovations
    residual[...] = residual_now
    direction[...] = direction_now
    start[...] = alpha * innovations
    spread_vector(direction, column)
    shared = (class_ref, share_ref, direction, column, across, sums, product)
    apply_share(reach_tiles, inverse_members, *shared)
    of_row = direction[pl.ds(row_index * per_row, per_row), :]
    curvature = total_of(direction_now * product[...]) + total_of(error_ref[...] * of_row * of_row)
    for peer in range(peers):
        at = (row_index ^ peer) * per_row + within
        sent[peer][0:1, :] = product[pl.ds(at, 1), :]
        sent[peer][1:2, :] = jnp.broadcast_to(curvature, (1, LANES))
    own = pl.ds(row_index * per_row + within, 1)
    state_ref[0:1, :] = start[own, :]
    state_ref[1:2, :] = residual[own, :]
    state_ref[2:3, :] = direction[own, :]
    state_ref[3:4, :] = error_ref[pl.ds(within, 1), :] * direction[own, :]
    state_ref[4:5, :] = jnp.broadcast_to(norm_next, (1, LANES))


def last_kernel(state_ref, *refs):
    parts, (solution_ref, residual_ref) = refs[:-2], refs[-2:]
    image = state_ref[3:4, :] + parts[0][0:1, :]
    curvature = parts[0][1:2, :]
    for part in parts[1:]:
        image = image + part[0:1, :]
        curvature = curvature + part[1:2, :]
    alpha = state_ref[4:5, :] / curvature
    solution_ref[...] = state_ref[0:1, :] + alpha * state_ref[2:3, :]
    residual_ref[...] = state_ref[1:2, :] - alpha * image


VMEM_SPEC = pl.BlockSpec(memory_space=pltpu.VMEM)
SMEM_SPEC = pl.BlockSpec(memory_space=pltpu.SMEM)
HBM_SPEC = pl.BlockSpec(memory_space=pltpu.HBM)


def in_hbm(x):
    return pltpu.with_memory_space_constraint(x, pltpu.HBM)


def exchange(axes, masks, values):
    count = math.prod(lax.axis_size(axis) for axis in axes)
    return [
        lax.ppermute(value, axes, [(i, i ^ mask) for i in range(count)]) if mask else value
        for mask, value in zip(masks, values)
    ]


def nearest_first(count):
    return tuple(range(count))


def farthest_first(count):
    return (0,) + tuple(range(count - 1, 0, -1))


def vectors_only(anomalies, innovations, obs_error, track_pos, taper_class):
    row_count = lax.axis_size("row")
    sub_count = lax.axis_size("sub")
    per_row = lax.axis_size("col") * sub_count
    local_members, total_obs = anomalies.shape
    member_total = local_members * row_count * sub_count
    inverse_members = 1.0 / (member_total - 1)
    reach_tiles = max(2, row_count // 4)
    pieces = total_obs // LANES
    block_len = total_obs // row_count
    f32 = jnp.float32
    row, here = ("row",), ("col", "sub")
    params = pltpu.CompilerParams(vmem_limit_bytes=16 * 1024 * 1024)

    mate = lax.ppermute(anomalies, "sub", [(0, 1), (1, 0)])
    chunk = innovations.reshape(1, LANES)
    error = obs_error.reshape(1, LANES)
    chunk_order = nearest_first(row_count)
    chunks = exchange(row, chunk_order, [chunk] * row_count)

    work = [pltpu.VMEM((block_len, LANES), f32), pltpu.VMEM((8, total_obs), f32)]
    pairs = off_diagonal(row_count)
    part_elements = (row_count + pairs) * block_len * block_len
    mate_bytes = anomalies.size * anomalies.dtype.itemsize
    turned_mate = pl.pallas_call(
        turn_kernel,
        out_shape=pltpu.VMEM((total_obs, local_members), anomalies.dtype),
        in_specs=[VMEM_SPEC],
        out_specs=VMEM_SPEC,
        compiler_params=params,
        cost_estimate=pl.CostEstimate(flops=4 * local_members * total_obs * total_obs, bytes_accessed=16 * mate_bytes, transcendentals=0),
        name="turn",
    )(mate)
    positions = track_pos.reshape(1, total_obs)
    strips, strip_columns, classes, both, turned, column = pl.pallas_call(
        functools.partial(strips_kernel, reach_tiles),
        out_shape=[
            pltpu.VMEM((row_count + pairs, LANES, block_len), f32),
            pltpu.VMEM((pairs, block_len, LANES), f32),
            pltpu.SMEM(taper_class.shape, jnp.int32),
            pltpu.VMEM((2 * local_members, total_obs), anomalies.dtype),
            pltpu.VMEM((total_obs, 2 * local_members), anomalies.dtype),
            pltpu.VMEM((total_obs, LANES), f32),
        ],
        in_specs=[HBM_SPEC] + [VMEM_SPEC] * 4,
        out_specs=[VMEM_SPEC] * 2 + [SMEM_SPEC] + [VMEM_SPEC] * 3,
        scratch_shapes=[pltpu.SemaphoreType.DMA(())],
        compiler_params=params,
        cost_estimate=pl.CostEstimate(
            flops=2 * local_members * part_elements,
            bytes_accessed=2 * part_elements,
            transcendentals=part_elements // 2,
        ),
        name="strips",
    )(in_hbm(taper_class), positions, anomalies, mate, turned_mate)

    payload = pl.pallas_call(
        functools.partial(first_kernel, reach_tiles, inverse_members, chunk_order),
        out_shape=pltpu.VMEM((pieces + 8, LANES), f32),
        in_specs=[SMEM_SPEC] + [VMEM_SPEC] * (row_count + 3),
        out_specs=VMEM_SPEC,
        scratch_shapes=[pltpu.VMEM((row_count, LANES), f32), pltpu.VMEM((row_count * LANES, LANES), f32)]
        + work,
        compiler_params=params,
        name="first",
    )(classes, strips, strip_columns, error, *chunks)
    payload_order = nearest_first(per_row)
    payloads = exchange(here, payload_order, [payload] * per_row)
    part = pl.pallas_call(
        functools.partial(middle_kernel, pieces),
        out_shape=pltpu.VMEM((pieces, LANES), f32),
        in_specs=[VMEM_SPEC] * per_row,
        out_specs=VMEM_SPEC,
        compiler_params=params,
        name="middle",
    )(*payloads)
    parts = exchange(row, nearest_first(row_count), [part] * row_count)
    whole, error = pl.pallas_call(
        functools.partial(gather_kernel, row_count, payload_order),
        out_shape=[pltpu.VMEM((pieces, LANES), f32), pltpu.VMEM((per_row, LANES), f32)],
        in_specs=[VMEM_SPEC] * per_row,
        out_specs=[VMEM_SPEC] * 2,
        compiler_params=params,
        name="gather",
    )(*payloads)

    share = pl.pallas_call(
        functools.partial(share_kernel, reach_tiles),
        out_shape=pltpu.VMEM((row_count + pairs, block_len, block_len), f32),
        in_specs=[SMEM_SPEC] + [VMEM_SPEC] * 5,
        out_specs=VMEM_SPEC,
        compiler_params=params,
        cost_estimate=pl.CostEstimate(
            flops=4 * local_members * part_elements,
            bytes_accessed=4 * part_elements,
            transcendentals=part_elements,
        ),
        name="share",
    )(classes, positions, both, turned, column, strips)
    *sent, state = pl.pallas_call(
        functools.partial(second_kernel, reach_tiles, inverse_members, row_count),
        out_shape=[pltpu.VMEM((8, LANES), f32) for _ in range(row_count + 1)],
        in_specs=[SMEM_SPEC] + [VMEM_SPEC] * (row_count + 3),
        out_specs=[VMEM_SPEC] * (row_count + 1),
        scratch_shapes=[pltpu.VMEM((pieces, LANES), f32)] * 3
        + [pltpu.VMEM((total_obs, LANES), f32)]
        + work
        + [pltpu.VMEM((pieces, LANES), f32)],
        compiler_params=params,
        name="second",
    )(classes, share, whole, error, *parts)
    last_order = farthest_first(row_count)
    got = exchange(row, last_order, [sent[mask] for mask in last_order])
    solution_part, residual_part = pl.pallas_call(
        last_kernel,
        out_shape=[jax.ShapeDtypeStruct((1, LANES), f32)] * 2,
        in_specs=[VMEM_SPEC] * (row_count + 1),
        out_specs=[VMEM_SPEC] * 2,
        compiler_params=pltpu.CompilerParams(vmem_limit_bytes=1024 * 1024),
        name="last",
    )(state, *got)
    return solution_part.reshape(LANES), residual_part.reshape(LANES)


def fits(anomalies, innovations, obs_error, track_pos, taper_class):
    row_count = lax.axis_size("row")
    per_row = lax.axis_size("col") * lax.axis_size("sub")
    local_members, total_obs = anomalies.shape
    block_len = total_obs // row_count
    share_bytes = 4 * (row_count + off_diagonal(row_count)) * block_len * block_len
    return (
        ITERS == 2
        and row_count in (2, 4)
        and per_row in (2, 4)
        and lax.axis_size("sub") == 2
        and innovations.shape[0] == LANES
        and total_obs == row_count * per_row * LANES
        and local_members % LANES == 0
        and share_bytes <= 16 * 1024 * 1024
    )


def per_device(*args):
    return vectors_only(*args) if fits(*args) else blocks(*args)


def squares(residual):
    return lax.psum(jnp.sum(residual * residual), ("row", "col", "sub"))


def blocks(anomalies, innovations, obs_error, track_pos, taper_class):
    row_count = lax.axis_size("row")
    col_count = lax.axis_size("col")
    sub_count = lax.axis_size("sub")
    row_index = lax.axis_index("row")
    col_index = lax.axis_index("col")
    local_members, total_obs = anomalies.shape
    block_len = total_obs // row_count
    quarter_len = block_len // col_count
    member_total = local_members * row_count * sub_count
    inverse_members = 1.0 / (member_total - 1)
    reach_tiles = max(2, row_count // 4)
    class_row = lax.dynamic_index_in_dim(taper_class, row_index, 0, keepdims=False)
    tile_weight = jnp.maximum(0.0, 1.0 - class_row.astype(jnp.float32) / reach_tiles)
    row_pos = lax.dynamic_slice_in_dim(track_pos, row_index * block_len, block_len, 0)
    col_pos = lax.dynamic_index_in_dim(
        track_pos.reshape(row_count, col_count, quarter_len), col_index, 1, keepdims=False
    )
    own_block = lax.all_to_all(anomalies, "row", split_axis=1, concat_axis=0, tiled=True)
    own_quarter = lax.dynamic_slice_in_dim(own_block, col_index * quarter_len, quarter_len, 1)

    def one_tile(piece, block_index, keep_factor):
        product = jnp.einsum("mi,mq->iq", own_block, piece, preferred_element_type=jnp.float32)
        column_pos = lax.dynamic_index_in_dim(col_pos, block_index, 0, keepdims=False)
        weight_here = lax.dynamic_index_in_dim(tile_weight, block_index, 0, keepdims=False)
        distance = row_pos[:, None] - column_pos[None, :]
        taper = weight_here * keep_factor * jnp.exp(-(distance * distance) / track_width)
        return product * (taper * inverse_members)

    def one_entry(entry):
        return one_tile(entry[0], entry[1], 1.0)

    piece = lax.all_gather(own_quarter[None], "row", axis=0, tiled=True)
    indices = jnp.arange(piece.shape[0], dtype=jnp.int32)
    tiles = lax.map(one_entry, (piece, indices))
    solution = jnp.zeros_like(innovations)
    residual = innovations
    direction_vec = innovations
    norm_now = squares(residual)
    for turn_index in range(ITERS):
        column_vec = lax.all_gather(direction_vec, ("row", "sub"), axis=0, tiled=True).reshape(
            row_count, quarter_len
        )
        direct = jnp.einsum("jiq,jq->i", tiles, column_vec, precision=lax.Precision.HIGHEST)
        extra = obs_error * direction_vec
        own_part = lax.psum_scatter(direct, ("col", "sub"), scatter_dimension=0, tiled=True)
        image = own_part + extra
        alpha = norm_now / lax.psum(jnp.sum(direction_vec * image), ("row", "col", "sub"))
        solution = solution + alpha * direction_vec
        residual = residual - alpha * image
        if turn_index + 1 < ITERS:
            norm_next = squares(residual)
            direction_vec = residual + norm_next / norm_now * direction_vec
            norm_now = norm_next
    return (solution, residual)


def solution(mesh):
    in_specs = (
        P(("group", "row", "sub"), None),
        P(("group", "row", "col", "sub")),
        P(("group", "row", "col", "sub")),
        P("group"),
        P("group", None),
    )
    out_specs = (P(("group", "row", "col", "sub")), P(("group", "row", "col", "sub")))
    return jax.shard_map(
        per_device, mesh=mesh, in_specs=in_specs, out_specs=out_specs, check_vma=False
    )
```

```python
import functools
import math

import jax
import jax.numpy as jnp
from jax import lax
from jax.experimental import pallas as pl
from jax.experimental.pallas import tpu as pltpu
from jax.sharding import PartitionSpec as P

ITERS = 2
LANES = 128


track_width = 0.0001
exp2_rate = -math.log2(math.e) / track_width


def off_diagonal(tiles):
    return tiles * (tiles - 1) // 2


def first_slot(a, tiles):
    return a * tiles - (a * (a + 1)) // 2


def for_each_pair(reach_tiles, class_ref, action):
    tiles = class_ref.shape[0]

    def one_pair(slot, carry):
        a = jnp.int32(0)
        for row in range(1, tiles - 1):
            a = a + (slot >= first_slot(row, tiles)).astype(jnp.int32)
        b = slot - first_slot(a, tiles) + a + 1
        pl.when(class_ref[a, b] < reach_tiles)(lambda: action(slot, a, b))
        return carry

    lax.fori_loop(0, off_diagonal(tiles), one_pair, 0)


def each_pair(reach_tiles, class_ref, action):
    tiles = class_ref.shape[0]
    for a in range(tiles):
        for b in range(a + 1, tiles):
            slot = first_slot(a, tiles) + b - a - 1
            pl.when(class_ref[a, b] < reach_tiles)(functools.partial(action, slot, a, b))


def block_at(a, block_len):
    return pl.ds(pl.multiple_of(a * block_len, LANES), block_len)


def make_part(target, left_turned, right, left_column, right_pos):
    product = jnp.dot(left_turned, right, preferred_element_type=jnp.float32)
    left_pos = jnp.concatenate([left_column] * (right_pos.shape[1] // LANES), axis=1)
    distance = left_pos - right_pos
    target[...] = product * jnp.exp2(distance * distance * exp2_rate)


def turn_kernel(mate_ref, turned_ref):
    turned_ref[...] = mate_ref[...].T


def strips_kernel(
    reach_tiles, class_hbm, pos_ref, own_ref, mate_ref, turned_mate_ref, row_strips, column_strips, class_ref, both,
    turned, column, arrived,
):
    members, total_obs = own_ref.shape
    tiles = class_ref.shape[0]
    block_len = total_obs // tiles
    class_copy = pltpu.make_async_copy(class_hbm, class_ref, arrived)
    class_copy.start()
    both[:members, :] = own_ref[...]
    both[members:, :] = mate_ref[...]
    turned[:, :members] = own_ref[...].T
    turned[:, members:] = turned_mate_ref[...]
    spread_columns(pos_ref[...], column)
    _, within, _ = place()

    def chunk_of(a):
        return pl.ds(pl.multiple_of(a * block_len + within * LANES, LANES), LANES)

    def row_strip(target, a, b):
        at, columns_at = chunk_of(a), block_at(b, block_len)
        make_part(target, turned[at, :], both[:, columns_at], column[at, :], pos_ref[:, columns_at])

    def make_pair(slot, a, b):
        row_strip(row_strips.at[slot + tiles], a, b)
        at, columns_at = block_at(a, block_len), chunk_of(b)
        make_part(column_strips.at[slot], turned[at, :], both[:, columns_at], column[at, :], pos_ref[:, columns_at])

    for slot in range(tiles):
        row_strip(row_strips.at[slot], slot, slot)
    class_copy.wait()
    each_pair(reach_tiles, class_ref, make_pair)


def share_kernel(reach_tiles, class_ref, pos_ref, both, turned, column, row_strips, share_ref):
    tiles = class_ref.shape[0]
    block_len = share_ref.shape[1]
    _, within, per_row = place()

    def make_tile(slot, a, b):
        tile, columns_at = share_ref.at[slot], block_at(b, block_len)
        right, right_pos = both[:, columns_at], pos_ref[:, columns_at]
        here = pl.ds(pl.multiple_of(within * LANES, LANES), LANES)
        tile[here, :] = row_strips[slot]
        for turn in range(1, per_row):
            begin = lax.rem(within + turn, per_row) * LANES
            here = pl.ds(pl.multiple_of(begin, LANES), LANES)
            at = pl.ds(pl.multiple_of(a * block_len + begin, LANES), LANES)
            make_part(tile.at[here, :], turned[at, :], right, column[at, :], right_pos)

    for slot in range(tiles):
        make_tile(slot, slot, slot)
    each_pair(reach_tiles, class_ref, lambda slot, a, b: make_tile(slot + tiles, a, b))


def spread_columns(row, column):
    for begin in range(0, column.shape[0], LANES):
        square = jnp.broadcast_to(row[:, begin : begin + LANES], (LANES, LANES))
        column[begin : begin + LANES, :] = square.T


def spread_vector(vector, column):
    for piece in range(vector.shape[0]):
        square = jnp.broadcast_to(vector[piece : piece + 1, :], (LANES, LANES))
        column[piece * LANES : (piece + 1) * LANES, :] = square.T


def tile_weight(klass, reach_tiles, inverse_members):
    return jnp.maximum(0.0, 1.0 - klass.astype(jnp.float32) / reach_tiles) * inverse_members


def add_sums(into, weight, totals):
    for lane, total in enumerate(totals):
        into[:, lane * LANES : (lane + 1) * LANES] += weight * total


def add_turned(into, weight, across):
    for lane in range(across.shape[0] // LANES):
        where = slice(lane * LANES, (lane + 1) * LANES)
        turned = across[where, :].T
        folded = turned[:8, :]
        for begin in range(8, LANES, 8):
            folded = folded + turned[begin : begin + 8, :]
        into[:, where] += weight * folded


def fold_sums(sums, out_ref):
    for piece in range(sums.shape[1] // LANES):
        out_ref[piece : piece + 1, :] = jnp.sum(sums[:, piece * LANES : (piece + 1) * LANES], axis=0, keepdims=True)


def apply_share(reach_tiles, inverse_members, class_ref, share_ref, vector, column, across, sums, out_ref):
    tiles = class_ref.shape[0]
    block_len = share_ref.shape[1]
    lanes = block_len // LANES
    sums[...] = jnp.zeros_like(sums)

    def add_diagonal(a):
        at = block_at(a, block_len)
        tile, factor = share_ref.at[a], column.at[at, :]
        totals = [None] * lanes
        for begin in range(0, block_len, 8):
            part = slice(begin, begin + 8)
            for lane in range(lanes):
                term = tile[part, lane * LANES : (lane + 1) * LANES] * factor[part, :]
                totals[lane] = term if totals[lane] is None else totals[lane] + term
        add_sums(sums.at[:, at], tile_weight(class_ref[a, a], reach_tiles, inverse_members), totals)

    def add_pair(slot, a, b):
        weight = tile_weight(class_ref[a, b], reach_tiles, inverse_members)
        at_a, at_b = block_at(a, block_len), block_at(b, block_len)
        tile, factor = share_ref.at[slot + tiles], column.at[at_a, :]
        rows_b = [jnp.broadcast_to(vector[pl.ds(b * lanes + lane, 1), :], (8, LANES)) for lane in range(lanes)]
        totals = [None] * lanes
        for begin in range(0, block_len, 8):
            part = slice(begin, begin + 8)
            line = None
            for lane in range(lanes):
                here = tile[part, lane * LANES : (lane + 1) * LANES]
                term = here * factor[part, :]
                totals[lane] = term if totals[lane] is None else totals[lane] + term
                term = here * rows_b[lane]
                line = term if line is None else line + term
            across[part, :] = line
        add_sums(sums.at[:, at_b], weight, totals)
        add_turned(sums.at[:, at_a], weight, across)

    for a in range(tiles):
        add_diagonal(a)
    each_pair(reach_tiles, class_ref, add_pair)
    fold_sums(sums, out_ref)


def place():
    sub_count = lax.axis_size("sub")
    within = lax.axis_index("col") * sub_count + lax.axis_index("sub")
    return lax.axis_index("row"), within, lax.axis_size("col") * sub_count


def first_kernel(reach_tiles, inverse_members, masks, class_ref, row_strips, column_strips, error_ref, *refs):
    tiles = class_ref.shape[0]
    chunks, refs = refs[:tiles], refs[tiles:]
    out_ref, vector, column, across, sums = refs
    row_index, within, per_row = place()
    block_len = row_strips.shape[2]
    lanes = block_len // LANES
    pieces = tiles * lanes
    for mask, chunk in zip(masks, chunks):
        vector[pl.ds(row_index ^ mask, 1), :] = chunk[...]
    spread_vector(vector, column)
    sums[...] = jnp.zeros_like(sums)

    def sums_of_rows(strip, a):
        factor = column.at[pl.ds(pl.multiple_of(a * LANES, LANES), LANES), :]
        totals = [None] * lanes
        for begin in range(0, LANES, 8):
            part = slice(begin, begin + 8)
            for lane in range(lanes):
                term = strip[part, lane * LANES : (lane + 1) * LANES] * factor[part, :]
                totals[lane] = term if totals[lane] is None else totals[lane] + term
        return totals

    def add_pair(slot, a, b):
        weight = tile_weight(class_ref[a, b], reach_tiles, inverse_members)
        add_sums(sums.at[:, block_at(b, block_len)], weight, sums_of_rows(row_strips.at[slot + tiles], a))
        across[...] = column_strips[slot] * vector[pl.ds(b, 1), :]
        add_turned(sums.at[:, block_at(a, block_len)], weight, across)

    for a in range(tiles):
        weight = tile_weight(class_ref[a, a], reach_tiles, inverse_members)
        add_sums(sums.at[:, a * block_len : (a + 1) * block_len], weight, sums_of_rows(row_strips.at[a], a))
    each_pair(reach_tiles, class_ref, add_pair)
    fold_sums(sums, out_ref)
    own = row_index * per_row + within
    out_ref[pl.ds(own, 1), :] += error_ref[...] * chunks[0][...]
    out_ref[pieces : pieces + tiles, :] = vector[...]
    out_ref[pieces + tiles : pieces + tiles + 1, :] = error_ref[...]


def middle_kernel(pieces, *refs):
    parts, out_ref = refs[:-1], refs[-1]
    total = parts[0][:pieces, :]
    for part in parts[1:]:
        total = total + part[:pieces, :]
    out_ref[...] = total


def gather_kernel(tiles, masks, *refs):
    parts, (innovations_ref, error_ref) = refs[:-2], refs[-2:]
    _, within, per_row = place()
    pieces = innovations_ref.shape[0]
    for mask, part in zip(masks, parts):
        there = within ^ mask
        for a in range(tiles):
            innovations_ref[pl.ds(a * per_row + there, 1), :] = part[pieces + a : pieces + a + 1, :]
        error_ref[pl.ds(there, 1), :] = part[pieces + tiles : pieces + tiles + 1, :]


def total_of(x):
    return jnp.sum(jnp.sum(x, axis=0, keepdims=True), axis=1, keepdims=True)


def second_kernel(reach_tiles, inverse_members, peers, class_ref, share_ref, innovations_ref, error_ref, *refs):
    parts, refs = refs[:peers], refs[peers:]
    sent, refs = refs[:peers], refs[peers:]
    state_ref, direction, residual, start, column, across, sums, product = refs
    row_index, within, per_row = place()
    innovations = innovations_ref[...]
    image = parts[0][...]
    for part in parts[1:]:
        image = image + part[...]
    norm_now = total_of(innovations * innovations)
    alpha = norm_now / total_of(innovations * image)
    residual_now = innovations - alpha * image
    norm_next = total_of(residual_now * residual_now)
    direction_now = residual_now + (norm_next / norm_now) * innovations
    residual[...] = residual_now
    direction[...] = direction_now
    start[...] = alpha * innovations
    spread_vector(direction, column)
    shared = (class_ref, share_ref, direction, column, across, sums, product)
    apply_share(reach_tiles, inverse_members, *shared)
    of_row = direction[pl.ds(row_index * per_row, per_row), :]
    curvature = total_of(direction_now * product[...]) + total_of(error_ref[...] * of_row * of_row)
    for peer in range(peers):
        at = (row_index ^ peer) * per_row + within
        sent[peer][0:1, :] = product[pl.ds(at, 1), :]
        sent[peer][1:2, :] = jnp.broadcast_to(curvature, (1, LANES))
    own = pl.ds(row_index * per_row + within, 1)
    state_ref[0:1, :] = start[own, :]
    state_ref[1:2, :] = residual[own, :]
    state_ref[2:3, :] = direction[own, :]
    state_ref[3:4, :] = error_ref[pl.ds(within, 1), :] * direction[own, :]
    state_ref[4:5, :] = jnp.broadcast_to(norm_next, (1, LANES))


def last_kernel(state_ref, *refs):
    parts, (solution_ref, residual_ref) = refs[:-2], refs[-2:]
    image = state_ref[3:4, :] + parts[0][0:1, :]
    curvature = parts[0][1:2, :]
    for part in parts[1:]:
        image = image + part[0:1, :]
        curvature = curvature + part[1:2, :]
    alpha = state_ref[4:5, :] / curvature
    solution_ref[...] = state_ref[0:1, :] + alpha * state_ref[2:3, :]
    residual_ref[...] = state_ref[1:2, :] - alpha * image


VMEM_SPEC = pl.BlockSpec(memory_space=pltpu.VMEM)
SMEM_SPEC = pl.BlockSpec(memory_space=pltpu.SMEM)
HBM_SPEC = pl.BlockSpec(memory_space=pltpu.HBM)


def in_hbm(x):
    return pltpu.with_memory_space_constraint(x, pltpu.HBM)


def exchange(axes, masks, values):
    count = math.prod(lax.axis_size(axis) for axis in axes)
    return [
        lax.ppermute(value, axes, [(i, i ^ mask) for i in range(count)]) if mask else value
        for mask, value in zip(masks, values)
    ]


def nearest_first(count):
    return tuple(range(count))


def farthest_first(count):
    return (0,) + tuple(range(count - 1, 0, -1))


def vectors_only(anomalies, innovations, obs_error, track_pos, taper_class):
    row_count = lax.axis_size("row")
    sub_count = lax.axis_size("sub")
    per_row = lax.axis_size("col") * sub_count
    local_members, total_obs = anomalies.shape
    member_total = local_members * row_count * sub_count
    inverse_members = 1.0 / (member_total - 1)
    reach_tiles = max(2, row_count // 4)
    pieces = total_obs // LANES
    block_len = total_obs // row_count
    f32 = jnp.float32
    row, here = ("row",), ("col", "sub")
    params = pltpu.CompilerParams(vmem_limit_bytes=16 * 1024 * 1024)

    mate = lax.ppermute(anomalies, "sub", [(0, 1), (1, 0)])
    chunk = innovations.reshape(1, LANES)
    error = obs_error.reshape(1, LANES)
    chunk_order = nearest_first(row_count)
    chunks = exchange(row, chunk_order, [chunk] * row_count)

    work = [pltpu.VMEM((block_len, LANES), f32), pltpu.VMEM((8, total_obs), f32)]
    pairs = off_diagonal(row_count)
    part_elements = (row_count + pairs) * block_len * block_len
    mate_bytes = anomalies.size * anomalies.dtype.itemsize
    turned_mate = pl.pallas_call(
        turn_kernel,
        out_shape=pltpu.VMEM((total_obs, local_members), anomalies.dtype),
        in_specs=[VMEM_SPEC],
        out_specs=VMEM_SPEC,
        compiler_params=params,
        cost_estimate=pl.CostEstimate(flops=4 * local_members * total_obs * total_obs, bytes_accessed=16 * mate_bytes, transcendentals=0),
        name="turn",
    )(mate)
    positions = track_pos.reshape(1, total_obs)
    strips, strip_columns, classes, both, turned, column = pl.pallas_call(
        functools.partial(strips_kernel, reach_tiles),
        out_shape=[
            pltpu.VMEM((row_count + pairs, LANES, block_len), f32),
            pltpu.VMEM((pairs, block_len, LANES), f32),
            pltpu.SMEM(taper_class.shape, jnp.int32),
            pltpu.VMEM((2 * local_members, total_obs), anomalies.dtype),
            pltpu.VMEM((total_obs, 2 * local_members), anomalies.dtype),
            pltpu.VMEM((total_obs, LANES), f32),
        ],
        in_specs=[HBM_SPEC] + [VMEM_SPEC] * 4,
        out_specs=[VMEM_SPEC] * 2 + [SMEM_SPEC] + [VMEM_SPEC] * 3,
        scratch_shapes=[pltpu.SemaphoreType.DMA(())],
        compiler_params=params,
        cost_estimate=pl.CostEstimate(
            flops=2 * local_members * part_elements,
            bytes_accessed=2 * part_elements,
            transcendentals=part_elements // 2,
        ),
        name="strips",
    )(in_hbm(taper_class), positions, anomalies, mate, turned_mate)

    payload = pl.pallas_call(
        functools.partial(first_kernel, reach_tiles, inverse_members, chunk_order),
        out_shape=pltpu.VMEM((pieces + 8, LANES), f32),
        in_specs=[SMEM_SPEC] + [VMEM_SPEC] * (row_count + 3),
        out_specs=VMEM_SPEC,
        scratch_shapes=[pltpu.VMEM((row_count, LANES), f32), pltpu.VMEM((row_count * LANES, LANES), f32)]
        + work,
        compiler_params=params,
        name="first",
    )(classes, strips, strip_columns, error, *chunks)
    payload_order = nearest_first(per_row)
    payloads = exchange(here, payload_order, [payload] * per_row)
    part = pl.pallas_call(
        functools.partial(middle_kernel, pieces),
        out_shape=pltpu.VMEM((pieces, LANES), f32),
        in_specs=[VMEM_SPEC] * per_row,
        out_specs=VMEM_SPEC,
        compiler_params=params,
        name="middle",
    )(*payloads)
    parts = exchange(row, nearest_first(row_count), [part] * row_count)
    whole, error = pl.pallas_call(
        functools.partial(gather_kernel, row_count, payload_order),
        out_shape=[pltpu.VMEM((pieces, LANES), f32), pltpu.VMEM((per_row, LANES), f32)],
        in_specs=[VMEM_SPEC] * per_row,
        out_specs=[VMEM_SPEC] * 2,
        compiler_params=params,
        name="gather",
    )(*payloads)

    share = pl.pallas_call(
        functools.partial(share_kernel, reach_tiles),
        out_shape=pltpu.VMEM((row_count + pairs, block_len, block_len), f32),
        in_specs=[SMEM_SPEC] + [VMEM_SPEC] * 5,
        out_specs=VMEM_SPEC,
        compiler_params=params,
        cost_estimate=pl.CostEstimate(
            flops=4 * local_members * part_elements,
            bytes_accessed=4 * part_elements,
            transcendentals=part_elements,
        ),
        name="share",
    )(classes, positions, both, turned, column, strips)
    *sent, state = pl.pallas_call(
        functools.partial(second_kernel, reach_tiles, inverse_members, row_count),
        out_shape=[pltpu.VMEM((8, LANES), f32) for _ in range(row_count + 1)],
        in_specs=[SMEM_SPEC] + [VMEM_SPEC] * (row_count + 3),
        out_specs=[VMEM_SPEC] * (row_count + 1),
        scratch_shapes=[pltpu.VMEM((pieces, LANES), f32)] * 3
        + [pltpu.VMEM((total_obs, LANES), f32)]
        + work
        + [pltpu.VMEM((pieces, LANES), f32)],
        compiler_params=params,
        name="second",
    )(classes, share, whole, error, *parts)
    last_order = farthest_first(row_count)
    got = exchange(row, last_order, [sent[mask] for mask in last_order])
    solution_part, residual_part = pl.pallas_call(
        last_kernel,
        out_shape=[jax.ShapeDtypeStruct((1, LANES), f32)] * 2,
        in_specs=[VMEM_SPEC] * (row_count + 1),
        out_specs=[VMEM_SPEC] * 2,
        compiler_params=pltpu.CompilerParams(vmem_limit_bytes=1024 * 1024),
        name="last",
    )(state, *got)
    return solution_part.reshape(LANES), residual_part.reshape(LANES)


def fits(anomalies, innovations, obs_error, track_pos, taper_class):
    row_count = lax.axis_size("row")
    per_row = lax.axis_size("col") * lax.axis_size("sub")
    local_members, total_obs = anomalies.shape
    block_len = total_obs // row_count
    share_bytes = 4 * (row_count + off_diagonal(row_count)) * block_len * block_len
    return (
        ITERS == 2
        and row_count in (2, 4)
        and per_row in (2, 4)
        and lax.axis_size("sub") == 2
        and innovations.shape[0] == LANES
        and total_obs == row_count * per_row * LANES
        and local_members % LANES == 0
        and share_bytes <= 16 * 1024 * 1024
    )


def per_device(*args):
    return vectors_only(*args) if fits(*args) else blocks(*args)


def squares(residual):
    return lax.psum(jnp.sum(residual * residual), ("row", "col", "sub"))


def blocks(anomalies, innovations, obs_error, track_pos, taper_class):
    row_count = lax.axis_size("row")
    col_count = lax.axis_size("col")
    sub_count = lax.axis_size("sub")
    row_index = lax.axis_index("row")
    col_index = lax.axis_index("col")
    local_members, total_obs = anomalies.shape
    block_len = total_obs // row_count
    quarter_len = block_len // col_count
    member_total = local_members * row_count * sub_count
    inverse_members = 1.0 / (member_total - 1)
    reach_tiles = max(2, row_count // 4)
    class_row = lax.dynamic_index_in_dim(taper_class, row_index, 0, keepdims=False)
    tile_weight = jnp.maximum(0.0, 1.0 - class_row.astype(jnp.float32) / reach_tiles)
    row_pos = lax.dynamic_slice_in_dim(track_pos, row_index * block_len, block_len, 0)
    col_pos = lax.dynamic_index_in_dim(
        track_pos.reshape(row_count, col_count, quarter_len), col_index, 1, keepdims=False
    )
    own_block = lax.all_to_all(anomalies, "row", split_axis=1, concat_axis=0, tiled=True)
    own_quarter = lax.dynamic_slice_in_dim(own_block, col_index * quarter_len, quarter_len, 1)

    def one_tile(piece, block_index, keep_factor):
        product = jnp.einsum("mi,mq->iq", own_block, piece, preferred_element_type=jnp.float32)
        column_pos = lax.dynamic_index_in_dim(col_pos, block_index, 0, keepdims=False)
        weight_here = lax.dynamic_index_in_dim(tile_weight, block_index, 0, keepdims=False)
        distance = row_pos[:, None] - column_pos[None, :]
        taper = weight_here * keep_factor * jnp.exp(-(distance * distance) / track_width)
        return product * (taper * inverse_members)

    def one_entry(entry):
        return one_tile(entry[0], entry[1], 1.0)

    piece = lax.all_gather(own_quarter[None], "row", axis=0, tiled=True)
    indices = jnp.arange(piece.shape[0], dtype=jnp.int32)
    tiles = lax.map(one_entry, (piece, indices))
    solution = jnp.zeros_like(innovations)
    residual = innovations
    direction_vec = innovations
    norm_now = squares(residual)
    for turn_index in range(ITERS):
        column_vec = lax.all_gather(direction_vec, ("row", "sub"), axis=0, tiled=True).reshape(
            row_count, quarter_len
        )
        direct = jnp.einsum("jiq,jq->i", tiles, column_vec, precision=lax.Precision.HIGHEST)
        extra = obs_error * direction_vec
        own_part = lax.psum_scatter(direct, ("col", "sub"), scatter_dimension=0, tiled=True)
        image = own_part + extra
        alpha = norm_now / lax.psum(jnp.sum(direction_vec * image), ("row", "col", "sub"))
        solution = solution + alpha * direction_vec
        residual = residual - alpha * image
        if turn_index + 1 < ITERS:
            norm_next = squares(residual)
            direction_vec = residual + norm_next / norm_now * direction_vec
            norm_now = norm_next
    return (solution, residual)


def solution(mesh):
    in_specs = (
        P(("group", "row", "sub"), None),
        P(("group", "row", "col", "sub")),
        P(("group", "row", "col", "sub")),
        P("group"),
        P("group", None),
    )
    out_specs = (P(("group", "row", "col", "sub")), P(("group", "row", "col", "sub")))
    return jax.shard_map(
        per_device, mesh=mesh, in_specs=in_specs, out_specs=out_specs, check_vma=False
    )
```

```python
import functools
import math

import jax
import jax.numpy as jnp
from jax import lax
from jax.experimental import pallas as pl
from jax.experimental.pallas import tpu as pltpu
from jax.sharding import PartitionSpec as P

ITERS = 2
LANES = 128


track_width = 0.0001
exp2_rate = -math.log2(math.e) / track_width


def off_diagonal(tiles):
    return tiles * (tiles - 1) // 2


def first_slot(a, tiles):
    return a * tiles - (a * (a + 1)) // 2


def each_pair(reach_tiles, class_ref, action):
    tiles = class_ref.shape[0]
    for a in range(tiles):
        for b in range(a + 1, tiles):
            slot = first_slot(a, tiles) + b - a - 1
            pl.when(class_ref[a, b] < reach_tiles)(functools.partial(action, slot, a, b))


def block_at(a, block_len):
    return pl.ds(pl.multiple_of(a * block_len, LANES), block_len)


def make_part(target, left_turned, right, left_column, right_pos):
    product = jnp.dot(left_turned, right, preferred_element_type=jnp.float32)
    left_pos = jnp.concatenate([left_column] * (right_pos.shape[1] // LANES), axis=1)
    distance = left_pos - right_pos
    target[...] = product * jnp.exp2(distance * distance * exp2_rate)


def turn_kernel(mate_ref, turned_ref):
    turned_ref[...] = mate_ref[...].T


def strips_kernel(
    reach_tiles, class_hbm, pos_ref, own_ref, mate_ref, turned_mate_ref, row_strips, column_strips, class_ref, both,
    turned, column, arrived,
):
    members, total_obs = own_ref.shape
    tiles = class_ref.shape[0]
    block_len = total_obs // tiles
    class_copy = pltpu.make_async_copy(class_hbm, class_ref, arrived)
    class_copy.start()
    both[:members, :] = own_ref[...]
    both[members:, :] = mate_ref[...]
    turned[:, :members] = own_ref[...].T
    turned[:, members:] = turned_mate_ref[...]
    spread_columns(pos_ref[...], column)
    _, within, _ = place()

    def chunk_of(a):
        return pl.ds(pl.multiple_of(a * block_len + within * LANES, LANES), LANES)

    def row_strip(target, a, b):
        at, columns_at = chunk_of(a), block_at(b, block_len)
        make_part(target, turned[at, :], both[:, columns_at], column[at, :], pos_ref[:, columns_at])

    def make_pair(slot, a, b):
        row_strip(row_strips.at[slot + tiles], a, b)
        at, columns_at = block_at(a, block_len), chunk_of(b)
        make_part(column_strips.at[slot], turned[at, :], both[:, columns_at], column[at, :], pos_ref[:, columns_at])

    for slot in range(tiles):
        row_strip(row_strips.at[slot], slot, slot)
    class_copy.wait()
    each_pair(reach_tiles, class_ref, make_pair)


def share_kernel(reach_tiles, class_ref, pos_ref, both, turned, column, row_strips, share_ref):
    tiles = class_ref.shape[0]
    block_len = share_ref.shape[1]
    _, within, per_row = place()

    def make_tile(slot, a, b):
        tile, columns_at = share_ref.at[slot], block_at(b, block_len)
        right, right_pos = both[:, columns_at], pos_ref[:, columns_at]
        here = pl.ds(pl.multiple_of(within * LANES, LANES), LANES)
        tile[here, :] = row_strips[slot]
        for turn in range(1, per_row):
            begin = lax.rem(within + turn, per_row) * LANES
            here = pl.ds(pl.multiple_of(begin, LANES), LANES)
            at = pl.ds(pl.multiple_of(a * block_len + begin, LANES), LANES)
            make_part(tile.at[here, :], turned[at, :], right, column[at, :], right_pos)

    for slot in range(tiles):
        make_tile(slot, slot, slot)
    each_pair(reach_tiles, class_ref, lambda slot, a, b: make_tile(slot + tiles, a, b))


def spread_columns(row, column):
    for begin in range(0, column.shape[0], LANES):
        square = jnp.broadcast_to(row[:, begin : begin + LANES], (LANES, LANES))
        column[begin : begin + LANES, :] = square.T


def spread_vector(vector, column):
    for piece in range(vector.shape[0]):
        square = jnp.broadcast_to(vector[piece : piece + 1, :], (LANES, LANES))
        column[piece * LANES : (piece + 1) * LANES, :] = square.T


def tile_weight(klass, reach_tiles, inverse_members):
    return jnp.maximum(0.0, 1.0 - klass.astype(jnp.float32) / reach_tiles) * inverse_members


def add_sums(into, weight, totals):
    for lane, total in enumerate(totals):
        into[:, lane * LANES : (lane + 1) * LANES] += weight * total


def add_turned(into, weight, across):
    for lane in range(across.shape[0] // LANES):
        where = slice(lane * LANES, (lane + 1) * LANES)
        turned = across[where, :].T
        folded = turned[:8, :]
        for begin in range(8, LANES, 8):
            folded = folded + turned[begin : begin + 8, :]
        into[:, where] += weight * folded


def fold_sums(sums, out_ref):
    for piece in range(sums.shape[1] // LANES):
        out_ref[piece : piece + 1, :] = jnp.sum(sums[:, piece * LANES : (piece + 1) * LANES], axis=0, keepdims=True)


def apply_share(reach_tiles, inverse_members, class_ref, share_ref, vector, column, across, sums, out_ref):
    tiles = class_ref.shape[0]
    block_len = share_ref.shape[1]
    lanes = block_len // LANES
    sums[...] = jnp.zeros_like(sums)

    def add_diagonal(a):
        at = block_at(a, block_len)
        tile, factor = share_ref.at[a], column.at[at, :]
        totals = [None] * lanes
        for begin in range(0, block_len, 8):
            part = slice(begin, begin + 8)
            for lane in range(lanes):
                term = tile[part, lane * LANES : (lane + 1) * LANES] * factor[part, :]
                totals[lane] = term if totals[lane] is None else totals[lane] + term
        add_sums(sums.at[:, at], tile_weight(class_ref[a, a], reach_tiles, inverse_members), totals)

    def add_pair(slot, a, b):
        weight = tile_weight(class_ref[a, b], reach_tiles, inverse_members)
        at_a, at_b = block_at(a, block_len), block_at(b, block_len)
        tile, factor = share_ref.at[slot + tiles], column.at[at_a, :]
        rows_b = [jnp.broadcast_to(vector[pl.ds(b * lanes + lane, 1), :], (8, LANES)) for lane in range(lanes)]
        totals = [None] * lanes
        for begin in range(0, block_len, 8):
            part = slice(begin, begin + 8)
            line = None
            for lane in range(lanes):
                here = tile[part, lane * LANES : (lane + 1) * LANES]
                term = here * factor[part, :]
                totals[lane] = term if totals[lane] is None else totals[lane] + term
                term = here * rows_b[lane]
                line = term if line is None else line + term
            across[part, :] = line
        add_sums(sums.at[:, at_b], weight, totals)
        add_turned(sums.at[:, at_a], weight, across)

    for a in range(tiles):
        add_diagonal(a)
    each_pair(reach_tiles, class_ref, add_pair)
    fold_sums(sums, out_ref)


def place():
    sub_count = lax.axis_size("sub")
    within = lax.axis_index("col") * sub_count + lax.axis_index("sub")
    return lax.axis_index("row"), within, lax.axis_size("col") * sub_count


def first_kernel(reach_tiles, inverse_members, masks, class_ref, row_strips, column_strips, error_ref, *refs):
    tiles = class_ref.shape[0]
    chunks, refs = refs[:tiles], refs[tiles:]
    out_ref, vector, column, across, sums = refs
    row_index, within, per_row = place()
    block_len = row_strips.shape[2]
    lanes = block_len // LANES
    pieces = tiles * lanes
    for mask, chunk in zip(masks, chunks):
        vector[pl.ds(row_index ^ mask, 1), :] = chunk[...]
    spread_vector(vector, column)
    sums[...] = jnp.zeros_like(sums)

    def sums_of_rows(strip, a):
        factor = column.at[pl.ds(pl.multiple_of(a * LANES, LANES), LANES), :]
        totals = [None] * lanes
        for begin in range(0, LANES, 8):
            part = slice(begin, begin + 8)
            for lane in range(lanes):
                term = strip[part, lane * LANES : (lane + 1) * LANES] * factor[part, :]
                totals[lane] = term if totals[lane] is None else totals[lane] + term
        return totals

    def add_pair(slot, a, b):
        weight = tile_weight(class_ref[a, b], reach_tiles, inverse_members)
        add_sums(sums.at[:, block_at(b, block_len)], weight, sums_of_rows(row_strips.at[slot + tiles], a))
        across[...] = column_strips[slot] * vector[pl.ds(b, 1), :]
        add_turned(sums.at[:, block_at(a, block_len)], weight, across)

    for a in range(tiles):
        weight = tile_weight(class_ref[a, a], reach_tiles, inverse_members)
        add_sums(sums.at[:, a * block_len : (a + 1) * block_len], weight, sums_of_rows(row_strips.at[a], a))
    each_pair(reach_tiles, class_ref, add_pair)
    fold_sums(sums, out_ref)
    own = row_index * per_row + within
    out_ref[pl.ds(own, 1), :] += error_ref[...] * chunks[0][...]
    out_ref[pieces : pieces + tiles, :] = vector[...]
    out_ref[pieces + tiles : pieces + tiles + 1, :] = error_ref[...]


def middle_kernel(pieces, *refs):
    parts, out_ref = refs[:-1], refs[-1]
    total = parts[0][:pieces, :]
    for part in parts[1:]:
        total = total + part[:pieces, :]
    out_ref[...] = total


def gather_kernel(tiles, masks, *refs):
    parts, (innovations_ref, error_ref) = refs[:-2], refs[-2:]
    _, within, per_row = place()
    pieces = innovations_ref.shape[0]
    for mask, part in zip(masks, parts):
        there = within ^ mask
        for a in range(tiles):
            innovations_ref[pl.ds(a * per_row + there, 1), :] = part[pieces + a : pieces + a + 1, :]
        error_ref[pl.ds(there, 1), :] = part[pieces + tiles : pieces + tiles + 1, :]


def total_of(x):
    return jnp.sum(jnp.sum(x, axis=0, keepdims=True), axis=1, keepdims=True)


def second_kernel(reach_tiles, inverse_members, peers, class_ref, share_ref, innovations_ref, error_ref, *refs):
    parts, refs = refs[:peers], refs[peers:]
    sent, refs = refs[:peers], refs[peers:]
    state_ref, direction, residual, start, whole_image, column, across, sums, product = refs
    row_index, within, per_row = place()
    innovations = innovations_ref[...]
    image = parts[0][...]
    for part in parts[1:]:
        image = image + part[...]
    norm_now = total_of(innovations * innovations)
    alpha = norm_now / total_of(innovations * image)
    residual_now = innovations - alpha * image
    residual[...] = residual_now
    spread_vector(residual, column)
    norm_next = total_of(residual_now * residual_now)
    ratio = norm_next / norm_now
    direction_now = residual_now + ratio * innovations
    direction[...] = direction_now
    start[...] = alpha * innovations
    whole_image[...] = image
    carried = ratio * total_of(direction_now * image)
    shared = (class_ref, share_ref, residual, column, across, sums, product)
    apply_share(reach_tiles, inverse_members, *shared)
    of_row = pl.ds(row_index * per_row, per_row)
    curvature = total_of(direction[...] * product[...])
    curvature = curvature + total_of(error_ref[...] * residual[of_row, :] * direction[of_row, :])
    for peer in range(peers):
        at = (row_index ^ peer) * per_row + within
        sent[peer][0:1, :] = product[pl.ds(at, 1), :]
        sent[peer][1:2, :] = jnp.broadcast_to(curvature, (1, LANES))
    own = pl.ds(row_index * per_row + within, 1)
    state_ref[0:1, :] = start[own, :]
    state_ref[1:2, :] = residual[own, :]
    state_ref[2:3, :] = direction[own, :]
    state_ref[3:4, :] = error_ref[pl.ds(within, 1), :] * residual[own, :] + ratio * whole_image[own, :]
    state_ref[4:5, :] = jnp.broadcast_to(norm_next, (1, LANES))
    state_ref[5:6, :] = jnp.broadcast_to(carried, (1, LANES))


def last_kernel(state_ref, *refs):
    parts, (solution_ref, residual_ref) = refs[:-2], refs[-2:]
    image, curvature = state_ref[3:4, :], state_ref[5:6, :]
    for part in parts:
        image = image + part[0:1, :]
        curvature = curvature + part[1:2, :]
    alpha = state_ref[4:5, :] / curvature
    solution_ref[...] = state_ref[0:1, :] + alpha * state_ref[2:3, :]
    residual_ref[...] = state_ref[1:2, :] - alpha * image


VMEM_SPEC = pl.BlockSpec(memory_space=pltpu.VMEM)
SMEM_SPEC = pl.BlockSpec(memory_space=pltpu.SMEM)
HBM_SPEC = pl.BlockSpec(memory_space=pltpu.HBM)


def in_hbm(x):
    return pltpu.with_memory_space_constraint(x, pltpu.HBM)


def exchange(axes, masks, values):
    count = math.prod(lax.axis_size(axis) for axis in axes)
    return [
        lax.ppermute(value, axes, [(i, i ^ mask) for i in range(count)]) if mask else value
        for mask, value in zip(masks, values)
    ]


def nearest_first(count):
    return tuple(range(count))


def farthest_pair_last(count):
    masks = list(range(count))
    masks[-2:] = masks[:-3:-1]
    return tuple(masks)


def farthest_first(count):
    return (0,) + tuple(range(count - 1, 0, -1))


def vectors_only(anomalies, innovations, obs_error, track_pos, taper_class):
    row_count = lax.axis_size("row")
    sub_count = lax.axis_size("sub")
    per_row = lax.axis_size("col") * sub_count
    local_members, total_obs = anomalies.shape
    member_total = local_members * row_count * sub_count
    inverse_members = 1.0 / (member_total - 1)
    reach_tiles = max(2, row_count // 4)
    pieces = total_obs // LANES
    block_len = total_obs // row_count
    f32 = jnp.float32
    row, here = ("row",), ("col", "sub")
    params = pltpu.CompilerParams(vmem_limit_bytes=16 * 1024 * 1024)

    mate = lax.ppermute(anomalies, "sub", [(0, 1), (1, 0)])
    chunk = innovations.reshape(1, LANES)
    error = obs_error.reshape(1, LANES)
    chunk_order = farthest_pair_last(row_count)
    chunks = exchange(row, chunk_order, [chunk] * row_count)

    work = [pltpu.VMEM((block_len, LANES), f32), pltpu.VMEM((8, total_obs), f32)]
    pairs = off_diagonal(row_count)
    part_elements = (row_count + pairs) * block_len * block_len
    mate_bytes = anomalies.size * anomalies.dtype.itemsize
    turned_mate = pl.pallas_call(
        turn_kernel,
        out_shape=pltpu.VMEM((total_obs, local_members), anomalies.dtype),
        in_specs=[VMEM_SPEC],
        out_specs=VMEM_SPEC,
        compiler_params=params,
        cost_estimate=pl.CostEstimate(flops=4 * local_members * total_obs * total_obs, bytes_accessed=16 * mate_bytes, transcendentals=0),
        name="turn",
    )(mate)
    positions = track_pos.reshape(1, total_obs)
    strips, strip_columns, classes, both, turned, column = pl.pallas_call(
        functools.partial(strips_kernel, reach_tiles),
        out_shape=[
            pltpu.VMEM((row_count + pairs, LANES, block_len), f32),
            pltpu.VMEM((pairs, block_len, LANES), f32),
            pltpu.SMEM(taper_class.shape, jnp.int32),
            pltpu.VMEM((2 * local_members, total_obs), anomalies.dtype),
            pltpu.VMEM((total_obs, 2 * local_members), anomalies.dtype),
            pltpu.VMEM((total_obs, LANES), f32),
        ],
        in_specs=[HBM_SPEC] + [VMEM_SPEC] * 4,
        out_specs=[VMEM_SPEC] * 2 + [SMEM_SPEC] + [VMEM_SPEC] * 3,
        scratch_shapes=[pltpu.SemaphoreType.DMA(())],
        compiler_params=params,
        cost_estimate=pl.CostEstimate(
            flops=2 * local_members * part_elements,
            bytes_accessed=2 * part_elements,
            transcendentals=part_elements // 2,
        ),
        name="strips",
    )(in_hbm(taper_class), positions, anomalies, mate, turned_mate)

    payload = pl.pallas_call(
        functools.partial(first_kernel, reach_tiles, inverse_members, chunk_order),
        out_shape=pltpu.VMEM((pieces + 8, LANES), f32),
        in_specs=[SMEM_SPEC] + [VMEM_SPEC] * (row_count + 3),
        out_specs=VMEM_SPEC,
        scratch_shapes=[pltpu.VMEM((row_count, LANES), f32), pltpu.VMEM((row_count * LANES, LANES), f32)]
        + work,
        compiler_params=params,
        name="first",
    )(classes, strips, strip_columns, error, *chunks)
    payload_order = nearest_first(per_row)
    payloads = exchange(here, payload_order, [payload] * per_row)
    part = pl.pallas_call(
        functools.partial(middle_kernel, pieces),
        out_shape=pltpu.VMEM((pieces, LANES), f32),
        in_specs=[VMEM_SPEC] * per_row,
        out_specs=VMEM_SPEC,
        compiler_params=params,
        name="middle",
    )(*payloads)
    parts = exchange(row, nearest_first(row_count), [part] * row_count)
    whole, error = pl.pallas_call(
        functools.partial(gather_kernel, row_count, payload_order),
        out_shape=[pltpu.VMEM((pieces, LANES), f32), pltpu.VMEM((per_row, LANES), f32)],
        in_specs=[VMEM_SPEC] * per_row,
        out_specs=[VMEM_SPEC] * 2,
        compiler_params=params,
        name="gather",
    )(*payloads)

    share = pl.pallas_call(
        functools.partial(share_kernel, reach_tiles),
        out_shape=pltpu.VMEM((row_count + pairs, block_len, block_len), f32),
        in_specs=[SMEM_SPEC] + [VMEM_SPEC] * 5,
        out_specs=VMEM_SPEC,
        compiler_params=params,
        cost_estimate=pl.CostEstimate(
            flops=4 * local_members * part_elements,
            bytes_accessed=4 * part_elements,
            transcendentals=part_elements,
        ),
        name="share",
    )(classes, positions, both, turned, column, strips)
    *sent, state = pl.pallas_call(
        functools.partial(second_kernel, reach_tiles, inverse_members, row_count),
        out_shape=[pltpu.VMEM((8, LANES), f32) for _ in range(row_count + 1)],
        in_specs=[SMEM_SPEC] + [VMEM_SPEC] * (row_count + 3),
        out_specs=[VMEM_SPEC] * (row_count + 1),
        scratch_shapes=[pltpu.VMEM((pieces, LANES), f32)] * 4
        + [pltpu.VMEM((total_obs, LANES), f32)]
        + work
        + [pltpu.VMEM((pieces, LANES), f32)],
        compiler_params=params,
        name="second",
    )(classes, share, whole, error, *parts)
    last_order = farthest_first(row_count)
    got = exchange(row, last_order, [sent[mask] for mask in last_order])
    solution_part, residual_part = pl.pallas_call(
        last_kernel,
        out_shape=[jax.ShapeDtypeStruct((1, LANES), f32)] * 2,
        in_specs=[VMEM_SPEC] * (row_count + 1),
        out_specs=[VMEM_SPEC] * 2,
        compiler_params=pltpu.CompilerParams(vmem_limit_bytes=1024 * 1024),
        name="last",
    )(state, *got)
    return solution_part.reshape(LANES), residual_part.reshape(LANES)


def fits(anomalies, innovations, obs_error, track_pos, taper_class):
    row_count = lax.axis_size("row")
    per_row = lax.axis_size("col") * lax.axis_size("sub")
    local_members, total_obs = anomalies.shape
    block_len = total_obs // row_count
    share_bytes = 4 * (row_count + off_diagonal(row_count)) * block_len * block_len
    return (
        ITERS == 2
        and row_count in (2, 4)
        and per_row in (2, 4)
        and lax.axis_size("sub") == 2
        and innovations.shape[0] == LANES
        and total_obs == row_count * per_row * LANES
        and local_members % LANES == 0
        and share_bytes <= 16 * 1024 * 1024
    )


def per_device(*args):
    return vectors_only(*args) if fits(*args) else blocks(*args)


def squares(residual):
    return lax.psum(jnp.sum(residual * residual), ("row", "col", "sub"))


def blocks(anomalies, innovations, obs_error, track_pos, taper_class):
    row_count = lax.axis_size("row")
    col_count = lax.axis_size("col")
    sub_count = lax.axis_size("sub")
    row_index = lax.axis_index("row")
    col_index = lax.axis_index("col")
    local_members, total_obs = anomalies.shape
    block_len = total_obs // row_count
    quarter_len = block_len // col_count
    member_total = local_members * row_count * sub_count
    inverse_members = 1.0 / (member_total - 1)
    reach_tiles = max(2, row_count // 4)
    class_row = lax.dynamic_index_in_dim(taper_class, row_index, 0, keepdims=False)
    tile_weight = jnp.maximum(0.0, 1.0 - class_row.astype(jnp.float32) / reach_tiles)
    row_pos = lax.dynamic_slice_in_dim(track_pos, row_index * block_len, block_len, 0)
    col_pos = lax.dynamic_index_in_dim(
        track_pos.reshape(row_count, col_count, quarter_len), col_index, 1, keepdims=False
    )
    own_block = lax.all_to_all(anomalies, "row", split_axis=1, concat_axis=0, tiled=True)
    own_quarter = lax.dynamic_slice_in_dim(own_block, col_index * quarter_len, quarter_len, 1)

    def one_tile(piece, block_index, keep_factor):
        product = jnp.einsum("mi,mq->iq", own_block, piece, preferred_element_type=jnp.float32)
        column_pos = lax.dynamic_index_in_dim(col_pos, block_index, 0, keepdims=False)
        weight_here = lax.dynamic_index_in_dim(tile_weight, block_index, 0, keepdims=False)
        distance = row_pos[:, None] - column_pos[None, :]
        taper = weight_here * keep_factor * jnp.exp(-(distance * distance) / track_width)
        return product * (taper * inverse_members)

    def one_entry(entry):
        return one_tile(entry[0], entry[1], 1.0)

    piece = lax.all_gather(own_quarter[None], "row", axis=0, tiled=True)
    indices = jnp.arange(piece.shape[0], dtype=jnp.int32)
    tiles = lax.map(one_entry, (piece, indices))
    solution = jnp.zeros_like(innovations)
    residual = innovations
    direction_vec = innovations
    norm_now = squares(residual)
    for turn_index in range(ITERS):
        column_vec = lax.all_gather(direction_vec, ("row", "sub"), axis=0, tiled=True).reshape(
            row_count, quarter_len
        )
        direct = jnp.einsum("jiq,jq->i", tiles, column_vec, precision=lax.Precision.HIGHEST)
        extra = obs_error * direction_vec
        own_part = lax.psum_scatter(direct, ("col", "sub"), scatter_dimension=0, tiled=True)
        image = own_part + extra
        alpha = norm_now / lax.psum(jnp.sum(direction_vec * image), ("row", "col", "sub"))
        solution = solution + alpha * direction_vec
        residual = residual - alpha * image
        if turn_index + 1 < ITERS:
            norm_next = squares(residual)
            direction_vec = residual + norm_next / norm_now * direction_vec
            norm_now = norm_next
    return (solution, residual)


def solution(mesh):
    in_specs = (
        P(("group", "row", "sub"), None),
        P(("group", "row", "col", "sub")),
        P(("group", "row", "col", "sub")),
        P("group"),
        P("group", None),
    )
    out_specs = (P(("group", "row", "col", "sub")), P(("group", "row", "col", "sub")))
    return jax.shard_map(
        per_device, mesh=mesh, in_specs=in_specs, out_specs=out_specs, check_vma=False
    )
```

```python
import functools
import math

import jax
import jax.numpy as jnp
from jax import lax
from jax.experimental import pallas as pl
from jax.experimental.pallas import tpu as pltpu
from jax.sharding import PartitionSpec as P

ITERS = 2
LANES = 128


track_width = 0.0001
exp2_rate = -math.log2(math.e) / track_width


def off_diagonal(tiles):
    return tiles * (tiles - 1) // 2


def first_slot(a, tiles):
    return a * tiles - (a * (a + 1)) // 2


def each_pair(reach_tiles, class_ref, action):
    tiles = class_ref.shape[0]
    for a in range(tiles):
        for b in range(a + 1, tiles):
            slot = first_slot(a, tiles) + b - a - 1
            pl.when(class_ref[a, b] < reach_tiles)(functools.partial(action, slot, a, b))


def block_at(a, block_len):
    return pl.ds(pl.multiple_of(a * block_len, LANES), block_len)


def make_part(target, left_turned, right, left_column, right_pos):
    product = jnp.dot(left_turned, right, preferred_element_type=jnp.float32)
    left_pos = jnp.concatenate([left_column] * (right_pos.shape[1] // LANES), axis=1)
    distance = left_pos - right_pos
    target[...] = product * jnp.exp2(distance * distance * exp2_rate)


def turn_kernel(mate_ref, turned_ref):
    turned_ref[...] = mate_ref[...].T


def strips_kernel(
    reach_tiles, class_hbm, pos_ref, own_ref, mate_ref, turned_mate_ref, row_strips, column_strips, class_ref, both,
    turned, column, arrived,
):
    members, total_obs = own_ref.shape
    tiles = class_ref.shape[0]
    block_len = total_obs // tiles
    class_copy = pltpu.make_async_copy(class_hbm, class_ref, arrived)
    class_copy.start()
    both[:members, :] = own_ref[...]
    both[members:, :] = mate_ref[...]
    turned[:, :members] = own_ref[...].T
    turned[:, members:] = turned_mate_ref[...]
    spread_columns(pos_ref[...], column)
    _, within, _ = place()

    def chunk_of(a):
        return pl.ds(pl.multiple_of(a * block_len + within * LANES, LANES), LANES)

    def row_strip(target, a, b):
        at, columns_at = chunk_of(a), block_at(b, block_len)
        make_part(target, turned[at, :], both[:, columns_at], column[at, :], pos_ref[:, columns_at])

    def make_pair(slot, a, b):
        row_strip(row_strips.at[slot + tiles], a, b)
        at, columns_at = block_at(a, block_len), chunk_of(b)
        make_part(column_strips.at[slot], turned[at, :], both[:, columns_at], column[at, :], pos_ref[:, columns_at])

    for slot in range(tiles):
        row_strip(row_strips.at[slot], slot, slot)
    class_copy.wait()
    each_pair(reach_tiles, class_ref, make_pair)


def share_kernel(reach_tiles, class_ref, pos_ref, both, turned, column, row_strips, share_ref):
    tiles = class_ref.shape[0]
    block_len = share_ref.shape[1]
    _, within, per_row = place()

    def make_tile(slot, a, b):
        tile, columns_at = share_ref.at[slot], block_at(b, block_len)
        right, right_pos = both[:, columns_at], pos_ref[:, columns_at]
        here = pl.ds(pl.multiple_of(within * LANES, LANES), LANES)
        tile[here, :] = row_strips[slot]
        for turn in range(1, per_row):
            begin = lax.rem(within + turn, per_row) * LANES
            here = pl.ds(pl.multiple_of(begin, LANES), LANES)
            at = pl.ds(pl.multiple_of(a * block_len + begin, LANES), LANES)
            make_part(tile.at[here, :], turned[at, :], right, column[at, :], right_pos)

    for slot in range(tiles):
        make_tile(slot, slot, slot)
    each_pair(reach_tiles, class_ref, lambda slot, a, b: make_tile(slot + tiles, a, b))


def spread_columns(row, column):
    for begin in range(0, column.shape[0], LANES):
        square = jnp.broadcast_to(row[:, begin : begin + LANES], (LANES, LANES))
        column[begin : begin + LANES, :] = square.T


def spread_vector(vector, column):
    for piece in range(vector.shape[0]):
        square = jnp.broadcast_to(vector[piece : piece + 1, :], (LANES, LANES))
        column[piece * LANES : (piece + 1) * LANES, :] = square.T


def tile_weight(klass, reach_tiles, inverse_members):
    return jnp.maximum(0.0, 1.0 - klass.astype(jnp.float32) / reach_tiles) * inverse_members


def add_sums(into, weight, totals):
    for lane, total in enumerate(totals):
        into[:, lane * LANES : (lane + 1) * LANES] += weight * total


def add_turned(into, weight, across):
    for lane in range(across.shape[0] // LANES):
        where = slice(lane * LANES, (lane + 1) * LANES)
        turned = across[where, :].T
        folded = turned[:8, :]
        for begin in range(8, LANES, 8):
            folded = folded + turned[begin : begin + 8, :]
        into[:, where] += weight * folded


def fold_sums(sums, out_ref):
    for piece in range(sums.shape[1] // LANES):
        out_ref[piece : piece + 1, :] = jnp.sum(sums[:, piece * LANES : (piece + 1) * LANES], axis=0, keepdims=True)


def apply_share(reach_tiles, inverse_members, class_ref, share_ref, vector, column, across, sums, out_ref):
    tiles = class_ref.shape[0]
    block_len = share_ref.shape[1]
    lanes = block_len // LANES
    sums[...] = jnp.zeros_like(sums)

    def add_diagonal(a):
        at = block_at(a, block_len)
        tile, factor = share_ref.at[a], column.at[at, :]
        totals = [None] * lanes
        for begin in range(0, block_len, 8):
            part = slice(begin, begin + 8)
            for lane in range(lanes):
                term = tile[part, lane * LANES : (lane + 1) * LANES] * factor[part, :]
                totals[lane] = term if totals[lane] is None else totals[lane] + term
        add_sums(sums.at[:, at], tile_weight(class_ref[a, a], reach_tiles, inverse_members), totals)

    def add_pair(slot, a, b):
        weight = tile_weight(class_ref[a, b], reach_tiles, inverse_members)
        at_a, at_b = block_at(a, block_len), block_at(b, block_len)
        tile, factor = share_ref.at[slot + tiles], column.at[at_a, :]
        rows_b = [jnp.broadcast_to(vector[pl.ds(b * lanes + lane, 1), :], (8, LANES)) for lane in range(lanes)]
        totals = [None] * lanes
        for begin in range(0, block_len, 8):
            part = slice(begin, begin + 8)
            line = None
            for lane in range(lanes):
                here = tile[part, lane * LANES : (lane + 1) * LANES]
                term = here * factor[part, :]
                totals[lane] = term if totals[lane] is None else totals[lane] + term
                term = here * rows_b[lane]
                line = term if line is None else line + term
            across[part, :] = line
        add_sums(sums.at[:, at_b], weight, totals)
        add_turned(sums.at[:, at_a], weight, across)

    for a in range(tiles):
        add_diagonal(a)
    each_pair(reach_tiles, class_ref, add_pair)
    fold_sums(sums, out_ref)


def place():
    sub_count = lax.axis_size("sub")
    within = lax.axis_index("col") * sub_count + lax.axis_index("sub")
    return lax.axis_index("row"), within, lax.axis_size("col") * sub_count


def first_kernel(reach_tiles, inverse_members, masks, class_ref, row_strips, column_strips, error_ref, *refs):
    tiles = class_ref.shape[0]
    chunks, refs = refs[:tiles], refs[tiles:]
    out_ref, vector, column, across, sums = refs
    row_index, within, per_row = place()
    block_len = row_strips.shape[2]
    lanes = block_len // LANES
    pieces = tiles * lanes
    for mask, chunk in zip(masks, chunks):
        vector[pl.ds(row_index ^ mask, 1), :] = chunk[...]
    spread_vector(vector, column)
    sums[...] = jnp.zeros_like(sums)

    def sums_of_rows(strip, a):
        factor = column.at[pl.ds(pl.multiple_of(a * LANES, LANES), LANES), :]
        totals = [None] * lanes
        for begin in range(0, LANES, 8):
            part = slice(begin, begin + 8)
            for lane in range(lanes):
                term = strip[part, lane * LANES : (lane + 1) * LANES] * factor[part, :]
                totals[lane] = term if totals[lane] is None else totals[lane] + term
        return totals

    def add_pair(slot, a, b):
        weight = tile_weight(class_ref[a, b], reach_tiles, inverse_members)
        add_sums(sums.at[:, block_at(b, block_len)], weight, sums_of_rows(row_strips.at[slot + tiles], a))
        across[...] = column_strips[slot] * vector[pl.ds(b, 1), :]
        add_turned(sums.at[:, block_at(a, block_len)], weight, across)

    for a in range(tiles):
        weight = tile_weight(class_ref[a, a], reach_tiles, inverse_members)
        add_sums(sums.at[:, a * block_len : (a + 1) * block_len], weight, sums_of_rows(row_strips.at[a], a))
    each_pair(reach_tiles, class_ref, add_pair)
    fold_sums(sums, out_ref)
    own = row_index * per_row + within
    out_ref[pl.ds(own, 1), :] += error_ref[...] * chunks[0][...]
    out_ref[pieces : pieces + tiles, :] = vector[...]
    out_ref[pieces + tiles : pieces + tiles + 1, :] = error_ref[...]


def middle_kernel(pieces, *refs):
    parts, out_ref = refs[:-1], refs[-1]
    total = parts[0][:pieces, :]
    for part in parts[1:]:
        total = total + part[:pieces, :]
    out_ref[...] = total


def gather_kernel(tiles, masks, *refs):
    parts, (innovations_ref, error_ref, norm_ref) = refs[:-3], refs[-3:]
    _, within, per_row = place()
    pieces = innovations_ref.shape[0]
    for mask, part in zip(masks, parts):
        there = within ^ mask
        for a in range(tiles):
            innovations_ref[pl.ds(a * per_row + there, 1), :] = part[pieces + a : pieces + a + 1, :]
        error_ref[pl.ds(there, 1), :] = part[pieces + tiles : pieces + tiles + 1, :]
    norm_ref[...] = jnp.broadcast_to(total_of(innovations_ref[...] * innovations_ref[...]), norm_ref.shape)


def total_of(x):
    return jnp.sum(jnp.sum(x, axis=0, keepdims=True), axis=1, keepdims=True)


def second_kernel(reach_tiles, inverse_members, peers, class_ref, share_ref, innovations_ref, error_ref, norm_ref, *refs):
    parts, refs = refs[:peers], refs[peers:]
    sent, refs = refs[:peers], refs[peers:]
    state_ref, direction, residual, start, whole_image, column, across, sums, product = refs
    row_index, within, per_row = place()
    innovations = innovations_ref[...]
    image = parts[0][...]
    for part in parts[1:]:
        image = image + part[...]
    norm_now = norm_ref[:, 0:1]
    alpha = norm_now / total_of(innovations * image)
    residual_now = innovations - alpha * image
    residual[...] = residual_now
    spread_vector(residual, column)
    norm_next = total_of(residual_now * residual_now)
    ratio = norm_next / norm_now
    direction_now = residual_now + ratio * innovations
    direction[...] = direction_now
    start[...] = alpha * innovations
    whole_image[...] = image
    carried = ratio * total_of(direction_now * image)
    shared = (class_ref, share_ref, residual, column, across, sums, product)
    apply_share(reach_tiles, inverse_members, *shared)
    of_row = pl.ds(row_index * per_row, per_row)
    curvature = total_of(direction[...] * product[...])
    curvature = curvature + total_of(error_ref[...] * residual[of_row, :] * direction[of_row, :])
    for peer in range(peers):
        at = (row_index ^ peer) * per_row + within
        sent[peer][0:1, :] = product[pl.ds(at, 1), :]
        sent[peer][1:2, :] = jnp.broadcast_to(curvature, (1, LANES))
    own = pl.ds(row_index * per_row + within, 1)
    state_ref[0:1, :] = start[own, :]
    state_ref[1:2, :] = residual[own, :]
    state_ref[2:3, :] = direction[own, :]
    state_ref[3:4, :] = error_ref[pl.ds(within, 1), :] * residual[own, :] + ratio * whole_image[own, :]
    state_ref[4:5, :] = jnp.broadcast_to(norm_next, (1, LANES))
    state_ref[5:6, :] = jnp.broadcast_to(carried, (1, LANES))


def last_kernel(state_ref, *refs):
    parts, (solution_ref, residual_ref) = refs[:-2], refs[-2:]
    image, curvature = state_ref[3:4, :], state_ref[5:6, :]
    for part in parts:
        image = image + part[0:1, :]
        curvature = curvature + part[1:2, :]
    alpha = state_ref[4:5, :] / curvature
    solution_ref[...] = state_ref[0:1, :] + alpha * state_ref[2:3, :]
    residual_ref[...] = state_ref[1:2, :] - alpha * image


VMEM_SPEC = pl.BlockSpec(memory_space=pltpu.VMEM)
SMEM_SPEC = pl.BlockSpec(memory_space=pltpu.SMEM)
HBM_SPEC = pl.BlockSpec(memory_space=pltpu.HBM)


def in_hbm(x):
    return pltpu.with_memory_space_constraint(x, pltpu.HBM)


def exchange(axes, masks, values):
    count = math.prod(lax.axis_size(axis) for axis in axes)
    return [
        lax.ppermute(value, axes, [(i, i ^ mask) for i in range(count)]) if mask else value
        for mask, value in zip(masks, values)
    ]


def nearest_first(count):
    return tuple(range(count))


def farthest_pair_last(count):
    masks = list(range(count))
    masks[-2:] = masks[:-3:-1]
    return tuple(masks)


def farthest_first(count):
    return (0,) + tuple(range(count - 1, 0, -1))


def vectors_only(anomalies, innovations, obs_error, track_pos, taper_class):
    row_count = lax.axis_size("row")
    sub_count = lax.axis_size("sub")
    per_row = lax.axis_size("col") * sub_count
    local_members, total_obs = anomalies.shape
    member_total = local_members * row_count * sub_count
    inverse_members = 1.0 / (member_total - 1)
    reach_tiles = max(2, row_count // 4)
    pieces = total_obs // LANES
    block_len = total_obs // row_count
    f32 = jnp.float32
    row, here = ("row",), ("col", "sub")
    params = pltpu.CompilerParams(vmem_limit_bytes=16 * 1024 * 1024)

    mate = lax.ppermute(anomalies, "sub", [(0, 1), (1, 0)])
    chunk = innovations.reshape(1, LANES)
    error = obs_error.reshape(1, LANES)
    chunk_order = farthest_pair_last(row_count)
    chunks = exchange(row, chunk_order, [chunk] * row_count)

    work = [pltpu.VMEM((block_len, LANES), f32), pltpu.VMEM((8, total_obs), f32)]
    pairs = off_diagonal(row_count)
    part_elements = (row_count + pairs) * block_len * block_len
    mate_bytes = anomalies.size * anomalies.dtype.itemsize
    turned_mate = pl.pallas_call(
        turn_kernel,
        out_shape=pltpu.VMEM((total_obs, local_members), anomalies.dtype),
        in_specs=[VMEM_SPEC],
        out_specs=VMEM_SPEC,
        compiler_params=params,
        cost_estimate=pl.CostEstimate(flops=4 * local_members * total_obs * total_obs, bytes_accessed=16 * mate_bytes, transcendentals=0),
        name="turn",
    )(mate)
    positions = track_pos.reshape(1, total_obs)
    strips, strip_columns, classes, both, turned, column = pl.pallas_call(
        functools.partial(strips_kernel, reach_tiles),
        out_shape=[
            pltpu.VMEM((row_count + pairs, LANES, block_len), f32),
            pltpu.VMEM((pairs, block_len, LANES), f32),
            pltpu.SMEM(taper_class.shape, jnp.int32),
            pltpu.VMEM((2 * local_members, total_obs), anomalies.dtype),
            pltpu.VMEM((total_obs, 2 * local_members), anomalies.dtype),
            pltpu.VMEM((total_obs, LANES), f32),
        ],
        in_specs=[HBM_SPEC] + [VMEM_SPEC] * 4,
        out_specs=[VMEM_SPEC] * 2 + [SMEM_SPEC] + [VMEM_SPEC] * 3,
        scratch_shapes=[pltpu.SemaphoreType.DMA(())],
        compiler_params=params,
        cost_estimate=pl.CostEstimate(
            flops=2 * local_members * part_elements,
            bytes_accessed=2 * part_elements,
            transcendentals=part_elements // 2,
        ),
        name="strips",
    )(in_hbm(taper_class), positions, anomalies, mate, turned_mate)

    payload = pl.pallas_call(
        functools.partial(first_kernel, reach_tiles, inverse_members, chunk_order),
        out_shape=pltpu.VMEM((pieces + 8, LANES), f32),
        in_specs=[SMEM_SPEC] + [VMEM_SPEC] * (row_count + 3),
        out_specs=VMEM_SPEC,
        scratch_shapes=[pltpu.VMEM((row_count, LANES), f32), pltpu.VMEM((row_count * LANES, LANES), f32)]
        + work,
        compiler_params=params,
        name="first",
    )(classes, strips, strip_columns, error, *chunks)
    payload_order = nearest_first(per_row)
    payloads = exchange(here, payload_order, [payload] * per_row)
    part = pl.pallas_call(
        functools.partial(middle_kernel, pieces),
        out_shape=pltpu.VMEM((pieces, LANES), f32),
        in_specs=[VMEM_SPEC] * per_row,
        out_specs=VMEM_SPEC,
        compiler_params=params,
        name="middle",
    )(*payloads)
    parts = exchange(row, nearest_first(row_count), [part] * row_count)
    whole, error, norm = pl.pallas_call(
        functools.partial(gather_kernel, row_count, payload_order),
        out_shape=[pltpu.VMEM(shape, f32) for shape in ((pieces, LANES), (per_row, LANES), (1, LANES))],
        in_specs=[VMEM_SPEC] * per_row,
        out_specs=[VMEM_SPEC] * 3,
        compiler_params=params,
        name="gather",
    )(*payloads)

    share = pl.pallas_call(
        functools.partial(share_kernel, reach_tiles),
        out_shape=pltpu.VMEM((row_count + pairs, block_len, block_len), f32),
        in_specs=[SMEM_SPEC] + [VMEM_SPEC] * 5,
        out_specs=VMEM_SPEC,
        compiler_params=params,
        cost_estimate=pl.CostEstimate(
            flops=4 * local_members * part_elements,
            bytes_accessed=4 * part_elements,
            transcendentals=part_elements,
        ),
        name="share",
    )(classes, positions, both, turned, column, strips)
    *sent, state = pl.pallas_call(
        functools.partial(second_kernel, reach_tiles, inverse_members, row_count),
        out_shape=[pltpu.VMEM((8, LANES), f32) for _ in range(row_count + 1)],
        in_specs=[SMEM_SPEC] + [VMEM_SPEC] * (row_count + 4),
        out_specs=[VMEM_SPEC] * (row_count + 1),
        scratch_shapes=[pltpu.VMEM((pieces, LANES), f32)] * 4
        + [pltpu.VMEM((total_obs, LANES), f32)]
        + work
        + [pltpu.VMEM((pieces, LANES), f32)],
        compiler_params=params,
        name="second",
    )(classes, share, whole, error, norm, *parts)
    last_order = farthest_first(row_count)
    got = exchange(row, last_order, [sent[mask] for mask in last_order])
    solution_part, residual_part = pl.pallas_call(
        last_kernel,
        out_shape=[jax.ShapeDtypeStruct((1, LANES), f32)] * 2,
        in_specs=[VMEM_SPEC] * (row_count + 1),
        out_specs=[VMEM_SPEC] * 2,
        compiler_params=pltpu.CompilerParams(vmem_limit_bytes=1024 * 1024),
        name="last",
    )(state, *got)
    return solution_part.reshape(LANES), residual_part.reshape(LANES)


def fits(anomalies, innovations, obs_error, track_pos, taper_class):
    row_count = lax.axis_size("row")
    per_row = lax.axis_size("col") * lax.axis_size("sub")
    local_members, total_obs = anomalies.shape
    block_len = total_obs // row_count
    share_bytes = 4 * (row_count + off_diagonal(row_count)) * block_len * block_len
    return (
        ITERS == 2
        and row_count in (2, 4)
        and per_row in (2, 4)
        and lax.axis_size("sub") == 2
        and innovations.shape[0] == LANES
        and total_obs == row_count * per_row * LANES
        and local_members % LANES == 0
        and share_bytes <= 16 * 1024 * 1024
    )


def per_device(*args):
    return vectors_only(*args) if fits(*args) else blocks(*args)


def squares(residual):
    return lax.psum(jnp.sum(residual * residual), ("row", "col", "sub"))


def blocks(anomalies, innovations, obs_error, track_pos, taper_class):
    row_count = lax.axis_size("row")
    col_count = lax.axis_size("col")
    sub_count = lax.axis_size("sub")
    row_index = lax.axis_index("row")
    col_index = lax.axis_index("col")
    local_members, total_obs = anomalies.shape
    block_len = total_obs // row_count
    quarter_len = block_len // col_count
    member_total = local_members * row_count * sub_count
    inverse_members = 1.0 / (member_total - 1)
    reach_tiles = max(2, row_count // 4)
    class_row = lax.dynamic_index_in_dim(taper_class, row_index, 0, keepdims=False)
    tile_weight = jnp.maximum(0.0, 1.0 - class_row.astype(jnp.float32) / reach_tiles)
    row_pos = lax.dynamic_slice_in_dim(track_pos, row_index * block_len, block_len, 0)
    col_pos = lax.dynamic_index_in_dim(
        track_pos.reshape(row_count, col_count, quarter_len), col_index, 1, keepdims=False
    )
    own_block = lax.all_to_all(anomalies, "row", split_axis=1, concat_axis=0, tiled=True)
    own_quarter = lax.dynamic_slice_in_dim(own_block, col_index * quarter_len, quarter_len, 1)

    def one_tile(piece, block_index, keep_factor):
        product = jnp.einsum("mi,mq->iq", own_block, piece, preferred_element_type=jnp.float32)
        column_pos = lax.dynamic_index_in_dim(col_pos, block_index, 0, keepdims=False)
        weight_here = lax.dynamic_index_in_dim(tile_weight, block_index, 0, keepdims=False)
        distance = row_pos[:, None] - column_pos[None, :]
        taper = weight_here * keep_factor * jnp.exp(-(distance * distance) / track_width)
        return product * (taper * inverse_members)

    def one_entry(entry):
        return one_tile(entry[0], entry[1], 1.0)

    piece = lax.all_gather(own_quarter[None], "row", axis=0, tiled=True)
    indices = jnp.arange(piece.shape[0], dtype=jnp.int32)
    tiles = lax.map(one_entry, (piece, indices))
    solution = jnp.zeros_like(innovations)
    residual = innovations
    direction_vec = innovations
    norm_now = squares(residual)
    for turn_index in range(ITERS):
        column_vec = lax.all_gather(direction_vec, ("row", "sub"), axis=0, tiled=True).reshape(
            row_count, quarter_len
        )
        direct = jnp.einsum("jiq,jq->i", tiles, column_vec, precision=lax.Precision.HIGHEST)
        extra = obs_error * direction_vec
        own_part = lax.psum_scatter(direct, ("col", "sub"), scatter_dimension=0, tiled=True)
        image = own_part + extra
        alpha = norm_now / lax.psum(jnp.sum(direction_vec * image), ("row", "col", "sub"))
        solution = solution + alpha * direction_vec
        residual = residual - alpha * image
        if turn_index + 1 < ITERS:
            norm_next = squares(residual)
            direction_vec = residual + norm_next / norm_now * direction_vec
            norm_now = norm_next
    return (solution, residual)


def solution(mesh):
    in_specs = (
        P(("group", "row", "sub"), None),
        P(("group", "row", "col", "sub")),
        P(("group", "row", "col", "sub")),
        P("group"),
        P("group", None),
    )
    out_specs = (P(("group", "row", "col", "sub")), P(("group", "row", "col", "sub")))
    return jax.shard_map(
        per_device, mesh=mesh, in_specs=in_specs, out_specs=out_specs, check_vma=False
    )
```
